32 devices in a mesh: shard: 2 (over y), ctx: 4 (over z), tp: 4 (over x, core).
Axes of the slice: x: 2, y: 2, z: 4, core: 2. Of those that a mesh axis runs over, the one named last changes fastest.
Arguments:
- x_in: float32 [4096, 768], P(('shard', 'ctx')), may hold values from -6 to 6
- norm_gain: bfloat16 [768], P(('shard', 'ctx')), may hold values from 0.5 to 1.5
- w_z: bfloat16 [768, 1536], P(('shard', 'ctx'), 'tp'), may hold values from -0.21875 to 0.21875
- w_x: bfloat16 [768, 1536], P(('shard', 'ctx'), 'tp'), may hold values from -0.21875 to 0.21875
- w_bc: bfloat16 [768, 256], P(('shard', 'ctx')), may hold values from -0.21875 to 0.21875
- w_dt: bfloat16 [768, 24], P(('shard', 'ctx'), 'tp'), may hold values from -0.21875 to 0.21875
- w_out: bfloat16 [768, 1536], P(('shard', 'ctx'), 'tp'), may hold values from -0.15625 to 0.15625
- conv_wx: float32 [4, 1536], P(None, 'tp'), may hold values from -3 to 3
- conv_bx: float32 [1536], P('tp'), may hold values from -0.5 to 0.5
- conv_wbc: float32 [4, 256], replicated, may hold values from -3 to 3
- conv_bbc: float32 [256], replicated, may hold values from -0.5 to 0.5
- dt_bias: float32 [24], P('tp'), may hold values from -6 to -3
- a_log: float32 [24], P('tp'), may hold values from -6 to 2
- d_skip: float32 [24], P('tp'), may hold values from 0.5 to 1.5
- gate_gain: float32 [1536], P('tp'), may hold values from 0.5 to 1.5
- seq_lens: int32 [2, 3], P('shard'), may hold values from 1 to 1280, 2048 in all within a row
- token_mask: int32 [4096], P(('shard', 'ctx')), may hold values 0 or 1
- d_out: float32 [4096, 768], P(('shard', 'ctx')), may hold values from -6 to 6
Outputs:
- block_out: float32 [4096, 768], P(('shard', 'ctx'))
- d_x: float32 [4096, 768], P(('shard', 'ctx'))
- d_norm_gain: float32 [768], P(('shard', 'ctx'))
- d_w_z: float32 [768, 1536], P(('shard', 'ctx'), 'tp')
- d_w_x: float32 [768, 1536], P(('shard', 'ctx'), 'tp')
- d_w_bc: float32 [768, 256], P(('shard', 'ctx'))
- d_w_dt: float32 [768, 24], P(('shard', 'ctx'), 'tp')
- d_w_out: float32 [768, 1536], P(('shard', 'ctx'), 'tp')
- d_conv_wx: float32 [4, 1536], P(None, 'tp')
- d_conv_bx: float32 [1536], P('tp')
- d_conv_wbc: float32 [4, 256], replicated
- d_conv_bbc: float32 [256], replicated
- d_dt_bias: float32 [24], P('tp')
- d_a_log: float32 [24], P('tp')
- d_d_skip: float32 [24], P('tp')
- d_gate_gain: float32 [1536], P('tp')
The draws below stay inside these ranges and needn't reach their ends.
Inputs may be any that keep to these rules, and one draw needn't show every extreme that they name: `seq_lens`: each row sums to 2048, and its longest sequence has exactly 1280 positions.
All inputs are finite; a program needn't handle non-finite values. No bound on the sum of `token_mask` on one device may be relied on, other than what follows from the above.
Results may differ from the reference program's by a relative error of at most 0.014.
Values may be sent and summed in bfloat16 or wider, within the bound.
No kernel may reach another device: no remote copies, remote signals or barrier semaphores. Data moves between devices by JAX's collectives and lax.ppermute only.
A program may use at most 128 MiB of HBM per device.

```python
import math
import jax
import jax.numpy as jnp
import numpy as np
from jax import lax

D = 768
HEADS = 24
NSTATE = 128
KCONV = 4
SPAN = 256
TOK_DEV = 512
SEQS = 3
INNER = 1536
GROUP = 2048
GROUPS = 2
TOKENS = 4096
LONGEST = 1280
N_CTX = 4


def set_ends(array, rng, smallest, largest):
    place = [jax.random.randint(jax.random.fold_in(rng, axis), (), 0, length) for axis, length in enumerate(array.shape)]
    widest = array.shape.index(max(array.shape))
    neighbour = place[:widest] + [(place[widest] + 1) % array.shape[widest]] + place[widest + 1:]
    return array.at[tuple(place)].set(smallest).at[tuple(neighbour)].set(largest)


def block_scale(stream_key, shape, shards, least, top_value):
    def one(axis_at, shards_of):
        steps = jax.random.uniform(jax.random.fold_in(jax.random.fold_in(stream_key, 6), axis_at), (shards_of,), jnp.float32, least / len(shards), top_value / len(shards))
        return jnp.repeat(jnp.exp(steps), shape[axis_at] // shards_of).reshape((-1,) + (1,) * (len(shape) - axis_at - 1))

    loudness = one(*shards[0])
    for cut in shards[1:]:
        loudness = loudness * one(*cut)
    return loudness


def profile(amount, total, most, slope):
    weights = [(1 << 20) // math.isqrt(rank ** slope) + 1 for rank in range(2, amount + 1)]
    rest, counts = total - most - (amount - 1), [1] * (amount - 1)
    while rest > 0:
        movable = [i for i in range(amount - 1) if counts[i] < most]
        pool, budget = sum([weights[i] for i in movable]), rest
        for i in movable:
            more = min(most - counts[i], max(1, budget * weights[i] // pool), rest)
            counts[i] = counts[i] + more
            rest = rest - more
    return np.array([most] + counts)


def uneven_parts(stream_key, count, total, reach, lean):
    if count == 2:
        one = jax.random.randint(stream_key, (), max(1, total - reach), min(reach, total - 1) + 1)
        return jnp.stack([one, total - one])
    tallies = jnp.asarray(profile(count, total, reach, lean), jnp.int32)
    couples = (count - 1) // 2
    source_of, taker = tallies[1:1 + 2 * couples:2], tallies[2:2 + 2 * couples:2]
    slack = jnp.minimum(source_of - 1, reach - taker)
    shifted = jax.random.randint(jax.random.fold_in(stream_key, 1), (couples,), 0, 1 << 20) % (slack + 1)
    tallies = tallies.at[1:1 + 2 * couples:2].set(source_of - shifted).at[2:2 + 2 * couples:2].set(taker + shifted)
    return tallies[jax.random.permutation(jax.random.fold_in(stream_key, 2), count)]


def scatter_about(own_key, shape, width, most, split=(), kind=jnp.bfloat16):
    loudness = block_scale(own_key, shape, split, -0.22, 0.18) if split else 1.0
    entries = jax.random.normal(own_key, shape, jnp.float32) * width * loudness
    return jnp.minimum(jnp.maximum(entries, -most), most).astype(kind)


def setup_inputs(seed: int = 0) -> dict:
    splits = jax.random.split(jax.random.key(seed), 19)
    return {
        "x_in": scatter_about(splits[0], (TOKENS, D), 1.0, 6.0, ((0, 8),), jnp.float32),
        "norm_gain": jnp.clip(1.0 + 0.1 * jax.random.normal(splits[1], (D,), jnp.float32), 0.5, 1.5).astype(jnp.bfloat16),
        "w_z": scatter_about(splits[2], (D, INNER), D ** -0.5, 0.21875, ((0, 8), (1, 4))),
        "w_x": scatter_about(splits[3], (D, INNER), D ** -0.5, 0.21875, ((0, 8), (1, 4))),
        "w_bc": scatter_about(splits[4], (D, 2 * NSTATE), D ** -0.5, 0.21875, ((0, 8),)),
        "w_dt": scatter_about(splits[5], (D, HEADS), D ** -0.5, 0.21875, ((0, 8), (1, 4))),
        "w_out": scatter_about(splits[6], (D, INNER), INNER ** -0.5, 0.15625, ((0, 8), (1, 4))),
        "conv_wx": scatter_about(splits[7], (KCONV, INNER), KCONV ** -0.5, 3.0, ((1, 4),), jnp.float32),
        "conv_bx": jnp.clip(jax.random.uniform(splits[8], (INNER,), jnp.float32, -0.5, 0.5) * block_scale(splits[8], (INNER,), ((0, 4),), -0.4, 0.0), -0.5, 0.5),
        "conv_wbc": scatter_about(splits[9], (KCONV, 2 * NSTATE), KCONV ** -0.5, 3.0, (), jnp.float32),
        "conv_bbc": jnp.clip(jax.random.uniform(splits[10], (2 * NSTATE,), jnp.float32, -0.5, 0.5), -0.5, 0.5),
        "dt_bias": jnp.clip(-6.0 + 3.0 * jax.random.uniform(splits[11], (HEADS,), jnp.float32) ** block_scale(splits[11], (HEADS,), ((0, 4),), -0.2, 0.2), -6.0, -3.0),
        "a_log": jnp.clip(-6.0 + 8.0 * jax.random.uniform(splits[12], (HEADS,), jnp.float32) ** block_scale(splits[12], (HEADS,), ((0, 4),), -0.2, 0.2), -6.0, 2.0),
        "d_skip": jnp.clip(0.5 + 1.0 * jax.random.uniform(splits[13], (HEADS,), jnp.float32) ** block_scale(splits[13], (HEADS,), ((0, 4),), -0.2, 0.2), 0.5, 1.5),
        "gate_gain": jnp.clip(1.0 + 0.1 * jax.random.normal(splits[14], (INNER,), jnp.float32), 0.5, 1.5),
        "seq_lens": jax.vmap(lambda own: uneven_parts(own, SEQS, GROUP, LONGEST, 2))(jax.random.split(splits[15], GROUPS)).reshape((GROUPS, SEQS)).astype(jnp.int32),
        "token_mask": set_ends((jax.random.randint(splits[16], (TOKENS,), 0, 16) < 15).astype(jnp.int32), jax.random.fold_in(splits[16], 1), 0, 1),
        "d_out": scatter_about(splits[17], (TOKENS, D), 1.0, 6.0, ((0, 8),), jnp.float32),
    }


norm_eps = 1e-05

def segment_ids(positions, lengths_row):
    bounds = jnp.cumsum(lengths_row.astype(jnp.int32)).astype(jnp.int32)
    counted = lax.optimization_barrier(jnp.sum((positions[:, None] >= bounds[None, :]).astype(jnp.int32), axis=1)).astype(jnp.int32)
    return jnp.where(positions < 0, -1, counted).astype(jnp.int32)

def conv_silu(extended, seg_ext, weight, conv_bias):
    width_taps = weight.shape[0]
    row_count = extended.shape[0] - (width_taps - 1)
    summed = jnp.zeros((row_count, extended.shape[1]), jnp.float32) + conv_bias[None, :]
    for offset in range(width_taps):
        same_doc = (seg_ext[offset:offset + row_count] == seg_ext[width_taps - 1:]).astype(jnp.float32)
        summed = summed + weight[offset][None, :] * extended[offset:offset + row_count] * same_doc[:, None]
    return jax.nn.silu(summed)

def span_output(ssm_in, step_size, decay_rate, b_state, c_state, segment, seg_prev, state_in):
    cumulated = jnp.cumsum(step_size * decay_rate[None, :], axis=0)
    length = ssm_in.shape[0]
    ordering = jnp.arange(length, dtype=jnp.int32)
    allowed = (segment[:, None] == segment[None, :]) & (ordering[:, None] >= ordering[None, :])
    log_gaps = cumulated[:, None, :] - cumulated[None, :, :]
    log_gaps = jnp.where(allowed[:, :, None], log_gaps, 0.0)
    decays = jnp.where(allowed[:, :, None], jnp.exp(log_gaps), 0.0)
    scores = lax.dot_general(c_state, b_state, (((1,), (1,)), ((), ())), precision=lax.Precision.HIGHEST)
    mixing = scores[:, :, None] * decays * step_size[None, :, :]
    within = jnp.einsum('tsh,shp->thp', mixing, ssm_in, precision=lax.Precision.HIGHEST)
    carried = jnp.einsum('tn,hpn->thp', c_state, state_in, precision=lax.Precision.HIGHEST)
    entering = jnp.exp(cumulated) * (segment == seg_prev).astype(jnp.float32)[:, None]
    return within + carried * entering[:, :, None]

def span_state(ssm_in, step_size, decay_rate, b_state, segment, seg_prev):
    cumulated = jnp.cumsum(step_size * decay_rate[None, :], axis=0)
    final_sum = cumulated[-1]
    kept = (segment == segment[-1])[:, None]
    remaining = jnp.where(kept, final_sum[None, :] - cumulated, 0.0)
    weighting = jnp.where(kept, jnp.exp(remaining) * step_size, 0.0)
    scaled_in = ssm_in * weighting[:, :, None]
    state_out = jnp.einsum('shp,sn->hpn', scaled_in, b_state, precision=lax.Precision.HIGHEST)
    passing = jnp.exp(final_sum) * (segment[-1] == seg_prev).astype(jnp.float32)
    return (passing, state_out)

def mixer_piece(proj_z, proj_x, proj_bc, proj_dt, conv_w, conv_b, dt_bias, a_log, d_skip, gate_gain, segment, mask_f):
    row_count = proj_x.shape[0]
    edge_rows = conv_w.shape[0] - 1
    inner = proj_x.shape[1]
    channels = inner + proj_bc.shape[1]
    head_count = dt_bias.shape[0]
    head_width = inner // head_count
    extended = jnp.concatenate([jnp.zeros((edge_rows, channels), jnp.float32), jnp.concatenate([proj_x, proj_bc], axis=1)], axis=0)
    seg_ext = jnp.concatenate([jnp.full((edge_rows,), -1, jnp.int32), segment]).astype(jnp.int32)
    activated = conv_silu(extended, seg_ext, conv_w, conv_b)
    ssm_in = activated[:, :inner].reshape(row_count, head_count, head_width)
    b_state = activated[:, inner:inner + NSTATE]
    c_state = activated[:, inner + NSTATE:]
    step_size = jax.nn.softplus(proj_dt + dt_bias[None, :]) * mask_f[:, None]
    decay_rate = -jnp.exp(a_log)
    span_count = row_count // SPAN
    seg_prev = jnp.concatenate([jnp.full((1,), -1, jnp.int32), segment]).astype(jnp.int32)[0:row_count:SPAN]

    def advance(state_now, items):
        piece_in, piece_dt, piece_b, piece_c, piece_seg, piece_prev = items
        result = span_output(piece_in, piece_dt, decay_rate, piece_b, piece_c, piece_seg, piece_prev, state_now)
        passing, state_out = span_state(piece_in, piece_dt, decay_rate, piece_b, piece_seg, piece_prev)
        return (passing[:, None, None] * state_now + state_out, result)
    start_state = jnp.zeros((head_count, head_width, NSTATE), jnp.float32)
    items = (ssm_in.reshape(span_count, SPAN, head_count, head_width), step_size.reshape(span_count, SPAN, head_count), b_state.reshape(span_count, SPAN, NSTATE), c_state.reshape(span_count, SPAN, NSTATE), segment.reshape(span_count, SPAN), seg_prev)
    final_state, outputs = lax.scan(advance, start_state, items)
    ssm_out = outputs.reshape(row_count, head_count, head_width) + d_skip[None, :, None] * ssm_in
    gated = ssm_out.reshape(row_count, inner) * jax.nn.silu(proj_z)
    inv_rms = lax.rsqrt(lax.optimization_barrier(jnp.mean(gated * gated, axis=1, keepdims=True)) + norm_eps)
    return gated * inv_rms * gate_gain[None, :]

def reference(x_in, norm_gain, w_z, w_x, w_bc, w_dt, w_out, conv_wx, conv_bx, conv_wbc, conv_bbc, dt_bias, a_log, d_skip, gate_gain, seq_lens, token_mask, d_out):
    group_rows = TOK_DEV * N_CTX
    inner = w_z.shape[1]
    w_in = jnp.concatenate([w_z, w_x, w_bc, w_dt], axis=1)
    conv_w = jnp.concatenate([conv_wx, conv_wbc], axis=1)
    conv_b = jnp.concatenate([conv_bx, conv_bbc])
    gain_f = norm_gain.astype(jnp.float32)
    positions = jnp.arange(group_rows, dtype=jnp.int32)
    split_two = 2 * inner
    split_three = 2 * inner + 2 * NSTATE

    def normalize(rows_in, gain_in):
        inv_rms = lax.rsqrt(lax.optimization_barrier(jnp.mean(rows_in * rows_in, axis=1, keepdims=True)) + norm_eps)
        return rows_in * inv_rms * gain_in[None, :]

    def group_step(totals, group_index):
        begin = (group_index * group_rows).astype(jnp.int32)
        rows_in = lax.dynamic_slice_in_dim(x_in, begin, group_rows, 0)
        grad_in = lax.dynamic_slice_in_dim(d_out, begin, group_rows, 0)
        mask_f = lax.dynamic_slice_in_dim(token_mask, begin, group_rows, 0).astype(jnp.float32)
        segment = segment_ids(positions, seq_lens[group_index])
        normed_f, norm_back = jax.vjp(normalize, rows_in, gain_f)
        normed = normed_f.astype(jnp.bfloat16)
        projected = jnp.dot(normed, w_in, preferred_element_type=jnp.float32).astype(jnp.bfloat16)
        projected = lax.optimization_barrier(projected).astype(jnp.float32)
        proj_z = projected[:, :inner]
        proj_x = projected[:, inner:split_two]
        proj_bc = projected[:, split_two:split_three]
        proj_dt = projected[:, split_three:]

        def mixing_call(z_arg, x_arg, bc_arg, dt_arg, cw_arg, cb_arg, bias_arg, alog_arg, skip_arg, ggain_arg):
            return mixer_piece(z_arg, x_arg, bc_arg, dt_arg, cw_arg, cb_arg, bias_arg, alog_arg, skip_arg, ggain_arg, segment, mask_f)
        mixed_f, mixer_back = jax.vjp(mixing_call, proj_z, proj_x, proj_bc, proj_dt, conv_w, conv_b, dt_bias, a_log, d_skip, gate_gain)
        mixed = mixed_f.astype(jnp.bfloat16)
        block_out = rows_in + jnp.dot(mixed, w_out.T, preferred_element_type=jnp.float32)
        grad_low = grad_in.astype(jnp.bfloat16)
        d_mixed = jnp.dot(grad_low, w_out, preferred_element_type=jnp.float32)
        d_w_out = jnp.dot(grad_low.T, mixed, preferred_element_type=jnp.float32)
        pieces = mixer_back(d_mixed)
        d_proj = jnp.concatenate([pieces[0], pieces[1], pieces[2], pieces[3]], axis=1).astype(jnp.bfloat16)
        d_w_in = jnp.dot(normed.T, d_proj, preferred_element_type=jnp.float32)
        d_normed = jnp.dot(d_proj, w_in.T, preferred_element_type=jnp.float32)
        d_rows, d_gain = norm_back(d_normed)
        d_input = grad_in + d_rows
        fresh = (d_gain, d_w_in, d_w_out, pieces[4], pieces[5], pieces[6], pieces[7], pieces[8], pieces[9])
        summed = tuple((older + newer for older, newer in zip(totals, fresh)))
        return (summed, (block_out, d_input))
    starting = (jnp.zeros(gain_f.shape, jnp.float32), jnp.zeros(w_in.shape, jnp.float32), jnp.zeros(w_out.shape, jnp.float32), jnp.zeros(conv_w.shape, jnp.float32), jnp.zeros(conv_b.shape, jnp.float32), jnp.zeros(dt_bias.shape, jnp.float32), jnp.zeros(a_log.shape, jnp.float32), jnp.zeros(d_skip.shape, jnp.float32), jnp.zeros(gate_gain.shape, jnp.float32))
    totals, stacked = lax.scan(group_step, starting, jnp.arange(GROUPS, dtype=jnp.int32))
    block_out = stacked[0].reshape(-1, x_in.shape[1])
    d_input = stacked[1].reshape(-1, x_in.shape[1])
    d_w_in = totals[1]
    return (block_out, d_input, totals[0], d_w_in[:, :inner], d_w_in[:, inner:split_two], d_w_in[:, split_two:split_three], d_w_in[:, split_three:], totals[2], totals[3][:, :inner], totals[4][:inner], totals[3][:, inner:], totals[4][inner:], totals[5], totals[6], totals[7], totals[8])
```

```python
import jax
import jax.numpy as jnp
from jax import lax
from jax.experimental import pallas as pl
from jax.experimental.pallas import tpu as pltpu
from jax.sharding import PartitionSpec as P

f32 = jnp.float32
bf16 = jnp.bfloat16
norm_eps = 1e-05
L = 128
NN = ((1,), (0,))
NT = ((1,), (1,))
TN = ((0,), (0,))
HI = lax.Precision.HIGHEST


def dot(a, b, dims=NN, precision=None):
    return lax.dot_general(a, b, (dims, ((), ())), preferred_element_type=f32, precision=precision)


def iota(shape, dim):
    return lax.broadcasted_iota(jnp.int32, shape, dim)


def sigmoid(v):
    return 1.0 / (1.0 + jnp.exp(-v))


def softplus(v):
    return jnp.maximum(v, 0.0) + jnp.log1p(jnp.exp(-jnp.abs(v)))


class Meta:
    def __init__(self, ref, sizes):
        self.ref, self.sizes = ref, sizes

    @property
    def base(self):
        return self.ref[0]

    @property
    def half(self):
        return self.ref[1]

    def bound(self, i):
        return self.ref[2 + i]

    def shard_row(self, i):
        return self.ref[2 + self.sizes["seqs"] + i]

    def block_row(self, i):
        return self.ref[2 + self.sizes["seqs"] + self.sizes["shards"] + i]

    def peer(self, k):
        return self.ref[2 + self.sizes["seqs"] + 2 * self.sizes["shards"] + k]

    def segment(self, pos):
        total = 0
        for i in range(self.sizes["seqs"]):
            total = total + jnp.where(pos >= self.bound(i), 1, 0)
        return jnp.where(pos < 0, -1, total)


def load_weights(meta, shards, scratch):
    rows = shards[0].shape[0]
    for i, shard in enumerate(shards):
        at = meta.shard_row(i) if len(shards) > 1 else 0
        if len(shards) > 1:
            at = pl.multiple_of(at, 16)
        scratch[pl.ds(at, rows), :] = shard[...]


def call(kernel, name, grid, ins, outs, scratch, flops, args):
    def spec(item):
        block, index = item[0], item[1]
        if block == "smem":
            return pl.BlockSpec(memory_space=pltpu.SMEM)
        return pl.BlockSpec(block, index)

    out_shape = [jax.ShapeDtypeStruct(o[2], o[3]) for o in outs]
    nbytes = sum(a.size * a.dtype.itemsize for a in args) + sum(
        o.size * o.dtype.itemsize for o in out_shape
    )
    return pl.pallas_call(
        kernel,
        name=name,
        grid=(grid,),
        in_specs=[spec(i) for i in ins],
        out_specs=[spec(o) for o in outs],
        out_shape=out_shape,
        scratch_shapes=scratch,
        cost_estimate=pl.CostEstimate(flops=flops, bytes_accessed=nbytes, transcendentals=0),
        compiler_params=pltpu.CompilerParams(dimension_semantics=("arbitrary",)),
    )(*args)


def whole(a):
    return (tuple(a.shape), lambda i, n=len(a.shape): (0,) * n)


def rows(a, count=L):
    return ((count, a.shape[1]), lambda i: (i, 0))


def cols(a):
    return ((a.shape[0], L), lambda i: (0, i))


def o_rows(shape, dtype, count=L):
    return ((count, shape[1]), lambda i: (i, 0), shape, dtype)


def o_cols(shape, dtype):
    return ((shape[0], L), lambda i: (0, i), shape, dtype)


def o_whole(shape, dtype):
    return (tuple(shape), lambda i, n=len(shape): (0,) * n, shape, dtype)


SMEM = ("smem", None)


def tri_leq():
    return jnp.where(iota((L, L), 0) <= iota((L, L), 1), 1.0, 0.0)


def pair_mask(hw, which):
    lane = iota((L, 128), 1)
    return (lane >= which * hw) & (lane < (which + 1) * hw)


def allowed_mask(meta, c):
    start = meta.base + c * L
    pt, ps = start + iota((L, L), 0), start + iota((L, L), 1)
    return (meta.segment(pt) == meta.segment(ps)) & (pt >= ps)


def chunk_edges(meta, c):
    start = meta.base + c * L
    return meta.segment(start - 1), meta.segment(start + L - 1)


def to_shift(meta, c, width, distance):
    pos = meta.base + c * L + iota((L, 128), 0)
    same = meta.segment(pos) == meta.segment(pos - distance)
    return tiled(jnp.where(same & (pos - distance >= 0), 1.0, 0.0), width)


def tiled(mask, width):
    return jnp.concatenate([mask] * (width // 128), axis=1)


def flag(cond):
    return jnp.where(cond, 1.0, 0.0).astype(f32)


def build(sizes):
    T, D, IN, N, H, TAPS = (sizes[k] for k in ("T", "D", "IN", "N", "H", "TAPS"))
    n_tp, n_ctx, nC = sizes["tp"], sizes["ctx"], sizes["T"] // L
    HW = IN // H
    HPT = 128 // HW
    SL = 2 * N // n_tp
    PAIRS = IN // 128
    DIRECT = sizes["shards"] > 1
    NSH = sizes["shards"]
    PK = IN + 128 + 2 * N
    EXT = IN + 2 * N
    SP = 16

    def expand_matrix():
        r, l = iota((128, IN), 0), iota((128, IN), 1)
        return jnp.where((r >= SL) & (r < SL + H) & (l // HW == r - SL), 1.0, 0.0)

    def head_select():
        r, l = iota((8, IN), 0), iota((8, IN), 1)
        return jnp.where((l // HW == r) & (r < H), 1.0, 0.0)

    def slab_select():
        r, l = iota((8, 128), 0), iota((8, 128), 1)
        return jnp.where((l == r + SL) & (r < H), 1.0, 0.0)

    def local_weights(cum, meta, c, last):
        return jnp.exp(cum[L - 1 : L, :] - cum) * in_segment(meta, c, last)

    def in_segment(meta, c, which):
        same = meta.segment(meta.base + c * L + iota((L, 128), 0)) == which
        return tiled(jnp.where(same, 1.0, 0.0), IN)

    def k_project(*refs):
        meta = Meta(refs[0], sizes)
        x_ref, xh_ref, cw_ref, hp_ref, hc_ref, mask_ref = refs[1:7]
        shards = refs[7 : 7 + NSH]
        (nb_ref, pr_ref, prh_ref, sm_ref, act_ref, dt_ref, cum_ref, dtr_ref, cumr_ref, hpre_ref,
         pp_ref, pack_ref) = refs[7 + NSH : 19 + NSH]
        gain_ref, w_ref, ext_ref, st_ref, ps_ref = refs[19 + NSH :]
        c = pl.program_id(0)

        @pl.when(c == 0)
        def _():
            load_weights(meta, shards, w_ref)
            xh = xh_ref[...]
            inv_h = lax.rsqrt(jnp.mean(xh * xh, axis=1, keepdims=True) + norm_eps)
            pick = jnp.where(iota((8, 128), 1) == SL + H, 1.0, 0.0).astype(bf16)
            gain_ref[...] = dot(pick, w_ref[:, IN : IN + 128], NT)
            nh = (xh * inv_h * gain_ref[...]).astype(bf16)
            ph = dot(nh, w_ref[...]).astype(bf16).astype(f32)
            prh_ref[...] = ph
            ext_ref[0:8, :IN] = ph[:, :IN]
            ext_ref[0:8, IN:] = ph[:, IN + 128 :]
            st_ref[...] = jnp.zeros((N, IN), f32)
            ps_ref[...] = jnp.ones((8, IN), f32)

        @pl.when(c > 0)
        def _():
            ext_ref[0:8, :] = ext_ref[L : L + 8, :]

        x = x_ref[...]
        inv = lax.rsqrt(jnp.mean(x * x, axis=1, keepdims=True) + norm_eps)
        nb = (x * inv * gain_ref[0:1, :]).astype(bf16)
        nb_ref[...] = nb
        pr = dot(nb, w_ref[...]).astype(bf16)
        pr_ref[...] = pr
        prf = pr.astype(f32)
        ext_ref[8 : 8 + L, :IN] = prf[:, :IN]
        ext_ref[8 : 8 + L, IN:] = prf[:, IN + 128 :]
        summed = jnp.zeros((L, EXT), f32) + cw_ref[TAPS : TAPS + 1, :]
        for k in range(TAPS):
            d = TAPS - 1 - k
            term = cw_ref[k : k + 1, :] * ext_ref[8 - d : 8 - d + L, :]
            summed = summed + (term if d == 0 else term * to_shift(meta, c, EXT, d))
        sm_ref[...] = summed
        act = summed * sigmoid(summed)
        act_ref[...] = act
        slab = pr[:, IN : IN + 128]
        hp, hc = hp_ref[...], hc_ref[...]
        mask8 = mask_ref[...]
        mask_c = dot(mask8, jnp.where(iota((8, IN), 0) == 0, 1.0, 0.0), TN)
        dt = softplus(dot(slab, expand_matrix().astype(bf16)) + hp[0:1, :]) * mask_c
        dtr = softplus(dot(slab_select().astype(bf16), slab, NT) + hc[:, 0:1]) * mask8[0:1, :]
        tri = tri_leq()
        cum = dot(tri, dt * hp[1:2, :], TN, HI)
        cumr = dot(dtr * hc[:, 1:2], tri, NN, HI)
        dt_ref[...], cum_ref[...], dtr_ref[...], cumr_ref[...] = dt, cum, dtr, cumr
        prev, last = chunk_edges(meta, c)
        xd = (dt * act[:, :IN]).astype(bf16)
        ws = local_weights(cum, meta, c, last)
        b = act[:, IN : IN + N].astype(bf16)
        passing = jnp.exp(cum[L - 1 : L, :]) * flag(prev == last)
        at = pl.multiple_of(c * N, N)
        st, ps = st_ref[...], ps_ref[...]
        hpre_ref[pl.ds(at, N), :] = st
        pp_ref[pl.ds(pl.multiple_of(c * 8, 8), 8), :] = ps
        st = passing * st + dot(b, (ws * xd.astype(f32)).astype(bf16), TN)
        ps = ps * passing
        st_ref[...], ps_ref[...] = st, ps

        @pl.when(c == nC - 1)
        def _():
            hpre_ref[nC * N : (nC + 1) * N, :] = st
            pp_ref[nC * 8 : nC * 8 + 8, :] = ps
            pack_ref[:N, :] = st.astype(bf16)
            pack_ref[N:, :] = jnp.concatenate([ps, ps], axis=0).astype(bf16)

    def project(meta, x, xh, cw, hp, hc, mask8, shards):
        outs = [
            o_rows((T, D), bf16), o_rows((T, PK), bf16), o_whole((8, PK), f32),
            o_rows((T, EXT), f32), o_rows((T, EXT), f32), o_rows((T, IN), f32),
            o_rows((T, IN), f32), o_cols((8, T), f32), o_cols((8, T), f32),
            o_whole(((nC + 1) * N, IN), f32), o_whole(((nC + 1) * 8, IN), f32),
            o_whole((N + SP, IN), bf16), o_whole((8, D), f32),
        ]
        ins = [SMEM, rows(x), whole(xh), whole(cw), whole(hp), whole(hc), cols(mask8)]
        ins += [whole(s) for s in shards]
        scratch = [
            pltpu.VMEM((D, PK), bf16), pltpu.VMEM((L + 8, EXT), f32),
            pltpu.VMEM((N, IN), f32), pltpu.VMEM((8, IN), f32),
        ]
        return call(k_project, "project", nC, ins, outs, scratch, 2 * T * D * PK,
                    [meta, x, xh, cw, hp, hc, mask8, *shards])

    def head_decay(meta_mask, cum, cumr, h):
        gap = cum[:, h * HW : h * HW + 1] - cumr[h : h + 1, :]
        return jnp.where(meta_mask, jnp.exp(gap), 0.0)

    def k_intra(mref, act_ref, dt_ref, cum_ref, cumr_ref, y_ref):
        meta = Meta(mref, sizes)
        c = pl.program_id(0)
        ok = allowed_mask(meta, c)
        b = act_ref[:, IN : IN + N].astype(bf16)
        cc = act_ref[:, IN + N :].astype(bf16)
        scores = dot(cc, b, NT)
        cum, cumr = cum_ref[...], cumr_ref[...]
        for p in range(PAIRS):
            sl = slice(p * 128, p * 128 + 128)
            xd = (dt_ref[:, sl] * act_ref[:, sl]).astype(bf16)
            y = None
            for j in range(HPT):
                g = (scores * head_decay(ok, cum, cumr, p * HPT + j)).astype(bf16)
                part = dot(g, xd)
                y = part if y is None else jnp.where(pair_mask(HW, j), part, y)
            y_ref[:, sl] = y

    def intra(meta, act, dt, cum, cumr):
        return call(k_intra, "intra", nC, [SMEM, rows(act), rows(dt), rows(cum), cols(cumr)],
                    [o_rows((T, IN), f32)], [], 4 * T * L * IN, [meta, act, dt, cum, cumr])[0]

    def k_gate(*refs):
        meta = Meta(refs[0], sizes)
        nb_ref, do_ref = refs[1:3]
        shards = refs[3 : 3 + NSH]
        z_ref, dm_ref, w_ref = refs[3 + NSH :]

        @pl.when(pl.program_id(0) == 0)
        def _():
            load_weights(meta, shards, w_ref)

        z_ref[...] = dot(nb_ref[...], w_ref[:, :IN]).astype(bf16)
        dm_ref[...] = dot(do_ref[...].astype(bf16), w_ref[:, IN:])

    def gate(meta, nb, d_out, shards):
        return call(k_gate, "gate", nC, [SMEM, rows(nb), rows(d_out)] + [whole(s) for s in shards],
                    [o_rows((T, IN), bf16), o_rows((T, IN), f32)],
                    [pltpu.VMEM((D, 2 * IN), bf16)], 4 * T * D * IN, [meta, nb, d_out, *shards])

    def chain(packs):
        total = None
        for pack in reversed(packs):
            state = pack[:N, :].astype(f32)
            total = state if total is None else state + pack[N : N + 1, :].astype(f32) * total
        return total

    def k_output(*refs):
        meta = Meta(refs[0], sizes)
        act_ref, cum_ref, y_ref, z_ref, dm_ref, hpre_ref, pp_ref, hp_ref, gg_ref = refs[1:10]
        packs = refs[10 : 10 + n_ctx - 1]
        yo_ref, stat_ref, ent_ref = refs[9 + n_ctx :]
        c = pl.program_id(0)

        @pl.when(c == 0)
        def _():
            ent_ref[...] = chain(packs)

        prev, _ = chunk_edges(meta, c)
        hin = (hpre_ref[...] + pp_ref[0:1, :] * ent_ref[...]).astype(bf16)
        cum = cum_ref[...]
        ent = jnp.exp(cum) * in_segment(meta, c, prev)
        y = y_ref[...] + ent * dot(act_ref[:, IN + N :].astype(bf16), hin)
        yo_ref[...] = y
        out = y + hp_ref[2:3, :] * act_ref[:, :IN]
        z = z_ref[...].astype(f32)
        gated = out * (z * sigmoid(z))
        ones = jnp.ones((8, IN), f32)
        sq = dot(ones, gated * gated, NT, HI)
        bd = dot(ones, dm_ref[...] * gg_ref[0:1, :] * gated, NT, HI)
        stat_ref[...] = jnp.where(iota((8, L), 0) == 0, sq, bd)

    def output(meta, act, cum, y, z, dm, hpre, pp, hp, gg, packs):
        ins = [SMEM, rows(act), rows(cum), rows(y), rows(z), rows(dm), rows(hpre, N), rows(pp, 8),
               whole(hp), whole(gg)] + [whole(p) for p in packs]
        outs = [o_rows((T, IN), f32), o_cols((8, T), f32), o_whole((N, IN), f32)]
        return call(k_output, "output", nC, ins, outs, [], 4 * T * IN * N,
                    [meta, act, cum, y, z, dm, hpre, pp, hp, gg, *packs])

    def k_norm(*refs):
        meta = Meta(refs[0], sizes)
        act_ref, cum_ref, y_ref, z_ref, dm_ref, hp_ref, gg_ref = refs[1:8]
        stats = refs[8 : 8 + n_tp]
        mix_ref, dz_ref, dy_ref, suf_ref, psuf_ref, pack_ref, sums_ref = refs[8 + n_tp : 15 + n_tp]
        st_ref, ps_ref = refs[15 + n_tp :]
        c = nC - 1 - pl.program_id(0)

        @pl.when(pl.program_id(0) == 0)
        def _():
            st_ref[...] = jnp.zeros((N, IN), f32)
            ps_ref[...] = jnp.ones((8, IN), f32)
            sums_ref[...] = jnp.zeros((8, IN), f32)

        stat = stats[0][...]
        for s in stats[1:]:
            stat = stat + s[...]
        inner = float(IN * n_tp)
        inv_r = lax.rsqrt(stat[0:1, :] / inner + norm_eps)
        beta_r = inv_r * inv_r * inv_r * stat[1:2, :] / inner
        row = iota((8, L), 0)
        both = jnp.where(row == 0, inv_r, jnp.where(row == 1, beta_r, 0.0))
        inv = dot(both, jnp.where(iota((8, IN), 0) == 0, 1.0, 0.0), TN, HI)
        beta = dot(both, jnp.where(iota((8, IN), 0) == 1, 1.0, 0.0), TN, HI)
        gg, skip = gg_ref[0:1, :], hp_ref[2:3, :]
        x = act_ref[:, :IN]
        out = y_ref[...] + skip * x
        z = z_ref[...].astype(f32)
        sig = sigmoid(z)
        ga = z * sig
        gated = out * ga
        dm = dm_ref[...]
        normal = gated * inv
        mix_ref[...] = (normal * gg).astype(bf16)
        dg = dm * gg * inv - gated * beta
        dz_ref[...] = (dg * out * sig * (1.0 + z * (1.0 - sig))).astype(bf16)
        dy = dg * ga
        dyb = dy.astype(bf16)
        dy_ref[...] = dyb
        s0 = jnp.sum(dm * normal, axis=0, keepdims=True)
        s1 = jnp.sum(dy * x, axis=0, keepdims=True)
        r8 = iota((8, IN), 0)
        sums_ref[...] += jnp.where(r8 == 0, s0, jnp.where(r8 == 1, s1, 0.0))
        prev, last = chunk_edges(meta, c)
        cum = cum_ref[...]
        ent = jnp.exp(cum) * in_segment(meta, c, prev)
        passing = jnp.exp(cum[L - 1 : L, :]) * flag(prev == last)
        st, ps = st_ref[...], ps_ref[...]
        suf_ref[...] = st
        psuf_ref[...] = ps
        cc = act_ref[:, IN + N :].astype(bf16)
        st = passing * st + dot(cc, (ent * dyb.astype(f32)).astype(bf16), TN)
        ps = passing * ps
        st_ref[...], ps_ref[...] = st, ps

        @pl.when(c == 0)
        def _():
            pack_ref[:N, :] = st.astype(bf16)
            pack_ref[N:, :] = jnp.concatenate([ps, ps], axis=0).astype(bf16)

    def norm(meta, act, cum, y, z, dm, hp, gg, stats):
        def back(item):
            block, index = item[0], item[1]
            return (block, lambda i: index(nC - 1 - i)) + tuple(item[2:])

        ins = [SMEM] + [back(rows(a)) for a in (act, cum, y, z, dm)] + [whole(hp), whole(gg)]
        ins += [back(cols(s)) for s in stats]
        outs = [back(o_rows((T, IN), bf16)), back(o_rows((T, IN), bf16)), back(o_rows((T, IN), bf16)),
                back(o_rows((nC * N, IN), f32, N)), back(o_rows((nC * 8, IN), f32, 8)),
                o_whole((N + SP, IN), bf16), o_whole((8, IN), f32)]
        scratch = [pltpu.VMEM((N, IN), f32), pltpu.VMEM((8, IN), f32)]
        return call(k_norm, "norm", nC, ins, outs, scratch, 2 * T * IN * N,
                    [meta, act, cum, y, z, dm, hp, gg, *stats])

    def k_intra_back(mref, act_ref, dt_ref, cum_ref, cumr_ref, dy_ref, dxd_ref, dbc_ref):
        meta = Meta(mref, sizes)
        c = pl.program_id(0)
        ok = allowed_mask(meta, c)
        b = act_ref[:, IN : IN + N].astype(bf16)
        cc = act_ref[:, IN + N :].astype(bf16)
        scores = dot(cc, b, NT)
        cum, cumr = cum_ref[...], cumr_ref[...]
        d_scores = jnp.zeros((L, L), f32)
        for p in range(PAIRS):
            sl = slice(p * 128, p * 128 + 128)
            xd = (dt_ref[:, sl] * act_ref[:, sl]).astype(bf16)
            dy = dy_ref[:, sl]
            dxd = None
            for j in range(HPT):
                decay = head_decay(ok, cum, cumr, p * HPT + j)
                g = (scores * decay).astype(bf16)
                part = dot(g, dy, TN)
                dxd = part if dxd is None else jnp.where(pair_mask(HW, j), part, dxd)
                own = jnp.where(pair_mask(HW, j), dy.astype(f32), 0.0).astype(bf16)
                d_scores = d_scores + dot(own, xd, NT) * decay
            dxd_ref[:, sl] = dxd
        ds = d_scores.astype(bf16)
        dbc_ref[:, :N] = dot(ds, cc, TN)
        dbc_ref[:, N:] = dot(ds, b)

    def intra_back(meta, act, dt, cum, cumr, dy):
        return call(k_intra_back, "intra_back", nC,
                    [SMEM, rows(act), rows(dt), rows(cum), cols(cumr), rows(dy)],
                    [o_rows((T, IN), f32), o_rows((T, 2 * N), f32)], [], 8 * T * L * IN,
                    [meta, act, dt, cum, cumr, dy])

    def write_blocks(meta, total, outs):
        if not DIRECT:
            outs[0][...] = total[...].astype(bf16)
            return
        br = D // NSH
        for i in range(NSH):
            at = pl.multiple_of(meta.block_row(i), 8)
            outs[i // n_ctx][(i % n_ctx) * br : (i % n_ctx + 1) * br, :] = total[
                pl.ds(at, br), :
            ].astype(bf16)

    n_groups = NSH // n_ctx if DIRECT else 1
    group_rows = n_ctx * (D // NSH) if DIRECT else D

    def split_rows(meta, c, value, keep, send):
        at = pl.multiple_of(lax.rem(c, nC // 2) * L, L)

        @pl.when(c // (nC // 2) == meta.half)
        def _():
            keep[pl.ds(at, L), :] = value

        @pl.when(c // (nC // 2) != meta.half)
        def _():
            send[pl.ds(at, L), :] = value.astype(bf16)

    def k_outer(*refs):
        meta = Meta(refs[0], sizes)
        nb_ref, do_ref, mix_ref, dz_ref = refs[1:5]
        shards = refs[5 : 5 + NSH]
        outs = refs[5 + NSH : 5 + NSH + n_groups]
        keep_ref, send_ref = refs[5 + NSH + n_groups : 7 + NSH + n_groups]
        w_ref, total = refs[7 + NSH + n_groups :]
        c = pl.program_id(0)

        @pl.when(c == 0)
        def _():
            load_weights(meta, shards, w_ref)
            total[...] = jnp.zeros((D, 2 * IN), f32)

        total[:, :IN] += dot(nb_ref[...], dz_ref[...], TN)
        total[:, IN:] += dot(do_ref[...].astype(bf16), mix_ref[...], TN)
        split_rows(meta, c, dot(mix_ref[...], w_ref[:, IN:], NT), keep_ref, send_ref)

        @pl.when(c == nC - 1)
        def _():
            write_blocks(meta, total, outs)

    def outer(meta, nb, d_out, mix, dz, shards):
        outs = [o_whole((group_rows, 2 * IN), bf16)] * n_groups
        outs += [o_whole((T // 2, D), f32), o_whole((T // 2, D), bf16)]
        ins = [SMEM, rows(nb), rows(d_out), rows(mix), rows(dz)] + [whole(s) for s in shards]
        scratch = [pltpu.VMEM((D, 2 * IN), bf16), pltpu.VMEM((D, 2 * IN), f32)]
        got = call(k_outer, "outer", nC, ins, outs, scratch, 6 * T * D * IN,
                   [meta, nb, d_out, mix, dz, *shards])
        return got[:n_groups], got[n_groups], got[n_groups + 1]

    def k_scan_back(*refs):
        meta = Meta(refs[0], sizes)
        (act_ref, sm_ref, pr_ref, dt_ref, cum_ref, dtr_ref, y_ref, dy_ref, dxd_ref, dbc_ref, hpre_ref,
         hnext_ref, pp_ref, pnext_ref, ent_ref, suf_ref, psuf_ref, hp_ref, hc_ref, mask_ref) = refs[1:21]
        packs = refs[21 : 20 + n_ctx]
        dsx_ref, ddt_ref, sums_ref, edge_ref = refs[20 + n_ctx : 24 + n_ctx]
        slices = refs[24 + n_ctx : 24 + n_ctx + n_tp]
        edges = refs[24 + n_ctx + n_tp : 23 + n_ctx + 2 * n_tp]
        exit_ref = refs[23 + n_ctx + 2 * n_tp]
        c = pl.program_id(0)

        @pl.when(c == 0)
        def _():
            exit_ref[...] = chain(packs)
            sums_ref[...] = jnp.zeros((16, 128), f32)

        prev, last = chunk_edges(meta, c)
        hin = hpre_ref[...] + pp_ref[0:1, :] * ent_ref[...]
        hout = hnext_ref[...] + pnext_ref[0:1, :] * ent_ref[...]
        dh = suf_ref[...] + psuf_ref[0:1, :] * exit_ref[...]
        hinb, dhb = hin.astype(bf16), dh.astype(bf16)
        cum, dt, x = cum_ref[...], dt_ref[...], act_ref[:, :IN]
        b = act_ref[:, IN : IN + N].astype(bf16)
        ws = local_weights(cum, meta, c, last)
        ent = jnp.exp(cum) * in_segment(meta, c, prev)
        xd = (dt * x).astype(bf16).astype(f32)
        dyf = dy_ref[...].astype(f32)
        leaving = dot(b, dhb)
        wx = (ws * xd).astype(bf16)
        dxd_in = dxd_ref[...]
        dxd = dxd_in + ws * leaving
        db = dbc_ref[:, :N] + dot(wx, dhb, NT)
        dc = dbc_ref[:, N:] + dot((ent * dyf).astype(bf16), hinb, NT)
        hs = head_select()
        dcum = dot(hs, dyf * y_ref[...] - xd * dxd_in - wx.astype(f32) * leaving, NT, HI)
        final = dot(hs, jnp.zeros((8, IN), f32) + jnp.sum(dhb.astype(f32) * hout, axis=0, keepdims=True), NT, HI)
        da = dot(dcum, tri_leq(), NT, HI) + final[:, 0:1]
        hc = hc_ref[...]
        dtr, mask8 = dtr_ref[...], mask_ref[...]
        ddt = da * hc[:, 1:2] + dot(hs, dxd * x, NT, HI)
        slab = pr_ref[:, IN : IN + 128]
        pre_r = dot(slab_select().astype(bf16), slab, NT) + hc[:, 0:1]
        dpre = ddt * mask8[0:1, :] * sigmoid(pre_r)
        ddt_ref[...] = dot(dpre.astype(bf16), slab_select().astype(bf16), TN).astype(bf16)
        ones = jnp.ones((L, 128), f32)
        sums_ref[0:8, :] += dot(dpre, ones, NN, HI)
        sums_ref[8:16, :] += dot(da * dtr, ones, NN, HI)
        sm = sm_ref[...]
        sig = sigmoid(sm)
        dsilu = sig * (1.0 + sm * (1.0 - sig))
        dsx = (hp_ref[2:3, :] * dyf + dt * dxd) * dsilu[:, :IN]
        dsx_ref[...] = dsx
        dsb = (jnp.concatenate([db, dc], axis=1) * dsilu[:, IN:]).astype(bf16)
        quarter = c // (nC // 2)
        at = pl.multiple_of(lax.rem(c, nC // 2) * L, L)
        r, l = iota((2 * N, 128), 0), iota((2 * N, 128), 1)
        for k in range(n_tp):
            left = meta.peer(k) * SL
            lane0 = quarter * SL
            pick = jnp.where((r - left == l - lane0) & (l >= lane0) & (l < lane0 + SL), 1.0, 0.0)
            part = dot(dsb, pick.astype(bf16)).astype(bf16)

            @pl.when(quarter == 0)
            def _():
                slices[k][pl.ds(at, L), :] = part

            @pl.when(quarter != 0)
            def _():
                slices[k][pl.ds(at, L), :] = slices[k][pl.ds(at, L), :] + part

            @pl.when(c == 0)
            def _():
                if k == 0:
                    edge_ref[:, :IN] = dsx[0:8, :]
                    edge_ref[:, IN:] = part[0:8, :].astype(f32)
                else:
                    edges[k - 1][...] = part[0:8, :].astype(f32)

    def scan_back(meta, act, sm, pr, dt, cum, dtr, y, dy, dxd, dbc, hpre, pp, ent, suf, psuf, hp, hc,
                  mask8, packs):
        def later(item):
            return (item[0], lambda i: item[1](i + 1))

        ins = [SMEM, rows(act), rows(sm), rows(pr), rows(dt), rows(cum), cols(dtr), rows(y), rows(dy),
               rows(dxd), rows(dbc), rows(hpre, N), later(rows(hpre, N)), rows(pp, 8),
               later(rows(pp, 8)), whole(ent), rows(suf, N), rows(psuf, 8), whole(hp), whole(hc),
               cols(mask8)] + [whole(p) for p in packs]
        outs = [o_rows((T, IN), f32), o_rows((T, 128), bf16), o_whole((16, 128), f32),
                o_whole((8, IN + 128), f32)]
        outs += [o_whole((T // 2, 128), bf16)] * n_tp + [o_whole((8, 128), f32)] * (n_tp - 1)
        got = call(k_scan_back, "scan_back", nC, ins, outs, [pltpu.VMEM((N, IN), f32)],
                   6 * T * IN * N,
                   [meta, act, sm, pr, dt, cum, dtr, y, dy, dxd, dbc, hpre, hpre, pp, pp, ent, suf,
                    psuf, hp, hc, mask8, *packs])
        return got[:4], got[4 : 4 + n_tp], got[4 + n_tp :]

    PW = IN + 128
    br9 = D // NSH

    def k_conv_back(*refs):
        meta = Meta(refs[0], sizes)
        nb_ref, pr_ref, prp_ref, prh_ref, dz_ref, ddt_ref, dsx_ref, dsn_ref = refs[1:9]
        cw_ref, sums_ref, ssum_ref, edge_ref = refs[9:13]
        at = 13
        slices, at = refs[at : at + n_tp], at + n_tp
        edges, at = refs[at : at + n_tp - 1], at + n_tp - 1
        shards, at = refs[at : at + NSH], at + NSH
        zshards, at = refs[at : at + NSH], at + NSH
        g_ref, keep_ref, send_ref, w_ref, wz_ref, ex_ref, px_ref, sl_ref, total, tap_ref = refs[at:]
        c = pl.program_id(0)

        @pl.when(c == 0)
        def _():
            load_weights(meta, shards, w_ref)
            load_weights(meta, zshards, wz_ref)
            total[...] = jnp.zeros((D, PW), f32)
            tap_ref[...] = jnp.zeros((8, PW), f32)
            sl = slices[0][...].astype(f32)
            for s in slices[1:]:
                sl = sl + s[...].astype(f32)
            low = iota((T // 2, 128), 1) < SL
            sl_ref[0 : T // 2, :] = jnp.where(low, sl, 0.0)
            sl_ref[T // 2 : T, :] = jnp.where(low, pltpu.roll(sl, 128 - SL, 1), 0.0)
            e = edge_ref[:, IN:]
            for s in edges:
                e = e + s[...]
            sl_ref[T : T + 8, :] = jnp.where(iota((8, 128), 1) < SL, e, 0.0)

        here = pl.multiple_of(c * L, L)
        after = pl.multiple_of(c * L + L, L)
        ex_ref[0:L, :IN] = dsx_ref[...]
        ex_ref[0:L, IN:] = sl_ref[pl.ds(here, L), :]
        ex_ref[L : L + 8, IN:] = sl_ref[pl.ds(after, 8), :]
        ex_ref[L : L + 8, :IN] = jnp.where(c == nC - 1, edge_ref[:, :IN], dsn_ref[...])
        low = iota((L, PW), 1) < IN + SL
        px_ref[8 : 8 + L, :] = pr_ref[:, :PW].astype(f32)
        px_ref[0:8, :] = jnp.where(c == 0, prh_ref[:, :PW], prp_ref[8:16, :PW].astype(f32))
        cw = cw_ref[...]
        ds = ex_ref[0:L, :]
        dpre = jnp.zeros((L, PW), f32)
        pos = meta.base + c * L + iota((L, 128), 0)
        seg = meta.segment(pos)
        group = T * n_ctx
        r8 = iota((8, PW), 0)
        taps = jnp.where(r8 == TAPS, jnp.sum(ds, axis=0, keepdims=True), 0.0)
        for k in range(TAPS):
            d = TAPS - 1 - k
            reach = cw[k : k + 1, :] * ex_ref[d : d + L, :]
            prior = ds * px_ref[8 - d : 8 - d + L, :]
            if d > 0:
                ahead = jnp.where((seg == meta.segment(pos + d)) & (pos + d < group), 1.0, 0.0)
                reach = reach * tiled(ahead, PW)
                prior = prior * to_shift(meta, c, PW, d)
            dpre = dpre + reach
            taps = taps + jnp.where(r8 == k, jnp.sum(prior, axis=0, keepdims=True), 0.0)
        tap_ref[...] += taps
        dpre = jnp.where(low, dpre, 0.0)
        dproj = dpre.astype(bf16)
        dslab = (dpre[:, IN:] + ddt_ref[...].astype(f32)).astype(bf16)
        dproj = jnp.concatenate([dproj[:, :IN], dslab], axis=1)
        nb = nb_ref[...]
        total[...] += dot(nb, dproj, TN)
        q = dot(dproj, w_ref[:, :PW], NT) + dot(dz_ref[...], wz_ref[:, :IN], NT)
        split_rows(meta, c, q, keep_ref, send_ref)

        @pl.when(c == nC - 1)
        def _():
            low8 = iota((8, PW), 1) < IN + SL
            s = ssum_ref[...]
            zero = jnp.zeros((8, 128), f32)
            pad = jnp.concatenate([s, jnp.zeros((8, PW - IN), f32)], axis=1)
            first = jnp.where(low8, tap_ref[...], 0.0)
            first = jnp.where(r8 == 5, pad[0:1, :], jnp.where(r8 == 6, pad[1:2, :], first))
            lead = first.astype(bf16).astype(f32)
            first = jnp.where(r8 == 7, (first - lead)[TAPS : TAPS + 1, :], first)
            pair = [sums_ref[0:8, :], sums_ref[8:16, :]]
            rest = [p - p.astype(bf16).astype(f32) for p in pair]
            tail = pair + rest + [zero] * (PW // 128 - 4)
            small = jnp.concatenate([first, jnp.concatenate(tail, axis=1)], axis=0).astype(bf16)
            for i in range(NSH):
                g_ref[i * (br9 + 16) : i * (br9 + 16) + br9, :] = total[
                    i * br9 : (i + 1) * br9, :
                ].astype(bf16)
                g_ref[i * (br9 + 16) + br9 : (i + 1) * (br9 + 16), :] = small

    def conv_back(meta, nb, pr, prh, dz, ddt, dsx, cw9, sums, ssum, edge, slices, edges, shards,
                  zshards):
        step = L // 16
        prior = ((16, PK), lambda i: (jnp.maximum(i * step - 1, 0), 0))
        after = ((8, IN), lambda i: (jnp.minimum((i + 1) * (L // 8), T // 8 - 1), 0))
        ins = [SMEM, rows(nb), rows(pr), prior, whole(prh), rows(dz), rows(ddt), rows(dsx), after,
               whole(cw9), whole(sums), whole(ssum), whole(edge)]
        ins += [whole(a) for a in (*slices, *edges, *shards, *zshards)]
        outs = [o_whole((NSH * (br9 + 16), PW), bf16), o_whole((T // 2, D), f32),
                o_whole((T // 2, D), bf16)]
        scratch = [pltpu.VMEM((D, PK), bf16), pltpu.VMEM((D, 2 * IN), bf16),
                   pltpu.VMEM((L + 8, PW), f32), pltpu.VMEM((L + 8, PW), f32),
                   pltpu.VMEM((T + 8, 128), f32), pltpu.VMEM((D, PW), f32),
                   pltpu.VMEM((8, PW), f32)]
        return call(k_conv_back, "conv_back", nC, ins, outs, scratch, 4 * T * D * (PW + IN),
                    [meta, nb, pr, pr, prh, dz, ddt, dsx, dsx, cw9, sums, ssum, edge, *slices, *edges,
                     *shards, *zshards])

    return dict(project=project, intra=intra, gate=gate, output=output, norm=norm,
                intra_back=intra_back, outer=outer, scan_back=scan_back, conv_back=conv_back,
                SL=SL, PW=PW)


def local(x_in, norm_gain, w_z, w_x, w_bc, w_dt, w_out, conv_wx, conv_bx, conv_wbc, conv_bbc, dt_bias,
          a_log, d_skip, gate_gain, seq_lens, token_mask, d_out):
    T, D = x_in.shape
    H, IN, N, TAPS = dt_bias.shape[0], w_z.shape[1], w_bc.shape[1] // 2, conv_wx.shape[0]
    n_sh, n_ctx, n_tp = (lax.axis_size(a) for a in ("shard", "ctx", "tp"))
    me_s, me_c, me_t = (lax.axis_index(a) for a in ("shard", "ctx", "tp"))
    direct = n_sh == 2 and n_ctx == 4
    NSH = n_sh * n_ctx if direct else 1
    seqs = seq_lens.shape[1]
    sizes = dict(T=T, D=D, IN=IN, N=N, H=H, TAPS=TAPS, tp=n_tp, ctx=n_ctx, seqs=seqs, shards=NSH)
    ops = build(sizes)
    SL, PW = ops["SL"], ops["PW"]
    HW = IN // H
    br = w_z.shape[0]

    def ring(count, step):
        return [(i, (i + step) % count) for i in range(count)]

    def xor(count, step):
        return [(i, i ^ step) for i in range(count)]

    def gather(part):
        if not direct:
            return [lax.all_gather(part, ("shard", "ctx"), axis=0, tiled=True)]
        here = [part] + [lax.ppermute(part, "ctx", ring(n_ctx, k)) for k in range(1, n_ctx)]
        return here + [lax.ppermute(p, "shard", ring(n_sh, 1)) for p in here]

    which = jnp.arange(NSH, dtype=jnp.int32)
    src = (((me_s + which // n_ctx) % n_sh) * n_ctx + (me_c - which % n_ctx + n_ctx) % n_ctx) * br
    dst = (((me_s + which // n_ctx) % n_sh) * n_ctx + (me_c + which % n_ctx) % n_ctx) * br
    peers = me_t ^ jnp.arange(n_tp, dtype=jnp.int32)
    head = jnp.stack([me_c * T, me_t % 2]).astype(jnp.int32)
    meta = jnp.concatenate([head, jnp.cumsum(seq_lens[0]), src, dst, peers]).astype(jnp.int32)

    gain = norm_gain.astype(f32)[:, None]
    w_slice = lax.dynamic_slice_in_dim(w_bc, me_t * SL, SL, 1)
    first = jnp.concatenate(
        [w_x, w_slice, w_dt, norm_gain[:, None], jnp.zeros((br, 127 - SL - H), bf16), w_bc], axis=1
    )
    second = jnp.concatenate([w_z, w_out], axis=1)
    x_tail = lax.ppermute(x_in[T - 8 :], "ctx", [(i, i + 1) for i in range(n_ctx - 1)])
    shards = gather(first)
    second, _ = lax.optimization_barrier((second, shards[-1]))
    shards2 = gather(second)

    cw = jnp.concatenate([jnp.concatenate([conv_wx, conv_wbc], axis=1),
                          jnp.concatenate([conv_bx, conv_bbc])[None, :],
                          jnp.zeros((8 - TAPS - 1, IN + 2 * N), f32)], axis=0)
    cw9 = jnp.concatenate([cw[:, :IN], lax.dynamic_slice_in_dim(cw, IN + me_t * SL, SL, 1),
                           jnp.zeros((8, 128 - SL), f32)], axis=1)
    rate = -jnp.exp(a_log)
    heads = jnp.stack([dt_bias, rate, d_skip])
    hp = jnp.pad(jnp.repeat(heads, HW, axis=1), ((0, 5), (0, 0)))
    hc = jnp.pad(heads.T, ((0, 8 - H), (0, 125)))
    gg = jnp.broadcast_to(gate_gain[None, :], (8, IN))
    mask8 = jnp.broadcast_to(token_mask.astype(f32)[None, :], (8, T))

    (nb, pr, prh, sm, act, dt, cum, dtr, cumr, hpre, pp, pack, gain_row) = ops["project"](
        meta, x_in, x_tail, cw, hp, hc, mask8, shards)
    packs = [lax.ppermute(pack, "ctx", [(i, i + k) for i in range(n_ctx - k)]) for k in range(1, n_ctx)]
    y_in = ops["intra"](meta, act, dt, cum, cumr)
    z, dm = ops["gate"](meta, nb, d_out, shards2)
    y, stat, entry = ops["output"](meta, act, cum, y_in, z, dm, hpre, pp, hp, gg, packs)
    stats = [stat] + [lax.ppermute(stat, "tp", xor(n_tp, k)) for k in range(1, n_tp)]
    mix, dz, dy, suf, psuf, bpack, ssum = ops["norm"](meta, act, cum, y, z, dm, hp, gg, stats)
    bpacks = [lax.ppermute(bpack, "ctx", [(i + k, i) for i in range(n_ctx - k)]) for k in range(1, n_ctx)]
    dxd, dbc = ops["intra_back"](meta, act, dt, cum, cumr, dy)
    groups, b_keep, b_send = ops["outer"](meta, nb, d_out, mix, dz, shards2)

    def tp_sum(keep, send):
        pair = (keep + lax.ppermute(send, "tp", xor(n_tp, 1)).astype(f32)).astype(bf16)
        total = pair.astype(f32)
        for k in range(2, n_tp, 2):
            total = total + lax.ppermute(pair, "tp", xor(n_tp, k)).astype(f32)
        return total

    def both_halves(part):
        mine = part.astype(bf16)
        other = lax.ppermute(mine, "tp", xor(n_tp, 1))
        flip = me_t % 2 == 1
        low, high = jnp.where(flip, other, mine), jnp.where(flip, mine, other)
        return jnp.concatenate([low, high], axis=0).astype(f32)

    (dsx, ddt, sums, edge), slices, edges = ops["scan_back"](
        meta, act, sm, pr, dt, cum, dtr, y, dy, dxd, dbc, hpre, pp, entry, suf, psuf, hp, hc, mask8,
        bpacks)
    got_slices = [slices[0]] + [lax.ppermute(slices[k], "tp", xor(n_tp, k)) for k in range(1, n_tp)]
    got_edge = lax.ppermute(edge, "ctx", [(i + 1, i) for i in range(n_ctx - 1)])
    got_edges = [
        lax.ppermute(edges[k - 1], ("ctx", "tp"),
                     [((i + 1) * n_tp + j, i * n_tp + (j ^ k)) for i in range(n_ctx - 1) for j in range(n_tp)])
        for k in range(1, n_tp)
    ]
    grads, q_keep, q_send = ops["conv_back"](
        meta, nb, pr, prh, dz, ddt, dsx, cw9, sums, ssum, got_edge, got_slices, got_edges, shards,
        shards2)

    block_half = tp_sum(b_keep, b_send)
    block_out = x_in + both_halves(block_half)

    if direct:
        keep, send = groups
        other = lax.ppermute(send, "shard", ring(n_sh, 1))
        total = None
        for r in range(n_ctx):
            part = keep[r * br : (r + 1) * br].astype(f32) + other[r * br : (r + 1) * br].astype(f32)
            if r > 0:
                part = lax.ppermute(part.astype(bf16), "ctx", ring(n_ctx, r)).astype(f32)
            total = part if total is None else total + part
        moved = lax.all_to_all(grads, ("shard", "ctx"), 0, 0, tiled=True)
        moved = jnp.sum(moved.reshape(NSH, br + 16, PW).astype(f32), axis=0)
        g_first, small = moved[:br], moved[br:]
    else:
        axes = ("shard", "ctx")
        total = lax.psum_scatter(groups[0].astype(f32), axes, scatter_dimension=0, tiled=True)
        g_first = lax.psum_scatter(grads[:D].astype(f32), axes, scatter_dimension=0, tiled=True)
        small = lax.psum(grads[D:].astype(f32), axes)
    bias_row = small[TAPS] + small[7]
    sums = small[8 : 8 + H, 0:256] + small[8 : 8 + H, 256:512]

    q_half = tp_sum(q_keep, q_send)
    x_half = lax.dynamic_slice_in_dim(x_in, (me_t % 2) * (T // 2), T // 2, 0)
    inv = lax.rsqrt(jnp.mean(x_half * x_half, axis=1, keepdims=True) + norm_eps)
    q_half = q_half * gain_row[0:1, :]
    row_dot = jnp.sum(q_half * x_half, axis=1, keepdims=True)
    d_input = d_out + both_halves(q_half * inv - x_half * (inv * inv * inv) * row_dot / D)

    g_z, g_out = total[:, :IN], total[:, IN:]
    w_slab = jnp.concatenate([w_slice, w_dt], axis=1).astype(f32)
    g_slab = g_first[:, IN : IN + SL + H]
    d_gain = jnp.sum(w_z.astype(f32) * g_z + w_x.astype(f32) * g_first[:, :IN], axis=1)
    d_gain = (d_gain + jnp.sum(w_slab * g_slab, axis=1)) / gain[:, 0]
    last = jnp.concatenate([
        jnp.concatenate([g_slab[:, :SL], d_gain[:, None], jnp.zeros((br, 127 - SL), f32)], axis=1),
        jnp.pad(jnp.concatenate([small[:TAPS], bias_row[None, :]], axis=0)[:, IN : IN + SL],
                ((0, 7 - TAPS), (0, 128 - SL)))], axis=0)
    last = lax.all_gather(last, "tp")
    d_w_bc = jnp.concatenate([last[k, :br, :SL] for k in range(n_tp)], axis=1)
    d_norm_gain = jnp.sum(last[:, :br, SL], axis=0)
    d_cbc = jnp.concatenate([last[k, br : br + TAPS + 1, :SL] for k in range(n_tp)], axis=1)
    return (
        block_out, d_input, d_norm_gain,
        g_z, g_first[:, :IN], d_w_bc, g_slab[:, SL:], g_out,
        small[:TAPS, :IN], bias_row[:IN], d_cbc[:TAPS], d_cbc[TAPS],
        sums[:, 0], sums[:, 128] * rate,
        jnp.sum(small[6, :IN].reshape(H, HW), axis=1), small[5, :IN],
    )


def solution(mesh):
    row = ("shard", "ctx")
    in_specs = (
        P(row, None), P(row), P(row, "tp"), P(row, "tp"), P(row, None), P(row, "tp"), P(row, "tp"),
        P(None, "tp"), P("tp"), P(), P(), P("tp"), P("tp"), P("tp"), P("tp"), P("shard", None), P(row),
        P(row, None),
    )
    out_specs = (
        P(row, None), P(row, None), P(row), P(row, "tp"), P(row, "tp"), P(row, None), P(row, "tp"),
        P(row, "tp"), P(None, "tp"), P("tp"), P(), P(), P("tp"), P("tp"), P("tp"), P("tp"),
    )
    return jax.shard_map(local, mesh=mesh, in_specs=in_specs, out_specs=out_specs, check_vma=False)
```

```python
import jax
import jax.numpy as jnp
from jax import lax
from jax.experimental import pallas as pl
from jax.experimental.pallas import tpu as pltpu
from jax.sharding import PartitionSpec as P


f32 = jnp.float32
bf16 = jnp.bfloat16
norm_eps = 1e-05
L = 128
NN = ((1,), (0,))
NT = ((1,), (1,))
TN = ((0,), (0,))
HI = lax.Precision.HIGHEST


def dot(a, b, dims=NN, precision=None):
    return lax.dot_general(a, b, (dims, ((), ())), preferred_element_type=f32, precision=precision)


def split(v):
    if v.dtype == bf16:
        return v, None
    high = v.astype(bf16)
    return high, (v - high.astype(f32)).astype(bf16)


def dot3(a, b, dims=NN):
    ah, al = split(a) if not isinstance(a, tuple) else a
    bh, bl = split(b) if not isinstance(b, tuple) else b
    total = dot(ah, bh, dims)
    if bl is not None:
        total = total + dot(ah, bl, dims)
    if al is not None:
        total = total + dot(al, bh, dims)
    return total


def iota(shape, dim):
    return lax.broadcasted_iota(jnp.int32, shape, dim)


def sigmoid(v):
    return 1.0 / (1.0 + jnp.exp(-v))


def softplus(v):
    return jnp.maximum(v, 0.0) + jnp.log1p(jnp.exp(-jnp.abs(v)))


class Meta:
    def __init__(self, ref, sizes):
        self.ref, self.sizes = ref, sizes
        self.me_s, self.me_c, self.me_t = ref[0], ref[1], ref[2]
        self.base = self.me_c * sizes["T"]
        self.half = lax.rem(self.me_t, 2)
        bounds, total = [], 0
        for i in range(sizes["seqs"]):
            total = total + ref[3 + i]
            bounds.append(total)
        self.bounds = bounds

    def place(self, i, sign):
        n_ctx, n_sh = self.sizes["ctx"], self.sizes["shards"] // self.sizes["ctx"]
        shard = lax.rem(self.me_s + i // n_ctx, n_sh)
        ctx = lax.rem(self.me_c + sign * (i % n_ctx) + n_ctx, n_ctx)
        return (shard * n_ctx + ctx) * (self.sizes["D"] // self.sizes["shards"])

    def shard_row(self, i):
        return self.place(i, -1)

    def block_row(self, i):
        return self.place(i, 1)

    def peer(self, k):
        return jnp.bitwise_xor(self.me_t, k)

    def segment(self, pos):
        total = 0
        for bound in self.bounds:
            total = total + jnp.where(pos >= bound, 1, 0)
        return jnp.where(pos < 0, -1, total)


def load_weights(meta, shards, scratch):
    rows = shards[0].shape[0]
    for i, shard in enumerate(shards):
        at = meta.shard_row(i) if len(shards) > 1 else 0
        if len(shards) > 1:
            at = pl.multiple_of(at, 16)
        scratch[pl.ds(at, rows), :] = shard[...]


class Step:
    chunk, inner, count = None, 0, 1


def when_first(body):
    if Step.inner == 0:
        pl.when(pl.program_id(0) == 0)(body)


def when_later(body):
    if Step.inner == 0:
        pl.when(pl.program_id(0) > 0)(body)
    else:
        body()


def when_last(body):
    if Step.inner == Step.count - 1:
        pl.when(pl.program_id(0) == pl.num_programs(0) - 1)(body)


def unrolled(kernel, ins, outs, count):
    axes, wide = [], []
    for item in (*ins, *outs):
        axis = None
        if item[0] != "smem":
            moved = [d for d, (a, b) in enumerate(zip(item[1](0), item[1](1))) if a != b]
            axis = moved[0] if moved else None
        if axis is not None:
            block = tuple(n * count if d == axis else n for d, n in enumerate(item[0]))
            item = (block,) + tuple(item[1:])
        axes.append(axis)
        wide.append(item)

    def body(*refs):
        for inner in range(count):
            views = []
            for k, ref in enumerate(refs):
                axis = axes[k] if k < len(axes) else None
                if axis is None:
                    views.append(ref)
                    continue
                size = wide[k][0][axis] // count
                at = tuple(
                    slice(inner * size, (inner + 1) * size) if d == axis else slice(None)
                    for d in range(len(wide[k][0]))
                )
                views.append(ref.at[at])
            Step.chunk, Step.inner, Step.count = pl.program_id(0) * count + inner, inner, count
            kernel(*views)

    return body, wide[: len(ins)], wide[len(ins) :]


def call(kernel, grid, ins, outs, scratch, flops, args, unroll=1):
    if unroll > 1 and grid % unroll == 0:
        kernel, ins, outs = unrolled(kernel, ins, outs, unroll)
        grid = grid // unroll
    else:
        inner_kernel = kernel

        def kernel(*refs):
            Step.chunk, Step.inner, Step.count = pl.program_id(0), 0, 1
            inner_kernel(*refs)


    def spec(item):
        block, index = item[0], item[1]
        if block == "smem":
            return pl.BlockSpec(memory_space=pltpu.SMEM)
        return pl.BlockSpec(block, index)

    out_shape = [jax.ShapeDtypeStruct(o[2], o[3]) for o in outs]
    nbytes = sum(a.size * a.dtype.itemsize for a in args) + sum(
        o.size * o.dtype.itemsize for o in out_shape
    )
    return pl.pallas_call(
        kernel,
        grid=(grid,),
        in_specs=[spec(i) for i in ins],
        out_specs=[spec(o) for o in outs],
        out_shape=out_shape,
        scratch_shapes=scratch,
        cost_estimate=pl.CostEstimate(flops=flops, bytes_accessed=nbytes, transcendentals=0),
        compiler_params=pltpu.CompilerParams(dimension_semantics=("arbitrary",)),
    )(*args)


def whole(a):
    return (tuple(a.shape), lambda i, n=len(a.shape): (0,) * n)


def rows(a, count=L):
    return ((count, a.shape[1]), lambda i: (i, 0))


def cols(a):
    return ((a.shape[0], L), lambda i: (0, i))


def o_rows(shape, dtype, count=L):
    return ((count, shape[1]), lambda i: (i, 0), shape, dtype)


def o_cols(shape, dtype):
    return ((shape[0], L), lambda i: (0, i), shape, dtype)


def o_whole(shape, dtype):
    return (tuple(shape), lambda i, n=len(shape): (0,) * n, shape, dtype)


SMEM = ("smem", None)


def tri_leq():
    return jnp.where(iota((L, L), 0) <= iota((L, L), 1), 1.0, 0.0)


def pair_mask(hw, which):
    lane = iota((L, 128), 1)
    return (lane >= which * hw) & (lane < (which + 1) * hw)


def allowed_mask(meta, c):
    start = meta.base + c * L
    pt, ps = start + iota((L, L), 0), start + iota((L, L), 1)
    return (meta.segment(pt) == meta.segment(ps)) & (pt >= ps)


def chunk_edges(meta, c):
    start = meta.base + c * L
    return meta.segment(start - 1), meta.segment(start + L - 1)


def pair_sum(left, right):
    def kernel(a, b, out):
        out[...] = (a[...].astype(f32) + b[...].astype(f32)).astype(bf16)

    vmem = pl.BlockSpec(memory_space=pltpu.VMEM)
    return pl.pallas_call(
        kernel, in_specs=[vmem, vmem], out_specs=vmem,
        out_shape=jax.ShapeDtypeStruct(left.shape, bf16),
        cost_estimate=pl.CostEstimate(flops=left.size, bytes_accessed=6 * left.size, transcendentals=0),
    )(left, right)


def to_shift(meta, c, width, distance):
    pos = meta.base + c * L + iota((L, 128), 0)
    same = meta.segment(pos) == meta.segment(pos - distance)
    return tiled(jnp.where(same & (pos - distance >= 0), 1.0, 0.0), width)


def tiled(mask, width):
    return jnp.concatenate([mask] * (width // 128), axis=1)


def flag(cond):
    return jnp.where(cond, 1.0, 0.0).astype(f32)


def build(sizes):
    T, D, IN, N, H, TAPS = (sizes[k] for k in ("T", "D", "IN", "N", "H", "TAPS"))
    n_tp, n_ctx, nC = sizes["tp"], sizes["ctx"], sizes["T"] // L
    HW = IN // H
    HPT = 128 // HW
    SL = 2 * N // n_tp
    PAIRS = IN // 128
    DIRECT = sizes["shards"] > 1
    NSH = sizes["shards"]
    PK = IN + 128 + 2 * N
    EXT = IN + 2 * N
    SP = 16
    HB = T // 2 // nC

    def expand_matrix():
        r, l = iota((128, IN), 0), iota((128, IN), 1)
        return jnp.where((r >= SL) & (r < SL + H) & (l // HW == r - SL), 1.0, 0.0)

    def head_select():
        r, l = iota((8, IN), 0), iota((8, IN), 1)
        return jnp.where((l // HW == r) & (r < H), 1.0, 0.0)

    def slab_select():
        r, l = iota((8, 128), 0), iota((8, 128), 1)
        return jnp.where((l == r + SL) & (r < H), 1.0, 0.0)

    def local_weights(cum, meta, c, last):
        return jnp.exp(cum[L - 1 : L, :] - cum) * in_segment(meta, c, last)

    def in_segment(meta, c, which):
        same = meta.segment(meta.base + c * L + iota((L, 128), 0)) == which
        return tiled(jnp.where(same, 1.0, 0.0), IN)

    def k_project(*refs):
        meta = Meta(refs[0], sizes)
        x_ref, xh_ref, cw_ref, hp_ref, hc_ref, mask_ref = refs[1:7]
        shards = refs[7 : 7 + NSH]
        (nb_ref, pr_ref, prh_ref, sm_ref, act_ref, dt_ref, cum_ref, dtr_ref, cumr_ref, hpre_ref,
         pp_ref, pack_ref) = refs[7 + NSH : 19 + NSH]
        gain_ref, w_ref, ext_ref, st_ref, ps_ref = refs[19 + NSH :]
        c = Step.chunk

        @when_first
        def _():
            load_weights(meta, shards, w_ref)
            xh = xh_ref[...]
            inv_h = lax.rsqrt(jnp.mean(xh * xh, axis=1, keepdims=True) + norm_eps)
            pick = jnp.where(iota((8, 128), 1) == SL + H, 1.0, 0.0).astype(bf16)
            gain_ref[...] = dot(pick, w_ref[:, IN : IN + 128], NT)
            nh = (xh * inv_h * gain_ref[...]).astype(bf16)
            ph = dot(nh, w_ref[...]).astype(bf16).astype(f32)
            prh_ref[...] = ph
            ext_ref[0:8, :IN] = ph[:, :IN]
            ext_ref[0:8, IN:] = ph[:, IN + 128 :]
            st_ref[...] = jnp.zeros((N, IN), f32)
            ps_ref[...] = jnp.ones((8, IN), f32)

        @when_later
        def _():
            ext_ref[0:8, :] = ext_ref[L : L + 8, :]

        x = x_ref[...]
        inv = lax.rsqrt(jnp.mean(x * x, axis=1, keepdims=True) + norm_eps)
        nb = (x * inv * gain_ref[0:1, :]).astype(bf16)
        nb_ref[...] = nb
        pr = dot(nb, w_ref[...]).astype(bf16)
        pr_ref[...] = pr
        prf = pr.astype(f32)
        ext_ref[8 : 8 + L, :IN] = prf[:, :IN]
        ext_ref[8 : 8 + L, IN:] = prf[:, IN + 128 :]
        summed = jnp.zeros((L, EXT), f32) + cw_ref[TAPS : TAPS + 1, :]
        for k in range(TAPS):
            d = TAPS - 1 - k
            term = cw_ref[k : k + 1, :] * ext_ref[8 - d : 8 - d + L, :]
            summed = summed + (term if d == 0 else term * to_shift(meta, c, EXT, d))
        sm_ref[...] = summed
        act = summed * sigmoid(summed)
        act_ref[...] = act
        slab = pr[:, IN : IN + 128]
        hp, hc = hp_ref[...], hc_ref[...]
        mask8 = mask_ref[...]
        mask_c = dot(mask8, jnp.where(iota((8, IN), 0) == 0, 1.0, 0.0), TN)
        dt = softplus(dot(slab, expand_matrix().astype(bf16)) + hp[0:1, :]) * mask_c
        dtr = softplus(dot(slab_select().astype(bf16), slab, NT) + hc[:, 0:1]) * mask8[0:1, :]
        tri = tri_leq()
        cum = dot(tri, dt * hp[1:2, :], TN, HI)
        cumr = dot(dtr * hc[:, 1:2], tri, NN, HI)
        dt_ref[...], cum_ref[...], dtr_ref[...], cumr_ref[...] = dt, cum, dtr, cumr
        prev, last = chunk_edges(meta, c)
        xd = dt * act[:, :IN]
        ws = local_weights(cum, meta, c, last)
        b = act[:, IN : IN + N]
        passing = jnp.exp(cum[L - 1 : L, :]) * flag(prev == last)
        at = pl.multiple_of(c * N, N)
        st, ps = st_ref[...], ps_ref[...]
        hpre_ref[pl.ds(at, N), :] = st
        pp_ref[pl.ds(pl.multiple_of(c * 8, 8), 8), :] = ps
        st = passing * st + dot3(b, ws * xd, TN)
        ps = ps * passing
        st_ref[...], ps_ref[...] = st, ps

        @when_last
        def _():
            hpre_ref[nC * N : (nC + 1) * N, :] = st
            pp_ref[nC * 8 : nC * 8 + 8, :] = ps
            pack_ref[:N, :] = st.astype(bf16)
            pack_ref[N:, :] = jnp.concatenate([ps, ps], axis=0).astype(bf16)

    def project(meta, x, xh, cw, hp, hc, mask8, shards):
        outs = [
            o_rows((T, D), bf16), o_rows((T, PK), bf16), o_whole((8, PK), f32),
            o_rows((T, EXT), f32), o_rows((T, EXT), f32), o_rows((T, IN), f32),
            o_rows((T, IN), f32), o_cols((8, T), f32), o_cols((8, T), f32),
            o_whole(((nC + 1) * N, IN), f32), o_whole(((nC + 1) * 8, IN), f32),
            o_whole((N + SP, IN), bf16), o_whole((8, D), f32),
        ]
        ins = [SMEM, rows(x), whole(xh), whole(cw), whole(hp), whole(hc), cols(mask8)]
        ins += [whole(s) for s in shards]
        scratch = [
            pltpu.VMEM((D, PK), bf16), pltpu.VMEM((L + 8, EXT), f32),
            pltpu.VMEM((N, IN), f32), pltpu.VMEM((8, IN), f32),
        ]
        return call(k_project, nC, ins, outs, scratch, 2 * T * D * PK,
                    [meta, x, xh, cw, hp, hc, mask8, *shards], unroll=2)

    def head_decay(meta_mask, cum, cumr, h):
        gap = cum[:, h * HW : h * HW + 1] - cumr[h : h + 1, :]
        return jnp.where(meta_mask, jnp.exp(gap), 0.0)

    def k_intra(mref, act_ref, dt_ref, cum_ref, cumr_ref, y_ref):
        meta = Meta(mref, sizes)
        c = Step.chunk
        ok = allowed_mask(meta, c)
        b = act_ref[:, IN : IN + N]
        cc = act_ref[:, IN + N :]
        scores = dot3(cc, b, NT)
        cum, cumr = cum_ref[...], cumr_ref[...]
        for p in range(PAIRS):
            sl = slice(p * 128, p * 128 + 128)
            xd = (dt_ref[:, sl] * act_ref[:, sl])
            y = None
            for j in range(HPT):
                g = (scores * head_decay(ok, cum, cumr, p * HPT + j))
                part = dot3(g, xd)
                y = part if y is None else jnp.where(pair_mask(HW, j), part, y)
            y_ref[:, sl] = y

    def intra(meta, act, dt, cum, cumr):
        return call(k_intra, nC, [SMEM, rows(act), rows(dt), rows(cum), cols(cumr)],
                    [o_rows((T, IN), f32)], [], 4 * T * L * IN, [meta, act, dt, cum, cumr], unroll=2)[0]

    def k_gate(*refs):
        meta = Meta(refs[0], sizes)
        nb_ref, do_ref = refs[1:3]
        shards = refs[3 : 3 + NSH]
        z_ref, dm_ref, w_ref = refs[3 + NSH :]

        @when_first
        def _():
            load_weights(meta, shards, w_ref)

        z_ref[...] = dot(nb_ref[...], w_ref[:, :IN]).astype(bf16)
        dm_ref[...] = dot(do_ref[...].astype(bf16), w_ref[:, IN:])

    def gate(meta, nb, d_out, shards):
        return call(k_gate, nC, [SMEM, rows(nb), rows(d_out)] + [whole(s) for s in shards],
                    [o_rows((T, IN), bf16), o_rows((T, IN), f32)],
                    [pltpu.VMEM((D, 2 * IN), bf16)], 4 * T * D * IN, [meta, nb, d_out, *shards], unroll=2)

    def chain(packs):
        total = None
        for pack in reversed(packs):
            state = pack[:N, :].astype(f32)
            total = state if total is None else state + pack[N : N + 1, :].astype(f32) * total
        return total

    def k_output(*refs):
        meta = Meta(refs[0], sizes)
        act_ref, cum_ref, y_ref, z_ref, dm_ref, hpre_ref, pp_ref, hp_ref, gg_ref = refs[1:10]
        packs = refs[10 : 10 + n_ctx - 1]
        yo_ref, stat_ref, ent_ref = refs[9 + n_ctx :]
        c = Step.chunk

        @when_first
        def _():
            ent_ref[...] = chain(packs)

        prev, _ = chunk_edges(meta, c)
        hin = (hpre_ref[...] + pp_ref[0:1, :] * ent_ref[...])
        cum = cum_ref[...]
        ent = jnp.exp(cum) * in_segment(meta, c, prev)
        y = y_ref[...] + ent * dot3(act_ref[:, IN + N :], hin)
        yo_ref[...] = y
        out = y + hp_ref[2:3, :] * act_ref[:, :IN]
        z = z_ref[...].astype(f32)
        gated = out * (z * sigmoid(z))
        ones = jnp.ones((8, IN), f32)
        sq = dot(ones, gated * gated, NT, HI)
        bd = dot(ones, dm_ref[...] * gg_ref[0:1, :] * gated, NT, HI)
        stat_ref[...] = jnp.where(iota((8, L), 0) == 0, sq, bd)

    def output(meta, act, cum, y, z, dm, hpre, pp, hp, gg, packs):
        ins = [SMEM, rows(act), rows(cum), rows(y), rows(z), rows(dm), rows(hpre, N), rows(pp, 8),
               whole(hp), whole(gg)] + [whole(p) for p in packs]
        outs = [o_rows((T, IN), f32), o_cols((8, T), f32), o_whole((N, IN), f32)]
        return call(k_output, nC, ins, outs, [], 4 * T * IN * N,
                    [meta, act, cum, y, z, dm, hpre, pp, hp, gg, *packs], unroll=2)

    def k_norm(*refs):
        meta = Meta(refs[0], sizes)
        act_ref, cum_ref, y_ref, z_ref, dm_ref, hp_ref, gg_ref = refs[1:8]
        stats = refs[8 : 8 + n_tp]
        mix_ref, dz_ref, dy_ref, suf_ref, psuf_ref, pack_ref, sums_ref = refs[8 + n_tp : 15 + n_tp]
        st_ref, ps_ref = refs[15 + n_tp :]
        c = nC - 1 - pl.program_id(0)

        @pl.when(pl.program_id(0) == 0)
        def _():
            st_ref[...] = jnp.zeros((N, IN), f32)
            ps_ref[...] = jnp.ones((8, IN), f32)
            sums_ref[...] = jnp.zeros((8, IN), f32)

        stat = stats[0][...]
        for s in stats[1:]:
            stat = stat + s[...]
        inner = float(IN * n_tp)
        inv_r = lax.rsqrt(stat[0:1, :] / inner + norm_eps)
        beta_r = inv_r * inv_r * inv_r * stat[1:2, :] / inner
        row = iota((8, L), 0)
        both = jnp.where(row == 0, inv_r, jnp.where(row == 1, beta_r, 0.0))
        inv = dot(both, jnp.where(iota((8, IN), 0) == 0, 1.0, 0.0), TN, HI)
        beta = dot(both, jnp.where(iota((8, IN), 0) == 1, 1.0, 0.0), TN, HI)
        gg, skip = gg_ref[0:1, :], hp_ref[2:3, :]
        x = act_ref[:, :IN]
        out = y_ref[...] + skip * x
        z = z_ref[...].astype(f32)
        sig = sigmoid(z)
        ga = z * sig
        gated = out * ga
        dm = dm_ref[...]
        normal = gated * inv
        mix_ref[...] = (normal * gg).astype(bf16)
        dg = dm * gg * inv - gated * beta
        dz_ref[...] = (dg * out * sig * (1.0 + z * (1.0 - sig))).astype(bf16)
        dy = dg * ga
        dyb = dy
        dy_ref[...] = dyb
        s0 = jnp.sum(dm * normal, axis=0, keepdims=True)
        s1 = jnp.sum(dy * x, axis=0, keepdims=True)
        r8 = iota((8, IN), 0)
        sums_ref[...] += jnp.where(r8 == 0, s0, jnp.where(r8 == 1, s1, 0.0))
        prev, last = chunk_edges(meta, c)
        cum = cum_ref[...]
        ent = jnp.exp(cum) * in_segment(meta, c, prev)
        passing = jnp.exp(cum[L - 1 : L, :]) * flag(prev == last)
        st, ps = st_ref[...], ps_ref[...]
        suf_ref[...] = st
        psuf_ref[...] = ps
        cc = act_ref[:, IN + N :]
        st = passing * st + dot3(cc, ent * dyb.astype(f32), TN)
        ps = passing * ps
        st_ref[...], ps_ref[...] = st, ps

        @pl.when(c == 0)
        def _():
            pack_ref[:N, :] = st.astype(bf16)
            pack_ref[N:, :] = jnp.concatenate([ps, ps], axis=0).astype(bf16)

    def norm(meta, act, cum, y, z, dm, hp, gg, stats):
        def back(item):
            block, index = item[0], item[1]
            return (block, lambda i: index(nC - 1 - i)) + tuple(item[2:])

        ins = [SMEM] + [back(rows(a)) for a in (act, cum, y, z, dm)] + [whole(hp), whole(gg)]
        ins += [back(cols(s)) for s in stats]
        outs = [back(o_rows((T, IN), bf16)), back(o_rows((T, IN), bf16)), back(o_rows((T, IN), f32)),
                back(o_rows((nC * N, IN), f32, N)), back(o_rows((nC * 8, IN), f32, 8)),
                o_whole((N + SP, IN), bf16), o_whole((8, IN), f32)]
        scratch = [pltpu.VMEM((N, IN), f32), pltpu.VMEM((8, IN), f32)]
        return call(k_norm, nC, ins, outs, scratch, 2 * T * IN * N,
                    [meta, act, cum, y, z, dm, hp, gg, *stats])

    def k_intra_back(mref, act_ref, dt_ref, cum_ref, cumr_ref, dy_ref, dxd_ref, dbc_ref):
        meta = Meta(mref, sizes)
        c = Step.chunk
        ok = allowed_mask(meta, c)
        b = act_ref[:, IN : IN + N]
        cc = act_ref[:, IN + N :]
        scores = dot3(cc, b, NT)
        cum, cumr = cum_ref[...], cumr_ref[...]
        d_scores = jnp.zeros((L, L), f32)
        for p in range(PAIRS):
            sl = slice(p * 128, p * 128 + 128)
            xd = (dt_ref[:, sl] * act_ref[:, sl])
            dy = dy_ref[:, sl]
            dxd = None
            for j in range(HPT):
                decay = head_decay(ok, cum, cumr, p * HPT + j)
                g = (scores * decay)
                part = dot3(g, dy, TN)
                dxd = part if dxd is None else jnp.where(pair_mask(HW, j), part, dxd)
                own = jnp.where(pair_mask(HW, j), dy.astype(f32), 0.0)
                d_scores = d_scores + dot3(own, xd, NT) * decay
            dxd_ref[:, sl] = dxd
        ds = d_scores
        dbc_ref[:, :N] = dot3(ds, cc, TN)
        dbc_ref[:, N:] = dot3(ds, b)

    def intra_back(meta, act, dt, cum, cumr, dy):
        return call(k_intra_back, nC,
                    [SMEM, rows(act), rows(dt), rows(cum), cols(cumr), rows(dy)],
                    [o_rows((T, IN), f32), o_rows((T, 2 * N), f32)], [], 8 * T * L * IN,
                    [meta, act, dt, cum, cumr, dy], unroll=2)

    def write_blocks(meta, total, outs):
        if not DIRECT:
            outs[0][...] = total[...].astype(bf16)
            return
        br = D // NSH
        for i in range(NSH):
            at = pl.multiple_of(meta.block_row(i), 8)
            outs[i % n_ctx][(i // n_ctx) * br : (i // n_ctx + 1) * br, :] = total[
                pl.ds(at, br), :
            ].astype(bf16)

    n_groups = n_ctx if DIRECT else 1
    group_rows = D // n_ctx if DIRECT else D

    def split_rows(meta, c, value, keep, send):
        at = pl.multiple_of(lax.rem(c, nC // 2) * L, L)

        @pl.when(c // (nC // 2) == meta.half)
        def _():
            keep[pl.ds(at, L), :] = value

        @pl.when(c // (nC // 2) != meta.half)
        def _():
            send[pl.ds(at, L), :] = value.astype(bf16)

    def k_outer(*refs):
        meta = Meta(refs[0], sizes)
        nb_ref, do_ref, mix_ref, dz_ref = refs[1:5]
        shards = refs[5 : 5 + NSH]
        outs = refs[5 + NSH : 5 + NSH + n_groups]
        keep_ref, send_ref = refs[5 + NSH + n_groups : 7 + NSH + n_groups]
        w_ref, total = refs[7 + NSH + n_groups :]
        c = pl.program_id(0)

        @pl.when(c == 0)
        def _():
            load_weights(meta, shards, w_ref)
            total[...] = jnp.zeros((D, 2 * IN), f32)

        total[:, :IN] += dot(nb_ref[...], dz_ref[...], TN)
        total[:, IN:] += dot(do_ref[...].astype(bf16), mix_ref[...], TN)
        split_rows(meta, c, dot(mix_ref[...], w_ref[:, IN:], NT), keep_ref, send_ref)

        @pl.when(c == nC - 1)
        def _():
            write_blocks(meta, total, outs)

    def outer(meta, nb, d_out, mix, dz, shards):
        outs = [o_whole((group_rows, 2 * IN), bf16)] * n_groups
        outs += [o_whole((T // 2, D), f32), o_whole((T // 2, D), bf16)]
        ins = [SMEM, rows(nb), rows(d_out), rows(mix), rows(dz)] + [whole(s) for s in shards]
        scratch = [pltpu.VMEM((D, 2 * IN), bf16), pltpu.VMEM((D, 2 * IN), f32)]
        got = call(k_outer, nC, ins, outs, scratch, 6 * T * D * IN,
                   [meta, nb, d_out, mix, dz, *shards])
        return got[:n_groups], got[n_groups], got[n_groups + 1]

    def k_scan_back(*refs):
        meta = Meta(refs[0], sizes)
        (act_ref, sm_ref, pr_ref, dt_ref, cum_ref, dtr_ref, y_ref, dy_ref, dxd_ref, dbc_ref, hpre_ref,
         hnext_ref, pp_ref, pnext_ref, ent_ref, suf_ref, psuf_ref, hp_ref, hc_ref, mask_ref, bk_ref,
         bg_ref) = refs[1:23]
        packs, at = refs[23 : 22 + n_ctx], 22 + n_ctx
        dsx_ref, ddt_ref, sums_ref, edge_ref, pair_ref = refs[at : at + 5]
        slices = refs[at + 5 : at + 5 + n_tp]
        edges = refs[at + 5 + n_tp : at + 4 + 2 * n_tp]
        exit_ref = refs[at + 4 + 2 * n_tp]
        c = pl.program_id(0)
        pair_ref[...] = (bk_ref[...] + bg_ref[...].astype(f32)).astype(bf16)

        @pl.when(c == 0)
        def _():
            exit_ref[...] = chain(packs)
            sums_ref[...] = jnp.zeros((16, 128), f32)

        prev, last = chunk_edges(meta, c)
        hin = hpre_ref[...] + pp_ref[0:1, :] * ent_ref[...]
        hout = hnext_ref[...] + pnext_ref[0:1, :] * ent_ref[...]
        dh = suf_ref[...] + psuf_ref[0:1, :] * exit_ref[...]
        hinb, dhb = hin, dh
        cum, dt, x = cum_ref[...], dt_ref[...], act_ref[:, :IN]
        b = act_ref[:, IN : IN + N]
        ws = local_weights(cum, meta, c, last)
        ent = jnp.exp(cum) * in_segment(meta, c, prev)
        xd = dt * x
        dyf = dy_ref[...].astype(f32)
        leaving = dot3(b, dhb)
        wx = ws * xd
        dxd_in = dxd_ref[...]
        dxd = dxd_in + ws * leaving
        db = dbc_ref[:, :N] + dot3(wx, dhb, NT)
        dc = dbc_ref[:, N:] + dot3(ent * dyf, hinb, NT)
        hs = head_select()
        dcum = dot(hs, dyf * y_ref[...] - xd * dxd_in - wx.astype(f32) * leaving, NT, HI)
        final = dot(hs, jnp.zeros((8, IN), f32) + jnp.sum(dhb.astype(f32) * hout, axis=0, keepdims=True), NT, HI)
        da = dot(dcum, tri_leq(), NT, HI) + final[:, 0:1]
        hc = hc_ref[...]
        dtr, mask8 = dtr_ref[...], mask_ref[...]
        ddt = da * hc[:, 1:2] + dot(hs, dxd * x, NT, HI)
        slab = pr_ref[:, IN : IN + 128]
        pre_r = dot(slab_select().astype(bf16), slab, NT) + hc[:, 0:1]
        dpre = ddt * mask8[0:1, :] * sigmoid(pre_r)
        ddt_ref[...] = dot(dpre.astype(bf16), slab_select().astype(bf16), TN).astype(bf16)
        ones = jnp.ones((L, 128), f32)
        sums_ref[0:8, :] += dot(dpre, ones, NN, HI)
        sums_ref[8:16, :] += dot(da * dtr, ones, NN, HI)
        sm = sm_ref[...]
        sig = sigmoid(sm)
        dsilu = sig * (1.0 + sm * (1.0 - sig))
        dsx = (hp_ref[2:3, :] * dyf + dt * dxd) * dsilu[:, :IN]
        dsx_ref[...] = dsx
        dsb = (jnp.concatenate([db, dc], axis=1) * dsilu[:, IN:]).astype(bf16)
        quarter = c // (nC // 2)
        at = pl.multiple_of(lax.rem(c, nC // 2) * L, L)
        r, l = iota((2 * N, 128), 0), iota((2 * N, 128), 1)
        for k in range(n_tp):
            left = meta.peer(k) * SL
            lane0 = quarter * SL
            pick = jnp.where((r - left == l - lane0) & (l >= lane0) & (l < lane0 + SL), 1.0, 0.0)
            part = dot(dsb, pick.astype(bf16)).astype(bf16)

            @pl.when(quarter == 0)
            def _():
                slices[k][pl.ds(at, L), :] = part

            @pl.when(quarter != 0)
            def _():
                slices[k][pl.ds(at, L), :] = slices[k][pl.ds(at, L), :] + part

            @pl.when(c == 0)
            def _():
                if k == 0:
                    edge_ref[:, :IN] = dsx[0:8, :]
                    edge_ref[:, IN:] = part[0:8, :].astype(f32)
                else:
                    edges[k - 1][...] = part[0:8, :].astype(f32)

    def scan_back(meta, act, sm, pr, dt, cum, dtr, y, dy, dxd, dbc, hpre, pp, ent, suf, psuf, hp, hc,
                  mask8, b_keep, b_got, packs):
        def later(item):
            return (item[0], lambda i: item[1](i + 1))

        ins = [SMEM, rows(act), rows(sm), rows(pr), rows(dt), rows(cum), cols(dtr), rows(y), rows(dy),
               rows(dxd), rows(dbc), rows(hpre, N), later(rows(hpre, N)), rows(pp, 8),
               later(rows(pp, 8)), whole(ent), rows(suf, N), rows(psuf, 8), whole(hp), whole(hc),
               cols(mask8), rows(b_keep, HB), rows(b_got, HB)] + [whole(p) for p in packs]
        outs = [o_rows((T, IN), f32), o_rows((T, 128), bf16), o_whole((16, 128), f32),
                o_whole((8, IN + 128), f32), o_rows((T // 2, D), bf16, HB)]
        outs += [o_whole((T // 2, 128), bf16)] * n_tp + [o_whole((8, 128), f32)] * (n_tp - 1)
        got = call(k_scan_back, nC, ins, outs, [pltpu.VMEM((N, IN), f32)],
                   6 * T * IN * N,
                   [meta, act, sm, pr, dt, cum, dtr, y, dy, dxd, dbc, hpre, hpre, pp, pp, ent, suf,
                    psuf, hp, hc, mask8, b_keep, b_got, *packs])
        return got[:5], got[5 : 5 + n_tp], got[5 + n_tp :]

    PW = IN + 128
    br9 = D // NSH

    def k_conv_back(*refs):
        meta = Meta(refs[0], sizes)
        nb_ref, pr_ref, prp_ref, prh_ref, dz_ref, ddt_ref, dsx_ref, dsn_ref = refs[1:9]
        cw_ref, sums_ref, ssum_ref, edge_ref = refs[9:13]
        at = 13
        slices, at = refs[at : at + n_tp], at + n_tp
        edges, at = refs[at : at + n_tp - 1], at + n_tp - 1
        shards, at = refs[at : at + NSH], at + NSH
        zshards, at = refs[at : at + NSH], at + NSH
        halves, at = refs[at : at + n_tp // 2], at + n_tp // 2
        gs, at = refs[at : at + NSH], at + NSH
        keep_ref, send_ref, half_ref = refs[at : at + 3]
        at += 3
        w_ref, wz_ref, ex_ref, px_ref, sl_ref, total, tap_ref = refs[at:]
        c = pl.program_id(0)
        half = halves[0][...].astype(f32)
        for h in halves[1:]:
            half = half + h[...].astype(f32)
        half_ref[...] = half.astype(bf16)

        @pl.when(c == 0)
        def _():
            load_weights(meta, shards, w_ref)
            load_weights(meta, zshards, wz_ref)
            total[...] = jnp.zeros((D, PW), f32)
            tap_ref[...] = jnp.zeros((8, PW), f32)
            sl = slices[0][...].astype(f32)
            for s in slices[1:]:
                sl = sl + s[...].astype(f32)
            low = iota((T // 2, 128), 1) < SL
            sl_ref[0 : T // 2, :] = jnp.where(low, sl, 0.0)
            sl_ref[T // 2 : T, :] = jnp.where(low, pltpu.roll(sl, 128 - SL, 1), 0.0)
            e = edge_ref[:, IN:]
            for s in edges:
                e = e + s[...]
            sl_ref[T : T + 8, :] = jnp.where(iota((8, 128), 1) < SL, e, 0.0)

        here = pl.multiple_of(c * L, L)
        after = pl.multiple_of(c * L + L, L)
        ex_ref[0:L, :IN] = dsx_ref[...]
        ex_ref[0:L, IN:] = sl_ref[pl.ds(here, L), :]
        ex_ref[L : L + 8, IN:] = sl_ref[pl.ds(after, 8), :]
        ex_ref[L : L + 8, :IN] = jnp.where(c == nC - 1, edge_ref[:, :IN], dsn_ref[...])
        low = iota((L, PW), 1) < IN + SL
        px_ref[8 : 8 + L, :] = pr_ref[:, :PW].astype(f32)
        px_ref[0:8, :] = jnp.where(c == 0, prh_ref[:, :PW], prp_ref[8:16, :PW].astype(f32))
        cw = cw_ref[...]
        ds = ex_ref[0:L, :]
        dpre = jnp.zeros((L, PW), f32)
        pos = meta.base + c * L + iota((L, 128), 0)
        seg = meta.segment(pos)
        group = T * n_ctx
        r8 = iota((8, PW), 0)
        taps = jnp.where(r8 == TAPS, jnp.sum(ds, axis=0, keepdims=True), 0.0)
        for k in range(TAPS):
            d = TAPS - 1 - k
            reach = cw[k : k + 1, :] * ex_ref[d : d + L, :]
            prior = ds * px_ref[8 - d : 8 - d + L, :]
            if d > 0:
                ahead = jnp.where((seg == meta.segment(pos + d)) & (pos + d < group), 1.0, 0.0)
                reach = reach * tiled(ahead, PW)
                prior = prior * to_shift(meta, c, PW, d)
            dpre = dpre + reach
            taps = taps + jnp.where(r8 == k, jnp.sum(prior, axis=0, keepdims=True), 0.0)
        tap_ref[...] += taps
        dpre = jnp.where(low, dpre, 0.0)
        dproj = dpre.astype(bf16)
        dslab = (dpre[:, IN:] + ddt_ref[...].astype(f32)).astype(bf16)
        dproj = jnp.concatenate([dproj[:, :IN], dslab], axis=1)
        nb = nb_ref[...]
        total[...] += dot(nb, dproj, TN)
        q = dot(dproj, w_ref[:, :PW], NT) + dot(dz_ref[...], wz_ref[:, :IN], NT)
        split_rows(meta, c, q, keep_ref, send_ref)

        @pl.when(c == nC - 1)
        def _():
            low8 = iota((8, PW), 1) < IN + SL
            s = ssum_ref[...]
            zero = jnp.zeros((8, 128), f32)
            pad = jnp.concatenate([s, jnp.zeros((8, PW - IN), f32)], axis=1)
            first = jnp.where(low8, tap_ref[...], 0.0)
            first = jnp.where(r8 == 5, pad[0:1, :], jnp.where(r8 == 6, pad[1:2, :], first))
            lead = first.astype(bf16).astype(f32)
            first = jnp.where(r8 == 7, (first - lead)[TAPS : TAPS + 1, :], first)
            pair = [sums_ref[0:8, :], sums_ref[8:16, :]]
            rest = [p - p.astype(bf16).astype(f32) for p in pair]
            tail = pair + rest + [zero] * (PW // 128 - 4)
            small = jnp.concatenate([first, jnp.concatenate(tail, axis=1)], axis=0).astype(bf16)
            if not DIRECT:
                gs[0][:D, :] = total[...].astype(bf16)
                gs[0][D:, :] = small
            else:
                for i in range(NSH):
                    at = pl.multiple_of(meta.block_row(i), 8)
                    gs[i][:br9, :] = total[pl.ds(at, br9), :].astype(bf16)
                    gs[i][br9:, :] = small

    def conv_back(meta, nb, pr, prh, dz, ddt, dsx, cw9, sums, ssum, edge, slices, edges, shards,
                  zshards, halves):
        step = L // 16
        prior = ((16, PK), lambda i: (jnp.maximum(i * step - 1, 0), 0))
        after = ((8, IN), lambda i: (jnp.minimum((i + 1) * (L // 8), T // 8 - 1), 0))
        ins = [SMEM, rows(nb), rows(pr), prior, whole(prh), rows(dz), rows(ddt), rows(dsx), after,
               whole(cw9), whole(sums), whole(ssum), whole(edge)]
        ins += [whole(a) for a in (*slices, *edges, *shards, *zshards)]
        ins += [rows(h, HB) for h in halves]
        outs = [o_whole((br9 + 16, PW), bf16)] * NSH
        outs += [o_whole((T // 2, D), f32), o_whole((T // 2, D), bf16), o_rows((T // 2, D), bf16, HB)]
        scratch = [pltpu.VMEM((D, PK), bf16), pltpu.VMEM((D, 2 * IN), bf16),
                   pltpu.VMEM((L + 8, PW), f32), pltpu.VMEM((L + 8, PW), f32),
                   pltpu.VMEM((T + 8, 128), f32), pltpu.VMEM((D, PW), f32),
                   pltpu.VMEM((8, PW), f32)]
        got = call(k_conv_back, nC, ins, outs, scratch, 4 * T * D * (PW + IN),
                    [meta, nb, pr, pr, prh, dz, ddt, dsx, dsx, cw9, sums, ssum, edge, *slices, *edges,
                     *shards, *zshards, *halves])
        return got[:NSH], got[NSH:]

    def k_tables(mref, wx, bx, wbc, bbc, bias, alog, skip, gain, mask, cw, cw9, hp, hc, gg, mask8):
        meta = Meta(mref, sizes)
        zeros = lambda n, w: jnp.zeros((n, w), f32)
        left = jnp.concatenate([wx[...], bx[...], zeros(7 - TAPS, IN)], axis=0)
        right = jnp.concatenate([wbc[...], bbc[...], zeros(7 - TAPS, 2 * N)], axis=0)
        cw[...] = jnp.concatenate([left, right], axis=1)
        r, l = iota((2 * N, 128), 0), iota((2 * N, 128), 1)
        pick = jnp.where((r == l + meta.me_t * SL) & (l < SL), 1.0, 0.0)
        cw9[...] = jnp.concatenate([left, dot(right, pick, NN, HI)], axis=1)
        rate = -jnp.exp(alog[...])
        row = iota((8, H), 0)
        rows8 = jnp.where(row == 0, bias[...], jnp.where(row == 1, rate, jnp.where(row == 2, skip[...], 0.0)))
        spread = jnp.where(iota((H, IN), 1) // HW == iota((H, IN), 0), 1.0, 0.0)
        hp[...] = dot(rows8, spread, NN, HI)
        eye = jnp.where(iota((8, 128), 0) == iota((8, 128), 1), 1.0, 0.0)
        turn = jnp.where(iota((8, H), 0) == iota((8, H), 1), 1.0, 0.0)
        hc[...] = dot(dot(turn, rows8, NT, HI), eye, NN, HI)
        gg[...] = jnp.zeros((8, IN), f32) + gain[...]
        mask8[...] = jnp.zeros((8, T), f32) + mask[...].astype(f32)

    def tables(*args):
        outs = [o_whole((8, EXT), f32), o_whole((8, PW), f32), o_whole((8, IN), f32),
                o_whole((8, 128), f32), o_whole((8, IN), f32), o_whole((8, T), f32)]
        return call(k_tables, 1, [SMEM] + [whole(a) for a in args[1:]], outs, [], 0, args)

    def k_finish(*refs):
        meta = Meta(refs[0], sizes)
        first_ref, second_ref = refs[1:3]
        blocks, parts = refs[3 : 3 + n_ctx], refs[3 + n_ctx : 5 + n_ctx]
        alog = refs[5 + n_ctx]
        gz, go, gx, slab_ref, wx, bx, gain_row, h_dt, h_log, h_skip, last, order = refs[6 + n_ctx :]
        zo = parts[0][...]
        for p in parts[1:]:
            zo = zo + p[...].astype(f32)
        gz[...], go[...] = zo[:, :IN], zo[:, IN:]
        total = None
        for r in range(n_ctx):
            b = blocks[r][...].astype(f32)
            total = b[:br9] if total is None else total + b[:br9]
            order[lax.rem(meta.me_c - r + n_ctx, n_ctx)] = b[br9:]
        small = order[0]
        for r in range(1, n_ctx):
            small = small + order[r]
        gx[...] = total[:, :IN]
        slab = total[:, IN:]
        slab_ref[...] = slab
        lane = iota((br9, 128), 1)
        w_slab = first_ref[:, IN : IN + 128].astype(f32)
        gain = jnp.sum(jnp.where(lane == SL + H, w_slab, 0.0), axis=1, keepdims=True)
        d_gain = jnp.sum(first_ref[:, :IN].astype(f32) * total[:, :IN], axis=1, keepdims=True)
        d_gain = d_gain + jnp.sum(second_ref[:, :IN].astype(f32) * zo[:, :IN], axis=1, keepdims=True)
        d_gain = d_gain + jnp.sum(jnp.where(lane < SL + H, w_slab * slab, 0.0), axis=1, keepdims=True)
        last[:br9, :] = jnp.where(lane < SL, slab, jnp.where(lane == SL, d_gain / gain, 0.0))
        top = small[0:8]
        bias = top[TAPS : TAPS + 1] + top[7:8]
        wx[...] = top[:TAPS, :IN]
        bx[...] = bias[:, :IN].reshape(IN)
        gain_row[...] = top[5:6, :IN].reshape(IN)
        taps = jnp.where(iota((8, PW), 0) == TAPS, bias, top)
        last[br9:, :] = jnp.where(iota((8, 128), 1) < SL, taps[:, IN:], 0.0)
        pair = small[8:16, 0:256] + small[8:16, 256:512]
        skip = dot(head_select(), jnp.zeros((8, IN), f32) + top[6:7, :IN], NT, HI)
        eye8 = iota((8, 128), 0) == iota((8, 128), 1)

        def flat(col):
            return jnp.sum(jnp.where(eye8, col, 0.0), axis=0, keepdims=True)[:, :H]

        h_dt[...] = flat(pair[:, 0:1]).reshape(H)
        h_log[...] = (flat(pair[:, 128:129]) * -jnp.exp(alog[...])).reshape(H)
        h_skip[...] = flat(skip[:, 0:1]).reshape(H)

    def finish(meta, first, second, blocks, parts, a_log):
        args = [meta, first, second, *blocks, *parts, a_log]
        outs = [o_whole((br9, IN), f32)] * 3 + [o_whole((br9, 128), f32), o_whole((TAPS, IN), f32),
                o_whole((IN,), f32), o_whole((IN,), f32), o_whole((H,), f32), o_whole((H,), f32),
                o_whole((H,), f32), o_whole((br9 + 8, 128), f32)]
        return call(k_finish, 1, [SMEM] + [whole(a) for a in args[1:]], outs,
                    [pltpu.VMEM((n_ctx, 16, PW), f32)], 0, args)

    def k_spread(mref, *refs):
        meta = Meta(mref, sizes)
        parts = refs[:n_tp]
        wbc, gain, taps, bias, last = refs[n_tp:]
        for k in range(n_tp):
            last[meta.peer(k)] = parts[k][...]
        per = 128 // SL
        lane = iota((br9 + 8, 128), 1)
        for t in range(n_tp // per):
            tile = last[t * per]
            for j in range(1, per):
                tile = jnp.where(lane >= j * SL, pltpu.roll(last[t * per + j], j * SL, 1), tile)
            sl = slice(t * 128, t * 128 + 128)
            wbc[:, sl] = tile[:br9]
            taps[:, sl] = tile[br9 : br9 + TAPS]
            bias[sl] = tile[br9 + TAPS : br9 + TAPS + 1].reshape(128)
        total = last[0][:br9]
        for k in range(1, n_tp):
            total = total + last[k][:br9]
        col = jnp.sum(jnp.where(iota((br9, 128), 1) == SL, total, 0.0), axis=1, keepdims=True)
        eye = iota((br9, br9), 0) == iota((br9, br9), 1)
        gain[...] = jnp.sum(jnp.where(eye, col, 0.0), axis=0, keepdims=True).reshape(br9)

    def spread(meta, parts):
        outs = [o_whole((br9, 2 * N), f32), o_whole((br9,), f32), o_whole((TAPS, 2 * N), f32),
                o_whole((2 * N,), f32)]
        return call(k_spread, 1, [SMEM] + [whole(p) for p in parts], outs,
                    [pltpu.VMEM((n_tp, br9 + 8, 128), f32)], 0, [meta, *parts])

    return dict(tables=tables, finish=finish, spread=spread, project=project, intra=intra, gate=gate, output=output, norm=norm,
                intra_back=intra_back, outer=outer, scan_back=scan_back, conv_back=conv_back,
                SL=SL, PW=PW)


def block(x_in, norm_gain, w_z, w_x, w_bc, w_dt, w_out, conv_wx, conv_bx, conv_wbc, conv_bbc, dt_bias,
          a_log, d_skip, gate_gain, seq_lens, token_mask, d_out):
    T, D = x_in.shape
    H, IN, N, TAPS = dt_bias.shape[0], w_z.shape[1], w_bc.shape[1] // 2, conv_wx.shape[0]
    n_sh, n_ctx, n_tp = (lax.axis_size(a) for a in ("shard", "ctx", "tp"))
    me_s, me_c, me_t = (lax.axis_index(a) for a in ("shard", "ctx", "tp"))
    direct = n_sh == 2 and n_ctx == 4
    NSH = n_sh * n_ctx if direct else 1
    seqs = seq_lens.shape[1]
    sizes = dict(T=T, D=D, IN=IN, N=N, H=H, TAPS=TAPS, tp=n_tp, ctx=n_ctx, seqs=seqs, shards=NSH)
    ops = build(sizes)
    SL = ops["SL"]
    HW = IN // H
    br = w_z.shape[0]

    def ring(count, step):
        return [(i, (i + step) % count) for i in range(count)]

    def xor(count, step):
        return [(i, i ^ step) for i in range(count)]

    def gather(part):
        if not direct:
            return [lax.all_gather(part, ("shard", "ctx"), axis=0, tiled=True)]
        here = [part]
        for k in range(1, n_ctx):
            here.append(lax.ppermute(part, "ctx", ring(n_ctx, k)))
        there = []
        for p in here:
            there.append(lax.ppermute(p, "shard", ring(n_sh, 1)))
        return here + there

    meta = jnp.concatenate([jnp.stack([me_s, me_c, me_t]).astype(jnp.int32), seq_lens[0]])

    w_slice = lax.dynamic_slice_in_dim(w_bc, me_t * SL, SL, 1)
    first = jnp.concatenate(
        [w_x, w_slice, w_dt, norm_gain[:, None], jnp.zeros((br, 127 - SL - H), bf16), w_bc], axis=1
    )
    x_tail = lax.ppermute(x_in[T - 8 :], "ctx", [(i, i + 1) for i in range(n_ctx - 1)])
    shards = gather(first)
    second = jnp.concatenate([w_z, w_out], axis=1)
    shards2 = gather(second)

    cw, cw9, hp, hc, gg, mask8 = ops["tables"](
        meta, conv_wx, conv_bx[None, :], conv_wbc, conv_bbc[None, :], dt_bias[None, :],
        a_log[None, :], d_skip[None, :], gate_gain[None, :], token_mask[None, :])

    (nb, pr, prh, sm, act, dt, cum, dtr, cumr, hpre, pp, pack, gain_row) = ops["project"](
        meta, x_in, x_tail, cw, hp, hc, mask8, shards)
    packs = [lax.ppermute(pack, "ctx", [(i, i + k) for i in range(n_ctx - k)]) for k in range(1, n_ctx)]
    y_in = ops["intra"](meta, act, dt, cum, cumr)
    z, dm = ops["gate"](meta, nb, d_out, shards2)
    y, stat, entry = ops["output"](meta, act, cum, y_in, z, dm, hpre, pp, hp, gg, packs)
    stats = [stat] + [lax.ppermute(stat, "tp", xor(n_tp, k)) for k in range(1, n_tp)]
    mix, dz, dy, suf, psuf, bpack, ssum = ops["norm"](meta, act, cum, y, z, dm, hp, gg, stats)
    bpacks = []
    for k in range(1, n_ctx):
        bpacks.append(lax.ppermute(bpack, "ctx", [(i + k, i) for i in range(n_ctx - k)]))
    dxd, dbc = ops["intra_back"](meta, act, dt, cum, cumr, dy)
    groups, b_keep, b_send = ops["outer"](meta, nb, d_out, mix, dz, shards2)

    def both_halves(part):
        mine = part.astype(bf16)
        other = lax.ppermute(mine, "tp", xor(n_tp, 1))
        flip = me_t % 2 == 1
        low, high = jnp.where(flip, other, mine), jnp.where(flip, mine, other)
        return jnp.concatenate([low, high], axis=0).astype(f32)

    b_got = lax.ppermute(b_send, "tp", xor(n_tp, 1))
    (dsx, ddt, sums, edge, b_pair), slices, edges = ops["scan_back"](
        meta, act, sm, pr, dt, cum, dtr, y, dy, dxd, dbc, hpre, pp, entry, suf, psuf, hp, hc, mask8,
        b_keep, b_got, bpacks)
    got_edge = lax.ppermute(edge, "ctx", [(i + 1, i) for i in range(n_ctx - 1)])
    got_slices = [slices[0]] + [lax.ppermute(slices[k], "tp", xor(n_tp, k)) for k in range(1, n_tp)]
    got_edges = [
        lax.ppermute(edges[k - 1], ("ctx", "tp"),
                     [((i + 1) * n_tp + j, i * n_tp + (j ^ k)) for i in range(n_ctx - 1) for j in range(n_tp)])
        for k in range(1, n_tp)
    ]
    halves = [b_pair] + [lax.ppermute(b_pair, "tp", xor(n_tp, k)) for k in range(2, n_tp, 2)]
    if direct:
        total = groups[0].astype(f32)
        for r in range(1, n_ctx):
            got = lax.ppermute(groups[r], "ctx", ring(n_ctx, r))
            total = total + got.astype(f32)
        other = lax.ppermute(total[br:].astype(bf16), "shard", ring(n_sh, 1))
        parts = [total[:br], other]
    grads, (q_keep, q_send, b_half) = ops["conv_back"](
        meta, nb, pr, prh, dz, ddt, dsx, cw9, sums, ssum, got_edge, got_slices, got_edges, shards,
        shards2, halves)
    if direct:
        moved = []
        for r in [*range(1, n_ctx), 0]:
            got = lax.ppermute(grads[n_ctx + r], "shard", ring(n_sh, 1))
            moved.append(pair_sum(grads[r], got))
        blocks = [moved[-1]]
        for r in range(1, n_ctx):
            blocks.append(lax.ppermute(moved[r - 1], "ctx", ring(n_ctx, r)))

    q_got = lax.ppermute(q_send, "tp", xor(n_tp, 1))
    q_pair = pair_sum(q_keep, q_got)
    q_half = q_pair.astype(f32)
    for k in range(2, n_tp, 2):
        q_half = q_half + lax.ppermute(q_pair, "tp", xor(n_tp, k)).astype(f32)
    block_out = x_in + both_halves(b_half)

    x_half = lax.dynamic_slice_in_dim(x_in, (me_t % 2) * (T // 2), T // 2, 0)
    inv = lax.rsqrt(jnp.mean(x_half * x_half, axis=1, keepdims=True) + norm_eps)
    q_half = q_half * gain_row[0:1, :]
    row_dot = jnp.sum(q_half * x_half, axis=1, keepdims=True)
    d_input = d_out + both_halves(q_half * inv - x_half * (inv * inv * inv) * row_dot / D)

    if direct:
        g_z, g_out, g_x, g_slab, d_cx, d_bx, d_gg, d_dt_bias, d_a_log, d_skips, last = ops["finish"](
            meta, first, second, blocks, parts, a_log[None, :])
        lasts = [last] + [lax.ppermute(last, "tp", xor(n_tp, k)) for k in range(1, n_tp)]
        d_w_bc, d_norm_gain, d_cbc, d_bbc = ops["spread"](meta, lasts)
        return (
            block_out, d_input, d_norm_gain, g_z, g_x, d_w_bc, g_slab[:, SL : SL + H], g_out,
            d_cx, d_bx, d_cbc, d_bbc, d_dt_bias, d_a_log, d_skips, d_gg,
        )

    axes = ("shard", "ctx")
    total = lax.psum_scatter(groups[0].astype(f32), axes, scatter_dimension=0, tiled=True)
    g_first = lax.psum_scatter(grads[0][:D].astype(f32), axes, scatter_dimension=0, tiled=True)
    small = lax.psum(grads[0][D:].astype(f32), axes)
    bias_row = small[TAPS] + small[7]
    sums = small[8 : 8 + H, 0:256] + small[8 : 8 + H, 256:512]
    gain = norm_gain.astype(f32)[:, None]
    g_z, g_out = total[:, :IN], total[:, IN:]
    w_slab = jnp.concatenate([w_slice, w_dt], axis=1).astype(f32)
    g_slab = g_first[:, IN : IN + SL + H]
    d_gain = jnp.sum(w_z.astype(f32) * g_z + w_x.astype(f32) * g_first[:, :IN], axis=1)
    d_gain = (d_gain + jnp.sum(w_slab * g_slab, axis=1)) / gain[:, 0]
    last = jnp.concatenate([
        jnp.concatenate([g_slab[:, :SL], d_gain[:, None], jnp.zeros((br, 127 - SL), f32)], axis=1),
        jnp.pad(jnp.concatenate([small[:TAPS], bias_row[None, :]], axis=0)[:, IN : IN + SL],
                ((0, 7 - TAPS), (0, 128 - SL)))], axis=0)
    last = lax.all_gather(last, "tp")
    d_w_bc = jnp.concatenate([last[k, :br, :SL] for k in range(n_tp)], axis=1)
    d_norm_gain = jnp.sum(last[:, :br, SL], axis=0)
    d_cbc = jnp.concatenate([last[k, br : br + TAPS + 1, :SL] for k in range(n_tp)], axis=1)
    return (
        block_out, d_input, d_norm_gain,
        g_z, g_first[:, :IN], d_w_bc, g_slab[:, SL:], g_out,
        small[:TAPS, :IN], bias_row[:IN], d_cbc[:TAPS], d_cbc[TAPS],
        sums[:, 0], sums[:, 128] * -jnp.exp(a_log),
        jnp.sum(small[6, :IN].reshape(H, HW), axis=1), small[5, :IN],
    )


def solution(mesh):
    row = ("shard", "ctx")
    in_specs = (
        P(row, None), P(row), P(row, "tp"), P(row, "tp"), P(row, None), P(row, "tp"), P(row, "tp"),
        P(None, "tp"), P("tp"), P(), P(), P("tp"), P("tp"), P("tp"), P("tp"), P("shard", None), P(row),
        P(row, None),
    )
    out_specs = (
        P(row, None), P(row, None), P(row), P(row, "tp"), P(row, "tp"), P(row, None), P(row, "tp"),
        P(row, "tp"), P(None, "tp"), P("tp"), P(), P(), P("tp"), P("tp"), P("tp"), P("tp"),
    )
    return jax.shard_map(block, mesh=mesh, in_specs=in_specs, out_specs=out_specs, check_vma=False)
```

```python
import jax
import jax.numpy as jnp
from jax import lax
from jax.experimental import pallas as pl
from jax.experimental.pallas import tpu as pltpu
from jax.sharding import PartitionSpec as P


f32 = jnp.float32
bf16 = jnp.bfloat16
norm_eps = 1e-05
L = 128
NN = ((1,), (0,))
NT = ((1,), (1,))
TN = ((0,), (0,))
HI = lax.Precision.HIGHEST


def dot(a, b, dims=NN, precision=None):
    return lax.dot_general(a, b, (dims, ((), ())), preferred_element_type=f32, precision=precision)


def split(v):
    if v.dtype == bf16:
        return v, None
    high = v.astype(bf16)
    return high, (v - high.astype(f32)).astype(bf16)


def dot3(a, b, dims=NN):
    ah, al = split(a) if not isinstance(a, tuple) else a
    bh, bl = split(b) if not isinstance(b, tuple) else b
    total = dot(ah, bh, dims)
    if bl is not None:
        total = total + dot(ah, bl, dims)
    if al is not None:
        total = total + dot(al, bh, dims)
    return total


def iota(shape, dim):
    return lax.broadcasted_iota(jnp.int32, shape, dim)


def sigmoid(v):
    return 1.0 / (1.0 + jnp.exp(-v))


def softplus(v):
    return jnp.maximum(v, 0.0) + jnp.log1p(jnp.exp(-jnp.abs(v)))


class Meta:
    def __init__(self, ref, sizes):
        self.ref, self.sizes = ref, sizes
        self.me_s, self.me_c, self.me_t = ref[0], ref[1], ref[2]
        self.base = self.me_c * sizes["T"]
        self.half = lax.rem(self.me_t, 2)
        bounds, total = [], 0
        for i in range(sizes["seqs"]):
            total = total + ref[3 + i]
            bounds.append(total)
        self.bounds = bounds

    def place(self, i, sign):
        n_ctx, n_sh = self.sizes["ctx"], self.sizes["shards"] // self.sizes["ctx"]
        shard = lax.rem(self.me_s + i // n_ctx, n_sh)
        ctx = lax.rem(self.me_c + sign * (i % n_ctx) + n_ctx, n_ctx)
        return (shard * n_ctx + ctx) * (self.sizes["D"] // self.sizes["shards"])

    def shard_row(self, i):
        return self.place(i, -1)

    def block_row(self, i):
        return self.place(i, 1)

    def peer(self, k):
        return jnp.bitwise_xor(self.me_t, k)

    def segment(self, pos):
        total = 0
        for bound in self.bounds:
            total = total + jnp.where(pos >= bound, 1, 0)
        return jnp.where(pos < 0, -1, total)


def load_weights(meta, shards, scratch):
    rows = shards[0].shape[0]
    for i, shard in enumerate(shards):
        at = meta.shard_row(i) if len(shards) > 1 else 0
        if len(shards) > 1:
            at = pl.multiple_of(at, 16)
        scratch[pl.ds(at, rows), :] = shard[...]


class Step:
    chunk, inner, count = None, 0, 1


def when_first(body):
    if Step.inner == 0:
        pl.when(pl.program_id(0) == 0)(body)


def when_later(body):
    if Step.inner == 0:
        pl.when(pl.program_id(0) > 0)(body)
    else:
        body()


def when_last(body):
    if Step.inner == Step.count - 1:
        pl.when(pl.program_id(0) == pl.num_programs(0) - 1)(body)


def unrolled(kernel, ins, outs, count):
    axes, wide, falls = [], [], []
    for item in (*ins, *outs):
        axis, falling = None, False
        if item[0] != "smem":
            moved = [d for d, (a, b) in enumerate(zip(item[1](0), item[1](1))) if a != b]
            axis = moved[0] if moved else None
        if axis is not None:
            block = tuple(n * count if d == axis else n for d, n in enumerate(item[0]))
            index = item[1]
            top = index(0)[axis]
            falling = index(1)[axis] < top
            if falling:
                top = (top + 1) // count - 1
                index = lambda i, axis=axis, top=top, n=len(block): tuple(
                    top - i if d == axis else 0 for d in range(n)
                )
            item = (block, index) + tuple(item[2:])
        axes.append(axis)
        falls.append(falling)
        wide.append(item)

    def body(*refs):
        for inner in range(count):
            views = []
            for k, ref in enumerate(refs):
                axis = axes[k] if k < len(axes) else None
                if axis is None:
                    views.append(ref)
                    continue
                size = wide[k][0][axis] // count
                j = count - 1 - inner if falls[k] else inner
                at = tuple(
                    slice(j * size, (j + 1) * size) if d == axis else slice(None)
                    for d in range(len(wide[k][0]))
                )
                views.append(ref.at[at])
            Step.chunk, Step.inner, Step.count = pl.program_id(0) * count + inner, inner, count
            kernel(*views)

    return body, wide[: len(ins)], wide[len(ins) :]


def call(kernel, grid, ins, outs, scratch, flops, args, unroll=1):
    if unroll > 1 and grid % unroll == 0:
        kernel, ins, outs = unrolled(kernel, ins, outs, unroll)
        grid = grid // unroll
    else:
        inner_kernel = kernel

        def kernel(*refs):
            Step.chunk, Step.inner, Step.count = pl.program_id(0), 0, 1
            inner_kernel(*refs)


    def spec(item):
        block, index = item[0], item[1]
        if block == "smem":
            return pl.BlockSpec(memory_space=pltpu.SMEM)
        return pl.BlockSpec(block, index)

    out_shape = [jax.ShapeDtypeStruct(o[2], o[3]) for o in outs]
    nbytes = sum(a.size * a.dtype.itemsize for a in args) + sum(
        o.size * o.dtype.itemsize for o in out_shape
    )
    return pl.pallas_call(
        kernel,
        grid=(grid,),
        in_specs=[spec(i) for i in ins],
        out_specs=[spec(o) for o in outs],
        out_shape=out_shape,
        scratch_shapes=scratch,
        cost_estimate=pl.CostEstimate(flops=flops, bytes_accessed=nbytes, transcendentals=0),
        compiler_params=pltpu.CompilerParams(dimension_semantics=("arbitrary",)),
    )(*args)


def whole(a):
    return (tuple(a.shape), lambda i, n=len(a.shape): (0,) * n)


def rows(a, count=L):
    return ((count, a.shape[1]), lambda i: (i, 0))


def cols(a):
    return ((a.shape[0], L), lambda i: (0, i))


def o_rows(shape, dtype, count=L):
    return ((count, shape[1]), lambda i: (i, 0), shape, dtype)


def o_cols(shape, dtype):
    return ((shape[0], L), lambda i: (0, i), shape, dtype)


def o_whole(shape, dtype):
    return (tuple(shape), lambda i, n=len(shape): (0,) * n, shape, dtype)


SMEM = ("smem", None)


def tri_leq():
    return jnp.where(iota((L, L), 0) <= iota((L, L), 1), 1.0, 0.0).astype(bf16)


def pair_mask(hw, which):
    lane = iota((L, 128), 1)
    return (lane >= which * hw) & (lane < (which + 1) * hw)


def allowed_mask(meta, c):
    start = meta.base + c * L
    pt, ps = start + iota((L, L), 0), start + iota((L, L), 1)
    return (meta.segment(pt) == meta.segment(ps)) & (pt >= ps)


def chunk_edges(meta, c):
    start = meta.base + c * L
    return meta.segment(start - 1), meta.segment(start + L - 1)


def pair_sum(left, right):
    def kernel(a, b, out):
        out[...] = (a[...].astype(f32) + b[...].astype(f32)).astype(bf16)

    vmem = pl.BlockSpec(memory_space=pltpu.VMEM)
    return pl.pallas_call(
        kernel, in_specs=[vmem, vmem], out_specs=vmem,
        out_shape=jax.ShapeDtypeStruct(left.shape, bf16),
        cost_estimate=pl.CostEstimate(flops=left.size, bytes_accessed=6 * left.size, transcendentals=0),
    )(left, right)


def to_shift(meta, c, width, distance):
    pos = meta.base + c * L + iota((L, 128), 0)
    same = meta.segment(pos) == meta.segment(pos - distance)
    return tiled(jnp.where(same & (pos - distance >= 0), 1.0, 0.0), width)


def tiled(mask, width):
    return jnp.concatenate([mask] * (width // 128), axis=1)


def flag(cond):
    return jnp.where(cond, 1.0, 0.0).astype(f32)


def build(sizes):
    T, D, IN, N, H, TAPS = (sizes[k] for k in ("T", "D", "IN", "N", "H", "TAPS"))
    n_tp, n_ctx, nC = sizes["tp"], sizes["ctx"], sizes["T"] // L
    HW = IN // H
    HPT = 128 // HW
    SL = 2 * N // n_tp
    PAIRS = IN // 128
    DIRECT = sizes["shards"] > 1
    NSH = sizes["shards"]
    PK = IN + 128 + 2 * N
    EXT = IN + 2 * N
    SP = 16
    HB = T // 2 // nC

    def expand_matrix():
        r, l = iota((128, IN), 0), iota((128, IN), 1)
        return jnp.where((r >= SL) & (r < SL + H) & (l // HW == r - SL), 1.0, 0.0)

    def head_select():
        r, l = iota((8, IN), 0), iota((8, IN), 1)
        return jnp.where((l // HW == r) & (r < H), 1.0, 0.0)

    def slab_select():
        r, l = iota((8, 128), 0), iota((8, 128), 1)
        return jnp.where((l == r + SL) & (r < H), 1.0, 0.0)

    def local_weights(cum, meta, c, last):
        return jnp.exp(cum[L - 1 : L, :] - cum) * in_segment(meta, c, last)

    def in_segment(meta, c, which):
        same = meta.segment(meta.base + c * L + iota((L, 128), 0)) == which
        return tiled(jnp.where(same, 1.0, 0.0), IN)

    def k_project(*refs):
        meta = Meta(refs[0], sizes)
        x_ref, xh_ref, cw_ref, hp_ref, hc_ref, mask_ref = refs[1:7]
        shards = refs[7 : 7 + NSH]
        (nb_ref, pr_ref, prh_ref, sm_ref, act_ref, dt_ref, cum_ref, dtr_ref, cumr_ref, hpre_ref,
         pp_ref, pack_ref) = refs[7 + NSH : 19 + NSH]
        gain_ref, w_ref, ext_ref, st_ref, ps_ref = refs[19 + NSH :]
        c = Step.chunk

        @when_first
        def _():
            load_weights(meta, shards, w_ref)
            xh = xh_ref[...]
            inv_h = lax.rsqrt(jnp.mean(xh * xh, axis=1, keepdims=True) + norm_eps)
            pick = jnp.where(iota((8, 128), 1) == SL + H, 1.0, 0.0).astype(bf16)
            gain_ref[...] = dot(pick, w_ref[:, IN : IN + 128], NT)
            nh = (xh * inv_h * gain_ref[...]).astype(bf16)
            ph = dot(nh, w_ref[...]).astype(bf16).astype(f32)
            prh_ref[...] = ph
            ext_ref[0:8, :IN] = ph[:, :IN]
            ext_ref[0:8, IN:] = ph[:, IN + 128 :]
            st_ref[...] = jnp.zeros((N, IN), f32)
            ps_ref[...] = jnp.ones((8, IN), f32)

        @when_later
        def _():
            ext_ref[0:8, :] = ext_ref[L : L + 8, :]

        x = x_ref[...]
        inv = lax.rsqrt(jnp.mean(x * x, axis=1, keepdims=True) + norm_eps)
        nb = (x * inv * gain_ref[0:1, :]).astype(bf16)
        nb_ref[...] = nb
        pr = dot(nb, w_ref[...]).astype(bf16)
        pr_ref[...] = pr
        prf = pr.astype(f32)
        ext_ref[8 : 8 + L, :IN] = prf[:, :IN]
        ext_ref[8 : 8 + L, IN:] = prf[:, IN + 128 :]
        summed = jnp.zeros((L, EXT), f32) + cw_ref[TAPS : TAPS + 1, :]
        for k in range(TAPS):
            d = TAPS - 1 - k
            term = cw_ref[k : k + 1, :] * ext_ref[8 - d : 8 - d + L, :]
            summed = summed + (term if d == 0 else term * to_shift(meta, c, EXT, d))
        sm_ref[...] = summed
        act = summed * sigmoid(summed)
        act_ref[...] = act
        slab = pr[:, IN : IN + 128]
        hp, hc = hp_ref[...], hc_ref[...]
        mask8 = mask_ref[...]
        mask_c = dot(mask8, jnp.where(iota((8, IN), 0) == 0, 1.0, 0.0), TN)
        dt = softplus(dot(slab, expand_matrix().astype(bf16)) + hp[0:1, :]) * mask_c
        dtr = softplus(dot(slab_select().astype(bf16), slab, NT) + hc[:, 0:1]) * mask8[0:1, :]
        tri = tri_leq()
        cum = dot3(tri, dt * hp[1:2, :], TN)
        cumr = dot3(dtr * hc[:, 1:2], tri)
        dt_ref[...], cum_ref[...], dtr_ref[...], cumr_ref[...] = dt, cum, dtr, cumr
        prev, last = chunk_edges(meta, c)
        xd = dt * act[:, :IN]
        ws = local_weights(cum, meta, c, last)
        b = act[:, IN : IN + N]
        passing = jnp.exp(cum[L - 1 : L, :]) * flag(prev == last)
        at = pl.multiple_of(c * N, N)
        st, ps = st_ref[...], ps_ref[...]
        hpre_ref[pl.ds(at, N), :] = st
        pp_ref[pl.ds(pl.multiple_of(c * 8, 8), 8), :] = ps
        st = passing * st + dot3(b, ws * xd, TN)
        ps = ps * passing
        st_ref[...], ps_ref[...] = st, ps

        @when_last
        def _():
            hpre_ref[nC * N : (nC + 1) * N, :] = st
            pp_ref[nC * 8 : nC * 8 + 8, :] = ps
            pack_ref[:N, :] = st.astype(bf16)
            pack_ref[N:, :] = jnp.concatenate([ps, ps], axis=0).astype(bf16)

    def project(meta, x, xh, cw, hp, hc, mask8, shards):
        outs = [
            o_rows((T, D), bf16), o_rows((T, PK), bf16), o_whole((8, PK), f32),
            o_rows((T, EXT), f32), o_rows((T, EXT), f32), o_rows((T, IN), f32),
            o_rows((T, IN), f32), o_cols((8, T), f32), o_cols((8, T), f32),
            o_whole(((nC + 1) * N, IN), f32), o_whole(((nC + 1) * 8, IN), f32),
            o_whole((N + SP, IN), bf16), o_whole((8, D), f32),
        ]
        ins = [SMEM, rows(x), whole(xh), whole(cw), whole(hp), whole(hc), cols(mask8)]
        ins += [whole(s) for s in shards]
        scratch = [
            pltpu.VMEM((D, PK), bf16), pltpu.VMEM((L + 8, EXT), f32),
            pltpu.VMEM((N, IN), f32), pltpu.VMEM((8, IN), f32),
        ]
        return call(k_project, nC, ins, outs, scratch, 2 * T * D * PK,
                    [meta, x, xh, cw, hp, hc, mask8, *shards], unroll=2)

    def head_decay(meta_mask, cum, cumr, h):
        gap = cum[:, h * HW : h * HW + 1] - cumr[h : h + 1, :]
        return jnp.where(meta_mask, jnp.exp(gap), 0.0)

    def k_intra(mref, act_ref, dt_ref, cum_ref, cumr_ref, y_ref):
        meta = Meta(mref, sizes)
        c = Step.chunk
        ok = allowed_mask(meta, c)
        b = act_ref[:, IN : IN + N]
        cc = act_ref[:, IN + N :]
        scores = dot3(cc, b, NT)
        cum, cumr = cum_ref[...], cumr_ref[...]
        for p in range(PAIRS):
            sl = slice(p * 128, p * 128 + 128)
            xd = (dt_ref[:, sl] * act_ref[:, sl])
            y = None
            for j in range(HPT):
                g = (scores * head_decay(ok, cum, cumr, p * HPT + j))
                part = dot3(g, xd)
                y = part if y is None else jnp.where(pair_mask(HW, j), part, y)
            y_ref[:, sl] = y

    def intra(meta, act, dt, cum, cumr):
        return call(k_intra, nC, [SMEM, rows(act), rows(dt), rows(cum), cols(cumr)],
                    [o_rows((T, IN), f32)], [], 4 * T * L * IN, [meta, act, dt, cum, cumr], unroll=2)[0]

    def k_gate(*refs):
        meta = Meta(refs[0], sizes)
        nb_ref, do_ref = refs[1:3]
        shards = refs[3 : 3 + NSH]
        z_ref, dm_ref, w_ref = refs[3 + NSH :]

        @when_first
        def _():
            load_weights(meta, shards, w_ref)

        z_ref[...] = dot(nb_ref[...], w_ref[:, :IN]).astype(bf16)
        dm_ref[...] = dot(do_ref[...].astype(bf16), w_ref[:, IN:])

    def gate(meta, nb, d_out, shards):
        return call(k_gate, nC, [SMEM, rows(nb), rows(d_out)] + [whole(s) for s in shards],
                    [o_rows((T, IN), bf16), o_rows((T, IN), f32)],
                    [pltpu.VMEM((D, 2 * IN), bf16)], 4 * T * D * IN, [meta, nb, d_out, *shards], unroll=2)

    def chain(packs):
        total = None
        for pack in reversed(packs):
            state = pack[:N, :].astype(f32)
            total = state if total is None else state + pack[N : N + 1, :].astype(f32) * total
        return total

    def k_output(*refs):
        meta = Meta(refs[0], sizes)
        act_ref, cum_ref, y_ref, z_ref, dm_ref, hpre_ref, pp_ref, hp_ref, gg_ref = refs[1:10]
        packs = refs[10 : 10 + n_ctx - 1]
        yo_ref, stat_ref, ent_ref = refs[9 + n_ctx :]
        c = Step.chunk

        @when_first
        def _():
            ent_ref[...] = chain(packs)

        prev, _ = chunk_edges(meta, c)
        hin = (hpre_ref[...] + pp_ref[0:1, :] * ent_ref[...])
        cum = cum_ref[...]
        ent = jnp.exp(cum) * in_segment(meta, c, prev)
        y = y_ref[...] + ent * dot3(act_ref[:, IN + N :], hin)
        yo_ref[...] = y
        out = y + hp_ref[2:3, :] * act_ref[:, :IN]
        z = z_ref[...].astype(f32)
        gated = out * (z * sigmoid(z))
        ones = jnp.ones((8, IN), bf16)
        sq = dot3(ones, gated * gated, NT)
        bd = dot3(ones, dm_ref[...] * gg_ref[0:1, :] * gated, NT)
        stat_ref[...] = jnp.where(iota((8, L), 0) == 0, sq, bd)

    def output(meta, act, cum, y, z, dm, hpre, pp, hp, gg, packs):
        ins = [SMEM, rows(act), rows(cum), rows(y), rows(z), rows(dm), rows(hpre, N), rows(pp, 8),
               whole(hp), whole(gg)] + [whole(p) for p in packs]
        outs = [o_rows((T, IN), f32), o_cols((8, T), f32), o_whole((N, IN), f32)]
        return call(k_output, nC, ins, outs, [], 4 * T * IN * N,
                    [meta, act, cum, y, z, dm, hpre, pp, hp, gg, *packs], unroll=2)

    def k_norm(*refs):
        meta = Meta(refs[0], sizes)
        act_ref, cum_ref, y_ref, z_ref, dm_ref, hp_ref, gg_ref = refs[1:8]
        stats = refs[8 : 8 + n_tp]
        mix_ref, dz_ref, dy_ref, suf_ref, psuf_ref, pack_ref, sums_ref = refs[8 + n_tp : 15 + n_tp]
        st_ref, ps_ref = refs[15 + n_tp :]
        c = nC - 1 - Step.chunk

        @when_first
        def _():
            st_ref[...] = jnp.zeros((N, IN), f32)
            ps_ref[...] = jnp.ones((8, IN), f32)
            sums_ref[...] = jnp.zeros((8, IN), f32)

        stat = stats[0][...]
        for s in stats[1:]:
            stat = stat + s[...]
        inner = float(IN * n_tp)
        inv_r = lax.rsqrt(stat[0:1, :] / inner + norm_eps)
        beta_r = inv_r * inv_r * inv_r * stat[1:2, :] / inner
        row = iota((8, L), 0)
        both = jnp.where(row == 0, inv_r, jnp.where(row == 1, beta_r, 0.0))
        inv = dot3(both, jnp.where(iota((8, IN), 0) == 0, 1.0, 0.0).astype(bf16), TN)
        beta = dot3(both, jnp.where(iota((8, IN), 0) == 1, 1.0, 0.0).astype(bf16), TN)
        gg, skip = gg_ref[0:1, :], hp_ref[2:3, :]
        x = act_ref[:, :IN]
        out = y_ref[...] + skip * x
        z = z_ref[...].astype(f32)
        sig = sigmoid(z)
        ga = z * sig
        gated = out * ga
        dm = dm_ref[...]
        normal = gated * inv
        mix_ref[...] = (normal * gg).astype(bf16)
        dg = dm * gg * inv - gated * beta
        dz_ref[...] = (dg * out * sig * (1.0 + z * (1.0 - sig))).astype(bf16)
        dy = dg * ga
        dyb = dy
        dy_ref[...] = dyb
        s0 = jnp.sum(dm * normal, axis=0, keepdims=True)
        s1 = jnp.sum(dy * x, axis=0, keepdims=True)
        r8 = iota((8, IN), 0)
        sums_ref[...] += jnp.where(r8 == 0, s0, jnp.where(r8 == 1, s1, 0.0))
        prev, last = chunk_edges(meta, c)
        cum = cum_ref[...]
        ent = jnp.exp(cum) * in_segment(meta, c, prev)
        passing = jnp.exp(cum[L - 1 : L, :]) * flag(prev == last)
        st, ps = st_ref[...], ps_ref[...]
        suf_ref[...] = st
        psuf_ref[...] = ps
        cc = act_ref[:, IN + N :]
        st = passing * st + dot3(cc, ent * dyb.astype(f32), TN)
        ps = passing * ps
        st_ref[...], ps_ref[...] = st, ps

        @when_last
        def _():
            pack_ref[:N, :] = st.astype(bf16)
            pack_ref[N:, :] = jnp.concatenate([ps, ps], axis=0).astype(bf16)

    def norm(meta, act, cum, y, z, dm, hp, gg, stats):
        def back(item):
            block, index = item[0], item[1]
            return (block, lambda i: index(nC - 1 - i)) + tuple(item[2:])

        ins = [SMEM] + [back(rows(a)) for a in (act, cum, y, z, dm)] + [whole(hp), whole(gg)]
        ins += [back(cols(s)) for s in stats]
        outs = [back(o_rows((T, IN), bf16)), back(o_rows((T, IN), bf16)), back(o_rows((T, IN), f32)),
                back(o_rows((nC * N, IN), f32, N)), back(o_rows((nC * 8, IN), f32, 8)),
                o_whole((N + SP, IN), bf16), o_whole((8, IN), f32)]
        scratch = [pltpu.VMEM((N, IN), f32), pltpu.VMEM((8, IN), f32)]
        return call(k_norm, nC, ins, outs, scratch, 2 * T * IN * N,
                    [meta, act, cum, y, z, dm, hp, gg, *stats], unroll=2)

    def k_intra_back(mref, act_ref, dt_ref, cum_ref, cumr_ref, dy_ref, dxd_ref, dbc_ref):
        meta = Meta(mref, sizes)
        c = Step.chunk
        ok = allowed_mask(meta, c)
        b = act_ref[:, IN : IN + N]
        cc = act_ref[:, IN + N :]
        scores = dot3(cc, b, NT)
        cum, cumr = cum_ref[...], cumr_ref[...]
        d_scores = jnp.zeros((L, L), f32)
        for p in range(PAIRS):
            sl = slice(p * 128, p * 128 + 128)
            xd = (dt_ref[:, sl] * act_ref[:, sl])
            dy = dy_ref[:, sl]
            dxd = None
            for j in range(HPT):
                decay = head_decay(ok, cum, cumr, p * HPT + j)
                g = (scores * decay)
                part = dot3(g, dy, TN)
                dxd = part if dxd is None else jnp.where(pair_mask(HW, j), part, dxd)
                own = jnp.where(pair_mask(HW, j), dy.astype(f32), 0.0)
                d_scores = d_scores + dot3(own, xd, NT) * decay
            dxd_ref[:, sl] = dxd
        ds = d_scores
        dbc_ref[:, :N] = dot3(ds, cc, TN)
        dbc_ref[:, N:] = dot3(ds, b)

    def intra_back(meta, act, dt, cum, cumr, dy):
        return call(k_intra_back, nC,
                    [SMEM, rows(act), rows(dt), rows(cum), cols(cumr), rows(dy)],
                    [o_rows((T, IN), f32), o_rows((T, 2 * N), f32)], [], 8 * T * L * IN,
                    [meta, act, dt, cum, cumr, dy], unroll=2)

    def write_blocks(meta, total, outs):
        if not DIRECT:
            outs[0][...] = total[...].astype(bf16)
            return
        br = D // NSH
        for i in range(NSH):
            at = pl.multiple_of(meta.block_row(i), 8)
            outs[i % n_ctx][(i // n_ctx) * br : (i // n_ctx + 1) * br, :] = total[
                pl.ds(at, br), :
            ].astype(bf16)

    n_groups = n_ctx if DIRECT else 1
    group_rows = D // n_ctx if DIRECT else D

    def split_rows(meta, c, value, keep, send):
        at = pl.multiple_of(lax.rem(c, nC // 2) * L, L)

        @pl.when(c // (nC // 2) == meta.half)
        def _():
            keep[pl.ds(at, L), :] = value

        @pl.when(c // (nC // 2) != meta.half)
        def _():
            send[pl.ds(at, L), :] = value.astype(bf16)

    def k_outer(*refs):
        meta = Meta(refs[0], sizes)
        nb_ref, do_ref, mix_ref, dz_ref = refs[1:5]
        shards = refs[5 : 5 + NSH]
        outs = refs[5 + NSH : 5 + NSH + n_groups]
        keep_ref, send_ref = refs[5 + NSH + n_groups : 7 + NSH + n_groups]
        w_ref, total = refs[7 + NSH + n_groups :]
        c = pl.program_id(0)

        @pl.when(c == 0)
        def _():
            load_weights(meta, shards, w_ref)

        mix = mix_ref[pl.ds(pl.multiple_of(c * L, L), L), :]
        split_rows(meta, c, dot(mix, w_ref[:, IN:], NT), keep_ref, send_ref)

        @pl.when(c == nC - 1)
        def _():
            total[:, :IN] = dot(nb_ref[...], dz_ref[...], TN)
            total[:, IN:] = dot(do_ref[...].astype(bf16), mix_ref[...], TN)
            write_blocks(meta, total, outs)

    def outer(meta, nb, d_out, mix, dz, shards):
        outs = [o_whole((group_rows, 2 * IN), bf16)] * n_groups
        outs += [o_whole((T // 2, D), f32), o_whole((T // 2, D), bf16)]
        ins = [SMEM] + [whole(a) for a in (nb, d_out, mix, dz, *shards)]
        scratch = [pltpu.VMEM((D, 2 * IN), bf16), pltpu.VMEM((D, 2 * IN), f32)]
        got = call(k_outer, nC, ins, outs, scratch, 6 * T * D * IN,
                   [meta, nb, d_out, mix, dz, *shards])
        return got[:n_groups], got[n_groups], got[n_groups + 1]

    def k_scan_back(*refs):
        meta = Meta(refs[0], sizes)
        (act_ref, sm_ref, pr_ref, dt_ref, cum_ref, dtr_ref, y_ref, dy_ref, dxd_ref, dbc_ref, hpre_ref,
         hnext_ref, pp_ref, pnext_ref, ent_ref, suf_ref, psuf_ref, hp_ref, hc_ref, mask_ref, bk_ref,
         bg_ref) = refs[1:23]
        packs, at = refs[23 : 22 + n_ctx], 22 + n_ctx
        dsx_ref, ddt_ref, sums_ref, edge_ref, pair_ref = refs[at : at + 5]
        slices = refs[at + 5 : at + 5 + n_tp]
        edges = refs[at + 5 + n_tp : at + 4 + 2 * n_tp]
        exit_ref = refs[at + 4 + 2 * n_tp]
        c = pl.program_id(0)
        pair_ref[...] = (bk_ref[...] + bg_ref[...].astype(f32)).astype(bf16)

        @pl.when(c == 0)
        def _():
            exit_ref[...] = chain(packs)
            sums_ref[...] = jnp.zeros((16, 128), f32)

        prev, last = chunk_edges(meta, c)
        hin = hpre_ref[...] + pp_ref[0:1, :] * ent_ref[...]
        hout = hnext_ref[...] + pnext_ref[0:1, :] * ent_ref[...]
        dh = suf_ref[...] + psuf_ref[0:1, :] * exit_ref[...]
        hinb, dhb = hin, dh
        cum, dt, x = cum_ref[...], dt_ref[...], act_ref[:, :IN]
        b = act_ref[:, IN : IN + N]
        ws = local_weights(cum, meta, c, last)
        ent = jnp.exp(cum) * in_segment(meta, c, prev)
        xd = dt * x
        dyf = dy_ref[...].astype(f32)
        leaving = dot3(b, dhb)
        wx = ws * xd
        dxd_in = dxd_ref[...]
        dxd = dxd_in + ws * leaving
        db = dbc_ref[:, :N] + dot3(wx, dhb, NT)
        dc = dbc_ref[:, N:] + dot3(ent * dyf, hinb, NT)
        hs = head_select().astype(bf16)
        dcum = dot3(hs, dyf * y_ref[...] - xd * dxd_in - wx.astype(f32) * leaving, NT)
        final = dot3(hs, jnp.zeros((8, IN), f32) + jnp.sum(dhb.astype(f32) * hout, axis=0, keepdims=True), NT)
        da = dot3(dcum, tri_leq(), NT) + final[:, 0:1]
        hc = hc_ref[...]
        dtr, mask8 = dtr_ref[...], mask_ref[...]
        ddt = da * hc[:, 1:2] + dot3(hs, dxd * x, NT)
        slab = pr_ref[:, IN : IN + 128]
        pre_r = dot(slab_select().astype(bf16), slab, NT) + hc[:, 0:1]
        dpre = ddt * mask8[0:1, :] * sigmoid(pre_r)
        ddt_ref[...] = dot(dpre.astype(bf16), slab_select().astype(bf16), TN).astype(bf16)
        ones = jnp.ones((L, 128), bf16)
        sums_ref[0:8, :] += dot3(dpre, ones)
        sums_ref[8:16, :] += dot3(da * dtr, ones)
        sm = sm_ref[...]
        sig = sigmoid(sm)
        dsilu = sig * (1.0 + sm * (1.0 - sig))
        dsx = (hp_ref[2:3, :] * dyf + dt * dxd) * dsilu[:, :IN]
        dsx_ref[...] = dsx
        dsb = (jnp.concatenate([db, dc], axis=1) * dsilu[:, IN:]).astype(bf16)
        quarter = c // (nC // 2)
        at = pl.multiple_of(lax.rem(c, nC // 2) * L, L)
        r, l = iota((2 * N, 128), 0), iota((2 * N, 128), 1)
        for k in range(n_tp):
            left = meta.peer(k) * SL
            lane0 = quarter * SL
            pick = jnp.where((r - left == l - lane0) & (l >= lane0) & (l < lane0 + SL), 1.0, 0.0)
            part = dot(dsb, pick.astype(bf16)).astype(bf16)

            @pl.when(quarter == 0)
            def _():
                slices[k][pl.ds(at, L), :] = part

            @pl.when(quarter != 0)
            def _():
                slices[k][pl.ds(at, L), :] = slices[k][pl.ds(at, L), :] + part

            @pl.when(c == 0)
            def _():
                if k == 0:
                    edge_ref[:, :IN] = dsx[0:8, :]
                    edge_ref[:, IN:] = part[0:8, :].astype(f32)
                else:
                    edges[k - 1][...] = part[0:8, :].astype(f32)

    def scan_back(meta, act, sm, pr, dt, cum, dtr, y, dy, dxd, dbc, hpre, pp, ent, suf, psuf, hp, hc,
                  mask8, b_keep, b_got, packs):
        def later(item):
            return (item[0], lambda i: item[1](i + 1))

        ins = [SMEM, rows(act), rows(sm), rows(pr), rows(dt), rows(cum), cols(dtr), rows(y), rows(dy),
               rows(dxd), rows(dbc), rows(hpre, N), later(rows(hpre, N)), rows(pp, 8),
               later(rows(pp, 8)), whole(ent), rows(suf, N), rows(psuf, 8), whole(hp), whole(hc),
               cols(mask8), rows(b_keep, HB), rows(b_got, HB)] + [whole(p) for p in packs]
        outs = [o_rows((T, IN), f32), o_rows((T, 128), bf16), o_whole((16, 128), f32),
                o_whole((8, IN + 128), f32), o_rows((T // 2, D), bf16, HB)]
        outs += [o_whole((T // 2, 128), bf16)] * n_tp + [o_whole((8, 128), f32)] * (n_tp - 1)
        got = call(k_scan_back, nC, ins, outs, [pltpu.VMEM((N, IN), f32)],
                   6 * T * IN * N,
                   [meta, act, sm, pr, dt, cum, dtr, y, dy, dxd, dbc, hpre, hpre, pp, pp, ent, suf,
                    psuf, hp, hc, mask8, b_keep, b_got, *packs])
        return got[:5], got[5 : 5 + n_tp], got[5 + n_tp :]

    PW = IN + 128
    br9 = D // NSH

    def k_conv_back(*refs):
        meta = Meta(refs[0], sizes)
        nb_ref, pr_ref, prp_ref, prh_ref, dz_ref, ddt_ref, dsx_ref, dsn_ref = refs[1:9]
        cw_ref, sums_ref, ssum_ref, edge_ref = refs[9:13]
        at = 13
        slices, at = refs[at : at + n_tp], at + n_tp
        edges, at = refs[at : at + n_tp - 1], at + n_tp - 1
        shards, at = refs[at : at + NSH], at + NSH
        zshards, at = refs[at : at + NSH], at + NSH
        gs, at = refs[at : at + NSH], at + NSH
        keep_ref, send_ref = refs[at : at + 2]
        at += 2
        w_ref, wz_ref, ex_ref, px_ref, sl_ref, total, tap_ref, dp_ref = refs[at:]
        c = pl.program_id(0)

        @pl.when(c == 0)
        def _():
            load_weights(meta, shards, w_ref)
            load_weights(meta, zshards, wz_ref)
            tap_ref[...] = jnp.zeros((8, PW), f32)
            sl = slices[0][...].astype(f32)
            for s in slices[1:]:
                sl = sl + s[...].astype(f32)
            low = iota((T // 2, 128), 1) < SL
            sl_ref[0 : T // 2, :] = jnp.where(low, sl, 0.0)
            sl_ref[T // 2 : T, :] = jnp.where(low, pltpu.roll(sl, 128 - SL, 1), 0.0)
            e = edge_ref[:, IN:]
            for s in edges:
                e = e + s[...]
            sl_ref[T : T + 8, :] = jnp.where(iota((8, 128), 1) < SL, e, 0.0)

        here = pl.multiple_of(c * L, L)
        after = pl.multiple_of(c * L + L, L)
        ex_ref[0:L, :IN] = dsx_ref[...]
        ex_ref[0:L, IN:] = sl_ref[pl.ds(here, L), :]
        ex_ref[L : L + 8, IN:] = sl_ref[pl.ds(after, 8), :]
        ex_ref[L : L + 8, :IN] = jnp.where(c == nC - 1, edge_ref[:, :IN], dsn_ref[...])
        low = iota((L, PW), 1) < IN + SL
        px_ref[8 : 8 + L, :] = pr_ref[:, :PW].astype(f32)
        px_ref[0:8, :] = jnp.where(c == 0, prh_ref[:, :PW], prp_ref[8:16, :PW].astype(f32))
        cw = cw_ref[...]
        ds = ex_ref[0:L, :]
        dpre = jnp.zeros((L, PW), f32)
        pos = meta.base + c * L + iota((L, 128), 0)
        seg = meta.segment(pos)
        group = T * n_ctx
        r8 = iota((8, PW), 0)
        taps = jnp.where(r8 == TAPS, jnp.sum(ds, axis=0, keepdims=True), 0.0)
        for k in range(TAPS):
            d = TAPS - 1 - k
            reach = cw[k : k + 1, :] * ex_ref[d : d + L, :]
            prior = ds * px_ref[8 - d : 8 - d + L, :]
            if d > 0:
                ahead = jnp.where((seg == meta.segment(pos + d)) & (pos + d < group), 1.0, 0.0)
                reach = reach * tiled(ahead, PW)
                prior = prior * to_shift(meta, c, PW, d)
            dpre = dpre + reach
            taps = taps + jnp.where(r8 == k, jnp.sum(prior, axis=0, keepdims=True), 0.0)
        tap_ref[...] += taps
        dpre = jnp.where(low, dpre, 0.0)
        dproj = dpre.astype(bf16)
        dslab = (dpre[:, IN:] + ddt_ref[...].astype(f32)).astype(bf16)
        dproj = jnp.concatenate([dproj[:, :IN], dslab], axis=1)
        dp_ref[pl.ds(here, L), :] = dproj
        q = dot(dproj, w_ref[:, :PW], NT) + dot(dz_ref[...], wz_ref[:, :IN], NT)
        split_rows(meta, c, q, keep_ref, send_ref)

        @pl.when(c == nC - 1)
        def _():
            total[...] = dot(nb_ref[...], dp_ref[...], TN)
            low8 = iota((8, PW), 1) < IN + SL
            s = ssum_ref[...]
            zero = jnp.zeros((8, 128), f32)
            pad = jnp.concatenate([s, jnp.zeros((8, PW - IN), f32)], axis=1)
            first = jnp.where(low8, tap_ref[...], 0.0)
            first = jnp.where(r8 == 5, pad[0:1, :], jnp.where(r8 == 6, pad[1:2, :], first))
            lead = first.astype(bf16).astype(f32)
            first = jnp.where(r8 == 7, (first - lead)[TAPS : TAPS + 1, :], first)
            pair = [sums_ref[0:8, :], sums_ref[8:16, :]]
            rest = [p - p.astype(bf16).astype(f32) for p in pair]
            tail = pair + rest + [zero] * (PW // 128 - 4)
            small = jnp.concatenate([first, jnp.concatenate(tail, axis=1)], axis=0).astype(bf16)
            if not DIRECT:
                gs[0][:D, :] = total[...].astype(bf16)
                gs[0][D:, :] = small
            else:
                for i in range(NSH):
                    at = pl.multiple_of(meta.block_row(i), 8)
                    gs[i][:br9, :] = total[pl.ds(at, br9), :].astype(bf16)
                    gs[i][br9:, :] = small

    def conv_back(meta, nb, pr, prh, dz, ddt, dsx, cw9, sums, ssum, edge, slices, edges, shards,
                  zshards):
        step = L // 16
        prior = ((16, PK), lambda i: (jnp.maximum(i * step - 1, 0), 0))
        after = ((8, IN), lambda i: (jnp.minimum((i + 1) * (L // 8), T // 8 - 1), 0))
        ins = [SMEM, whole(nb), rows(pr), prior, whole(prh), rows(dz), rows(ddt), rows(dsx), after,
               whole(cw9), whole(sums), whole(ssum), whole(edge)]
        ins += [whole(a) for a in (*slices, *edges, *shards, *zshards)]
        outs = [o_whole((br9 + 16, PW), bf16)] * NSH
        outs += [o_whole((T // 2, D), f32), o_whole((T // 2, D), bf16)]
        scratch = [pltpu.VMEM((D, PK), bf16), pltpu.VMEM((D, 2 * IN), bf16),
                   pltpu.VMEM((L + 8, PW), f32), pltpu.VMEM((L + 8, PW), f32),
                   pltpu.VMEM((T + 8, 128), f32), pltpu.VMEM((D, PW), f32),
                   pltpu.VMEM((8, PW), f32), pltpu.VMEM((T, PW), bf16)]
        got = call(k_conv_back, nC, ins, outs, scratch, 4 * T * D * (PW + IN),
                    [meta, nb, pr, pr, prh, dz, ddt, dsx, dsx, cw9, sums, ssum, edge, *slices, *edges,
                     *shards, *zshards])
        return got[:NSH], got[NSH:]

    def k_tables(mref, wx, bx, wbc, bbc, bias, alog, skip, gain, mask, cw, cw9, hp, hc, gg, mask8):
        meta = Meta(mref, sizes)
        zeros = lambda n, w: jnp.zeros((n, w), f32)
        left = jnp.concatenate([wx[...], bx[...], zeros(7 - TAPS, IN)], axis=0)
        right = jnp.concatenate([wbc[...], bbc[...], zeros(7 - TAPS, 2 * N)], axis=0)
        cw[...] = jnp.concatenate([left, right], axis=1)
        r, l = iota((2 * N, 128), 0), iota((2 * N, 128), 1)
        pick = jnp.where((r == l + meta.me_t * SL) & (l < SL), 1.0, 0.0)
        cw9[...] = jnp.concatenate([left, dot(right, pick, NN, HI)], axis=1)
        rate = -jnp.exp(alog[...])
        row = iota((8, H), 0)
        rows8 = jnp.where(row == 0, bias[...], jnp.where(row == 1, rate, jnp.where(row == 2, skip[...], 0.0)))
        spread = jnp.where(iota((H, IN), 1) // HW == iota((H, IN), 0), 1.0, 0.0)
        hp[...] = dot(rows8, spread, NN, HI)
        eye = jnp.where(iota((8, 128), 0) == iota((8, 128), 1), 1.0, 0.0)
        turn = jnp.where(iota((8, H), 0) == iota((8, H), 1), 1.0, 0.0)
        hc[...] = dot(dot(turn, rows8, NT, HI), eye, NN, HI)
        gg[...] = jnp.zeros((8, IN), f32) + gain[...]
        mask8[...] = jnp.zeros((8, T), f32) + mask[...].astype(f32)

    def tables(*args):
        outs = [o_whole((8, EXT), f32), o_whole((8, PW), f32), o_whole((8, IN), f32),
                o_whole((8, 128), f32), o_whole((8, IN), f32), o_whole((8, T), f32)]
        return call(k_tables, 1, [SMEM] + [whole(a) for a in args[1:]], outs, [], 0, args)

    def k_finish(*refs):
        meta = Meta(refs[0], sizes)
        first_ref, second_ref = refs[1:3]
        blocks, parts = refs[3 : 3 + n_ctx], refs[3 + n_ctx : 5 + n_ctx]
        alog = refs[5 + n_ctx]
        gz, go, gx, slab_ref, wx, bx, gain_row, h_dt, h_log, h_skip, last, order = refs[6 + n_ctx :]
        zo = parts[0][...]
        for p in parts[1:]:
            zo = zo + p[...].astype(f32)
        gz[...], go[...] = zo[:, :IN], zo[:, IN:]
        total = None
        for r in range(n_ctx):
            b = blocks[r][...].astype(f32)
            total = b[:br9] if total is None else total + b[:br9]
            order[lax.rem(meta.me_c - r + n_ctx, n_ctx)] = b[br9:]
        small = order[0]
        for r in range(1, n_ctx):
            small = small + order[r]
        gx[...] = total[:, :IN]
        slab = total[:, IN:]
        slab_ref[...] = slab
        lane = iota((br9, 128), 1)
        w_slab = first_ref[:, IN : IN + 128].astype(f32)
        gain = jnp.sum(jnp.where(lane == SL + H, w_slab, 0.0), axis=1, keepdims=True)
        d_gain = jnp.sum(first_ref[:, :IN].astype(f32) * total[:, :IN], axis=1, keepdims=True)
        d_gain = d_gain + jnp.sum(second_ref[:, :IN].astype(f32) * zo[:, :IN], axis=1, keepdims=True)
        d_gain = d_gain + jnp.sum(jnp.where(lane < SL + H, w_slab * slab, 0.0), axis=1, keepdims=True)
        last[:br9, :] = jnp.where(lane < SL, slab, jnp.where(lane == SL, d_gain / gain, 0.0))
        top = small[0:8]
        bias = top[TAPS : TAPS + 1] + top[7:8]
        wx[...] = top[:TAPS, :IN]
        bx[...] = bias[:, :IN].reshape(IN)
        gain_row[...] = top[5:6, :IN].reshape(IN)
        taps = jnp.where(iota((8, PW), 0) == TAPS, bias, top)
        last[br9:, :] = jnp.where(iota((8, 128), 1) < SL, taps[:, IN:], 0.0)
        pair = small[8:16, 0:256] + small[8:16, 256:512]
        skip = dot(head_select(), jnp.zeros((8, IN), f32) + top[6:7, :IN], NT, HI)
        eye8 = iota((8, 128), 0) == iota((8, 128), 1)

        def flat(col):
            return jnp.sum(jnp.where(eye8, col, 0.0), axis=0, keepdims=True)[:, :H]

        h_dt[...] = flat(pair[:, 0:1]).reshape(H)
        h_log[...] = (flat(pair[:, 128:129]) * -jnp.exp(alog[...])).reshape(H)
        h_skip[...] = flat(skip[:, 0:1]).reshape(H)

    def finish(meta, first, second, blocks, parts, a_log):
        args = [meta, first, second, *blocks, *parts, a_log]
        outs = [o_whole((br9, IN), f32)] * 3 + [o_whole((br9, 128), f32), o_whole((TAPS, IN), f32),
                o_whole((IN,), f32), o_whole((IN,), f32), o_whole((H,), f32), o_whole((H,), f32),
                o_whole((H,), f32), o_whole((br9 + 8, 128), f32)]
        return call(k_finish, 1, [SMEM] + [whole(a) for a in args[1:]], outs,
                    [pltpu.VMEM((n_ctx, 16, PW), f32)], 0, args)

    def k_spread(mref, *refs):
        meta = Meta(mref, sizes)
        parts = refs[:n_tp]
        wbc, gain, taps, bias, last = refs[n_tp:]
        for k in range(n_tp):
            last[meta.peer(k)] = parts[k][...]
        per = 128 // SL
        lane = iota((br9 + 8, 128), 1)
        for t in range(n_tp // per):
            tile = last[t * per]
            for j in range(1, per):
                tile = jnp.where(lane >= j * SL, pltpu.roll(last[t * per + j], j * SL, 1), tile)
            sl = slice(t * 128, t * 128 + 128)
            wbc[:, sl] = tile[:br9]
            taps[:, sl] = tile[br9 : br9 + TAPS]
            bias[sl] = tile[br9 + TAPS : br9 + TAPS + 1].reshape(128)
        total = last[0][:br9]
        for k in range(1, n_tp):
            total = total + last[k][:br9]
        col = jnp.sum(jnp.where(iota((br9, 128), 1) == SL, total, 0.0), axis=1, keepdims=True)
        eye = iota((br9, br9), 0) == iota((br9, br9), 1)
        gain[...] = jnp.sum(jnp.where(eye, col, 0.0), axis=0, keepdims=True).reshape(br9)

    def spread(meta, parts):
        outs = [o_whole((br9, 2 * N), f32), o_whole((br9,), f32), o_whole((TAPS, 2 * N), f32),
                o_whole((2 * N,), f32)]
        return call(k_spread, 1, [SMEM] + [whole(p) for p in parts], outs,
                    [pltpu.VMEM((n_tp, br9 + 8, 128), f32)], 0, [meta, *parts])

    return dict(tables=tables, finish=finish, spread=spread, project=project, intra=intra, gate=gate, output=output, norm=norm,
                intra_back=intra_back, outer=outer, scan_back=scan_back, conv_back=conv_back,
                SL=SL, PW=PW)


def block(x_in, norm_gain, w_z, w_x, w_bc, w_dt, w_out, conv_wx, conv_bx, conv_wbc, conv_bbc, dt_bias,
          a_log, d_skip, gate_gain, seq_lens, token_mask, d_out):
    T, D = x_in.shape
    H, IN, N, TAPS = dt_bias.shape[0], w_z.shape[1], w_bc.shape[1] // 2, conv_wx.shape[0]
    n_sh, n_ctx, n_tp = (lax.axis_size(a) for a in ("shard", "ctx", "tp"))
    me_s, me_c, me_t = (lax.axis_index(a) for a in ("shard", "ctx", "tp"))
    direct = n_sh == 2 and n_ctx == 4
    NSH = n_sh * n_ctx if direct else 1
    seqs = seq_lens.shape[1]
    sizes = dict(T=T, D=D, IN=IN, N=N, H=H, TAPS=TAPS, tp=n_tp, ctx=n_ctx, seqs=seqs, shards=NSH)
    ops = build(sizes)
    SL = ops["SL"]
    HW = IN // H
    br = w_z.shape[0]

    def ring(count, step):
        return [(i, (i + step) % count) for i in range(count)]

    def xor(count, step):
        return [(i, i ^ step) for i in range(count)]

    def gather(part):
        if not direct:
            return [lax.all_gather(part, ("shard", "ctx"), axis=0, tiled=True)]
        here = [part]
        for k in range(1, n_ctx):
            here.append(lax.ppermute(part, "ctx", ring(n_ctx, k)))
        there = []
        for p in here:
            there.append(lax.ppermute(p, "shard", ring(n_sh, 1)))
        return here + there

    meta = jnp.concatenate([jnp.stack([me_s, me_c, me_t]).astype(jnp.int32), seq_lens[0]])

    w_slice = lax.dynamic_slice_in_dim(w_bc, me_t * SL, SL, 1)
    first = jnp.concatenate(
        [w_x, w_slice, w_dt, norm_gain[:, None], jnp.zeros((br, 127 - SL - H), bf16), w_bc], axis=1
    )
    x_tail = lax.ppermute(x_in[T - 8 :], "ctx", [(i, i + 1) for i in range(n_ctx - 1)])
    shards = gather(first)
    second = jnp.concatenate([w_z, w_out], axis=1)
    shards2 = gather(second)

    cw, cw9, hp, hc, gg, mask8 = ops["tables"](
        meta, conv_wx, conv_bx[None, :], conv_wbc, conv_bbc[None, :], dt_bias[None, :],
        a_log[None, :], d_skip[None, :], gate_gain[None, :], token_mask[None, :])

    (nb, pr, prh, sm, act, dt, cum, dtr, cumr, hpre, pp, pack, gain_row) = ops["project"](
        meta, x_in, x_tail, cw, hp, hc, mask8, shards)
    packs = [lax.ppermute(pack, "ctx", [(i, i + k) for i in range(n_ctx - k)]) for k in range(1, n_ctx)]
    y_in = ops["intra"](meta, act, dt, cum, cumr)
    z, dm = ops["gate"](meta, nb, d_out, shards2)
    y, stat, entry = ops["output"](meta, act, cum, y_in, z, dm, hpre, pp, hp, gg, packs)
    stats = [stat] + [lax.ppermute(stat, "tp", xor(n_tp, k)) for k in range(1, n_tp)]
    mix, dz, dy, suf, psuf, bpack, ssum = ops["norm"](meta, act, cum, y, z, dm, hp, gg, stats)
    bpacks = []
    for k in range(1, n_ctx):
        bpacks.append(lax.ppermute(bpack, "ctx", [(i + k, i) for i in range(n_ctx - k)]))
    dxd, dbc = ops["intra_back"](meta, act, dt, cum, cumr, dy)
    groups, b_keep, b_send = ops["outer"](meta, nb, d_out, mix, dz, shards2)

    def both_halves(part):
        mine = part.astype(bf16)
        other = lax.ppermute(mine, "tp", xor(n_tp, 1))
        flip = me_t % 2 == 1
        low, high = jnp.where(flip, other, mine), jnp.where(flip, mine, other)
        return jnp.concatenate([low, high], axis=0).astype(f32)

    b_got = lax.ppermute(b_send, "tp", xor(n_tp, 1))
    (dsx, ddt, sums, edge, b_pair), slices, edges = ops["scan_back"](
        meta, act, sm, pr, dt, cum, dtr, y, dy, dxd, dbc, hpre, pp, entry, suf, psuf, hp, hc, mask8,
        b_keep, b_got, bpacks)
    got_edge = lax.ppermute(edge, "ctx", [(i + 1, i) for i in range(n_ctx - 1)])
    got_slices, got_edges = [slices[0]], []
    for k in range(1, n_tp):
        got_slices.append(lax.ppermute(slices[k], "tp", xor(n_tp, k)))
        across = [((i + 1) * n_tp + j, i * n_tp + (j ^ k)) for i in range(n_ctx - 1) for j in range(n_tp)]
        got_edges.append(lax.ppermute(edges[k - 1], ("ctx", "tp"), across))
    b_half = b_pair.astype(f32)
    for k in range(2, n_tp, 2):
        b_half = b_half + lax.ppermute(b_pair, "tp", xor(n_tp, k)).astype(f32)
    if direct:
        total = groups[0].astype(f32)
        for r in range(1, n_ctx):
            got = lax.ppermute(groups[r], "ctx", ring(n_ctx, r))
            total = total + got.astype(f32)
        other = lax.ppermute(total[br:].astype(bf16), "shard", ring(n_sh, 1))
        parts = [total[:br], other]
    grads, (q_keep, q_send) = ops["conv_back"](
        meta, nb, pr, prh, dz, ddt, dsx, cw9, sums, ssum, got_edge, got_slices, got_edges, shards,
        shards2)
    if direct:
        moved = []
        for r in [*range(1, n_ctx), 0]:
            got = lax.ppermute(grads[n_ctx + r], "shard", ring(n_sh, 1))
            moved.append(pair_sum(grads[r], got))
        blocks = [moved[-1]]
        for r in range(1, n_ctx):
            blocks.append(lax.ppermute(moved[r - 1], "ctx", ring(n_ctx, r)))

    q_got = lax.ppermute(q_send, "tp", xor(n_tp, 1))
    q_pair = pair_sum(q_keep, q_got)
    q_half = q_pair.astype(f32)
    for k in range(2, n_tp, 2):
        q_half = q_half + lax.ppermute(q_pair, "tp", xor(n_tp, k)).astype(f32)
    block_whole = both_halves(b_half)
    block_out = x_in + block_whole

    x_half = lax.dynamic_slice_in_dim(x_in, (me_t % 2) * (T // 2), T // 2, 0)
    inv = lax.rsqrt(jnp.mean(x_half * x_half, axis=1, keepdims=True) + norm_eps)
    q_half = q_half * gain_row[0:1, :]
    row_dot = jnp.sum(q_half * x_half, axis=1, keepdims=True)
    q_whole = both_halves(q_half * inv - x_half * (inv * inv * inv) * row_dot / D)
    d_input = d_out + q_whole

    if direct:
        g_z, g_out, g_x, g_slab, d_cx, d_bx, d_gg, d_dt_bias, d_a_log, d_skips, last = ops["finish"](
            meta, first, second, blocks, parts, a_log[None, :])
        lasts = [last]
        for k in range(1, n_tp):
            lasts.append(lax.ppermute(last, "tp", xor(n_tp, k)))
        d_w_dt = g_slab[:, SL : SL + H]
        d_w_bc, d_norm_gain, d_cbc, d_bbc = ops["spread"](meta, lasts)
        return (
            block_out, d_input, d_norm_gain, g_z, g_x, d_w_bc, d_w_dt, g_out,
            d_cx, d_bx, d_cbc, d_bbc, d_dt_bias, d_a_log, d_skips, d_gg,
        )

    axes = ("shard", "ctx")
    total = lax.psum_scatter(groups[0].astype(f32), axes, scatter_dimension=0, tiled=True)
    g_first = lax.psum_scatter(grads[0][:D].astype(f32), axes, scatter_dimension=0, tiled=True)
    small = lax.psum(grads[0][D:].astype(f32), axes)
    bias_row = small[TAPS] + small[7]
    sums = small[8 : 8 + H, 0:256] + small[8 : 8 + H, 256:512]
    gain = norm_gain.astype(f32)[:, None]
    g_z, g_out = total[:, :IN], total[:, IN:]
    w_slab = jnp.concatenate([w_slice, w_dt], axis=1).astype(f32)
    g_slab = g_first[:, IN : IN + SL + H]
    d_gain = jnp.sum(w_z.astype(f32) * g_z + w_x.astype(f32) * g_first[:, :IN], axis=1)
    d_gain = (d_gain + jnp.sum(w_slab * g_slab, axis=1)) / gain[:, 0]
    last = jnp.concatenate([
        jnp.concatenate([g_slab[:, :SL], d_gain[:, None], jnp.zeros((br, 127 - SL), f32)], axis=1),
        jnp.pad(jnp.concatenate([small[:TAPS], bias_row[None, :]], axis=0)[:, IN : IN + SL],
                ((0, 7 - TAPS), (0, 128 - SL)))], axis=0)
    last = lax.all_gather(last, "tp")
    d_w_bc = jnp.concatenate([last[k, :br, :SL] for k in range(n_tp)], axis=1)
    d_norm_gain = jnp.sum(last[:, :br, SL], axis=0)
    d_cbc = jnp.concatenate([last[k, br : br + TAPS + 1, :SL] for k in range(n_tp)], axis=1)
    return (
        block_out, d_input, d_norm_gain,
        g_z, g_first[:, :IN], d_w_bc, g_slab[:, SL:], g_out,
        small[:TAPS, :IN], bias_row[:IN], d_cbc[:TAPS], d_cbc[TAPS],
        sums[:, 0], sums[:, 128] * -jnp.exp(a_log),
        jnp.sum(small[6, :IN].reshape(H, HW), axis=1), small[5, :IN],
    )


def solution(mesh):
    row = ("shard", "ctx")
    in_specs = (
        P(row, None), P(row), P(row, "tp"), P(row, "tp"), P(row, None), P(row, "tp"), P(row, "tp"),
        P(None, "tp"), P("tp"), P(), P(), P("tp"), P("tp"), P("tp"), P("tp"), P("shard", None), P(row),
        P(row, None),
    )
    out_specs = (
        P(row, None), P(row, None), P(row), P(row, "tp"), P(row, "tp"), P(row, None), P(row, "tp"),
        P(row, "tp"), P(None, "tp"), P("tp"), P(), P(), P("tp"), P("tp"), P("tp"), P("tp"),
    )
    return jax.shard_map(block, mesh=mesh, in_specs=in_specs, out_specs=out_specs, check_vma=False)
```

```python
import jax
import jax.numpy as jnp
from jax import lax
from jax.experimental import pallas as pl
from jax.experimental.pallas import tpu as pltpu
from jax.sharding import PartitionSpec as P


f32 = jnp.float32
bf16 = jnp.bfloat16
norm_eps = 1e-05
L = 128
NN = ((1,), (0,))
NT = ((1,), (1,))
TN = ((0,), (0,))
AS, AC, AT = "shard", "ctx", "tp"
HI = lax.Precision.HIGHEST


def dot(a, b, dims=NN, precision=None):
    return lax.dot_general(a, b, (dims, ((), ())), preferred_element_type=f32, precision=precision)


def split(v):
    if v.dtype == bf16:
        return v, None
    high = v.astype(bf16)
    return high, (v - high.astype(f32)).astype(bf16)


def dot3(a, b, dims=NN):
    ah, al = split(a) if not isinstance(a, tuple) else a
    bh, bl = split(b) if not isinstance(b, tuple) else b
    total = dot(ah, bh, dims)
    if bl is not None:
        total = total + dot(ah, bl, dims)
    if al is not None:
        total = total + dot(al, bh, dims)
    return total


def iota(shape, dim):
    return lax.broadcasted_iota(jnp.int32, shape, dim)


def sigmoid(v):
    return 1.0 / (1.0 + jnp.exp(-v))


def softplus(v):
    return jnp.maximum(v, 0.0) + jnp.log1p(jnp.exp(-jnp.abs(v)))


class Meta:
    def __init__(self, ref, sizes):
        self.ref, self.sizes = ref, sizes
        self.me_s, self.me_c, self.me_t = ref[0], ref[1], ref[2]
        self.base = self.me_c * sizes["T"]
        self.half = lax.rem(self.me_t, 2)
        bounds, total = [], 0
        for i in range(sizes["seqs"]):
            total = total + ref[3 + i]
            bounds.append(total)
        self.bounds = bounds

    def place(self, i, sign):
        n_ctx, n_sh = self.sizes[AC], self.sizes["shards"] // self.sizes[AC]
        shard = lax.rem(self.me_s + i // n_ctx, n_sh)
        ctx = lax.rem(self.me_c + sign * (i % n_ctx) + n_ctx, n_ctx)
        return (shard * n_ctx + ctx) * (self.sizes["D"] // self.sizes["shards"])

    def shard_row(self, i):
        return self.place(i, -1)

    def block_row(self, i):
        return self.place(i, 1)

    def peer(self, k):
        return jnp.bitwise_xor(self.me_t, k)

    def segment(self, pos):
        total = 0
        for bound in self.bounds:
            total = total + jnp.where(pos >= bound, 1, 0)
        return jnp.where(pos < 0, -1, total)


def load_weights(meta, shards, scratch):
    rows = shards[0].shape[0]
    for i, shard in enumerate(shards):
        at = meta.shard_row(i) if len(shards) > 1 else 0
        if len(shards) > 1:
            at = pl.multiple_of(at, 16)
        scratch[pl.ds(at, rows), :] = shard[...]


class Step:
    chunk, inner, count = None, 0, 1


def when_first(body):
    if Step.inner == 0:
        pl.when(pl.program_id(0) == 0)(body)


def when_later(body):
    if Step.inner == 0:
        pl.when(pl.program_id(0) > 0)(body)
    else:
        body()


def when_last(body):
    if Step.inner == Step.count - 1:
        pl.when(pl.program_id(0) == pl.num_programs(0) - 1)(body)


def unrolled(kernel, ins, outs, count):
    axes, wide, falls = [], [], []
    for item in (*ins, *outs):
        axis, falling = None, False
        if item[0] != "smem":
            moved = [d for d, (a, b) in enumerate(zip(item[1](0), item[1](1))) if a != b]
            axis = moved[0] if moved else None
        if axis is not None:
            block = tuple(n * count if d == axis else n for d, n in enumerate(item[0]))
            index = item[1]
            top = index(0)[axis]
            falling = index(1)[axis] < top
            if falling:
                top = (top + 1) // count - 1
                index = lambda i, axis=axis, top=top, n=len(block): tuple(
                    top - i if d == axis else 0 for d in range(n)
                )
            item = (block, index) + tuple(item[2:])
        axes.append(axis)
        falls.append(falling)
        wide.append(item)

    def body(*refs):
        for inner in range(count):
            views = []
            for k, ref in enumerate(refs):
                axis = axes[k] if k < len(axes) else None
                if axis is None:
                    views.append(ref)
                    continue
                size = wide[k][0][axis] // count
                j = count - 1 - inner if falls[k] else inner
                at = tuple(
                    slice(j * size, (j + 1) * size) if d == axis else slice(None)
                    for d in range(len(wide[k][0]))
                )
                views.append(ref.at[at])
            Step.chunk, Step.inner, Step.count = pl.program_id(0) * count + inner, inner, count
            kernel(*views)

    return body, wide[: len(ins)], wide[len(ins) :]


def call(kernel, grid, ins, outs, scratch, flops, args, unroll=1):
    if unroll > 1 and grid % unroll == 0:
        kernel, ins, outs = unrolled(kernel, ins, outs, unroll)
        grid = grid // unroll
    else:
        inner_kernel = kernel

        def kernel(*refs):
            Step.chunk, Step.inner, Step.count = pl.program_id(0), 0, 1
            inner_kernel(*refs)


    def spec(item):
        block, index = item[0], item[1]
        if block == "smem":
            return pl.BlockSpec(memory_space=pltpu.SMEM)
        return pl.BlockSpec(block, index)

    out_shape = [jax.ShapeDtypeStruct(o[2], o[3]) for o in outs]
    nbytes = sum(a.size * a.dtype.itemsize for a in args) + sum(
        o.size * o.dtype.itemsize for o in out_shape
    )
    return pl.pallas_call(
        kernel,
        grid=(grid,),
        in_specs=[spec(i) for i in ins],
        out_specs=[spec(o) for o in outs],
        out_shape=out_shape,
        scratch_shapes=scratch,
        cost_estimate=pl.CostEstimate(flops=flops, bytes_accessed=nbytes, transcendentals=0),
        compiler_params=pltpu.CompilerParams(dimension_semantics=("arbitrary",)),
    )(*args)


def whole(a):
    return (tuple(a.shape), lambda i, n=len(a.shape): (0,) * n)


def rows(a, count=L):
    return ((count, a.shape[1]), lambda i: (i, 0))


def cols(a):
    return ((a.shape[0], L), lambda i: (0, i))


def o_rows(shape, dtype, count=L):
    return ((count, shape[1]), lambda i: (i, 0), shape, dtype)


def o_cols(shape, dtype):
    return ((shape[0], L), lambda i: (0, i), shape, dtype)


def o_whole(shape, dtype):
    return (tuple(shape), lambda i, n=len(shape): (0,) * n, shape, dtype)


SMEM = ("smem", None)


def tri_leq():
    return jnp.where(iota((L, L), 0) <= iota((L, L), 1), 1.0, 0.0).astype(bf16)


def pair_mask(hw, which):
    lane = iota((L, 128), 1)
    return (lane >= which * hw) & (lane < (which + 1) * hw)


def allowed_mask(meta, c):
    start = meta.base + c * L
    pt, ps = start + iota((L, L), 0), start + iota((L, L), 1)
    return (meta.segment(pt) == meta.segment(ps)) & (pt >= ps)


def chunk_edges(meta, c):
    start = meta.base + c * L
    return meta.segment(start - 1), meta.segment(start + L - 1)


def pair_sum(left, right):
    def kernel(a, b, out):
        out[...] = (a[...].astype(f32) + b[...].astype(f32)).astype(bf16)

    vmem = pl.BlockSpec(memory_space=pltpu.VMEM)
    return pl.pallas_call(
        kernel, in_specs=[vmem, vmem], out_specs=vmem,
        out_shape=jax.ShapeDtypeStruct(left.shape, bf16),
        cost_estimate=pl.CostEstimate(flops=left.size, bytes_accessed=6 * left.size, transcendentals=0),
    )(left, right)


def to_shift(meta, c, width, distance):
    pos = meta.base + c * L + iota((L, 128), 0)
    same = meta.segment(pos) == meta.segment(pos - distance)
    return tiled(jnp.where(same & (pos - distance >= 0), 1.0, 0.0), width)


def tiled(mask, width):
    return jnp.concatenate([mask] * (width // 128), axis=1)


def flag(cond):
    return jnp.where(cond, 1.0, 0.0).astype(f32)


def build(sizes):
    T, D, IN, N, H, TAPS = (sizes[k] for k in ("T", "D", "IN", "N", "H", "TAPS"))
    n_tp, n_ctx, nC = sizes[AT], sizes[AC], sizes["T"] // L
    HW = IN // H
    HPT = 128 // HW
    SL = 2 * N // n_tp
    PAIRS = IN // 128
    DIRECT = sizes["shards"] > 1
    NSH = sizes["shards"]
    PK = IN + 128 + 2 * N
    EXT = IN + 2 * N
    SP = 16
    HB = T // 2 // nC

    def expand_matrix():
        r, l = iota((128, IN), 0), iota((128, IN), 1)
        return jnp.where((r >= SL) & (r < SL + H) & (l // HW == r - SL), 1.0, 0.0)

    def head_select():
        r, l = iota((8, IN), 0), iota((8, IN), 1)
        return jnp.where((l // HW == r) & (r < H), 1.0, 0.0)

    def slab_select():
        r, l = iota((8, 128), 0), iota((8, 128), 1)
        return jnp.where((l == r + SL) & (r < H), 1.0, 0.0)

    def local_weights(cum, meta, c, last):
        return jnp.exp(cum[L - 1 : L, :] - cum) * in_segment(meta, c, last)

    def in_segment(meta, c, which):
        same = meta.segment(meta.base + c * L + iota((L, 128), 0)) == which
        return tiled(jnp.where(same, 1.0, 0.0), IN)

    def k_project(*refs):
        meta = Meta(refs[0], sizes)
        x_ref, xh_ref, cw_ref, hp_ref, hc_ref, mask_ref = refs[1:7]
        shards = refs[7 : 7 + NSH]
        (nb_ref, pr_ref, prh_ref, sm_ref, act_ref, dt_ref, cum_ref, dtr_ref, cumr_ref, hpre_ref,
         pp_ref, pack_ref) = refs[7 + NSH : 19 + NSH]
        gain_ref, w_ref, ext_ref, st_ref, ps_ref = refs[19 + NSH :]
        c = Step.chunk

        @when_first
        def _():
            load_weights(meta, shards, w_ref)
            xh = xh_ref[...]
            inv_h = lax.rsqrt(jnp.mean(xh * xh, axis=1, keepdims=True) + norm_eps)
            pick = jnp.where(iota((8, 128), 1) == SL + H, 1.0, 0.0).astype(bf16)
            gain_ref[...] = dot(pick, w_ref[:, IN : IN + 128], NT)
            nh = (xh * inv_h * gain_ref[...]).astype(bf16)
            ph = dot(nh, w_ref[...]).astype(bf16).astype(f32)
            prh_ref[...] = ph
            ext_ref[0:8, :IN] = ph[:, :IN]
            ext_ref[0:8, IN:] = ph[:, IN + 128 :]
            st_ref[...] = jnp.zeros((N, IN), f32)
            ps_ref[...] = jnp.ones((8, IN), f32)

        @when_later
        def _():
            ext_ref[0:8, :] = ext_ref[L : L + 8, :]

        x = x_ref[...]
        inv = lax.rsqrt(jnp.mean(x * x, axis=1, keepdims=True) + norm_eps)
        nb = (x * inv * gain_ref[0:1, :]).astype(bf16)
        nb_ref[...] = nb
        pr = dot(nb, w_ref[...]).astype(bf16)
        pr_ref[...] = pr
        prf = pr.astype(f32)
        ext_ref[8 : 8 + L, :IN] = prf[:, :IN]
        ext_ref[8 : 8 + L, IN:] = prf[:, IN + 128 :]
        summed = jnp.zeros((L, EXT), f32) + cw_ref[TAPS : TAPS + 1, :]
        for k in range(TAPS):
            d = TAPS - 1 - k
            term = cw_ref[k : k + 1, :] * ext_ref[8 - d : 8 - d + L, :]
            summed = summed + (term if d == 0 else term * to_shift(meta, c, EXT, d))
        sm_ref[...] = summed
        act = summed * sigmoid(summed)
        act_ref[...] = act
        slab = pr[:, IN : IN + 128]
        hp, hc = hp_ref[...], hc_ref[...]
        mask8 = mask_ref[...]
        mask_c = dot(mask8, jnp.where(iota((8, IN), 0) == 0, 1.0, 0.0), TN)
        dt = softplus(dot(slab, expand_matrix().astype(bf16)) + hp[0:1, :]) * mask_c
        dtr = softplus(dot(slab_select().astype(bf16), slab, NT) + hc[:, 0:1]) * mask8[0:1, :]
        tri = tri_leq()
        cum = dot3(tri, dt * hp[1:2, :], TN)
        cumr = dot3(dtr * hc[:, 1:2], tri)
        dt_ref[...], cum_ref[...], dtr_ref[...], cumr_ref[...] = dt, cum, dtr, cumr
        prev, last = chunk_edges(meta, c)
        xd = dt * act[:, :IN]
        ws = local_weights(cum, meta, c, last)
        b = act[:, IN : IN + N]
        passing = jnp.exp(cum[L - 1 : L, :]) * flag(prev == last)
        at = pl.multiple_of(c * N, N)
        st, ps = st_ref[...], ps_ref[...]
        hpre_ref[pl.ds(at, N), :] = st
        pp_ref[pl.ds(pl.multiple_of(c * 8, 8), 8), :] = ps
        st = passing * st + dot3(b, ws * xd, TN)
        ps = ps * passing
        st_ref[...], ps_ref[...] = st, ps

        @when_last
        def _():
            hpre_ref[nC * N : (nC + 1) * N, :] = st
            pp_ref[nC * 8 : nC * 8 + 8, :] = ps
            pack_ref[:N, :] = st.astype(bf16)
            pack_ref[N:, :] = jnp.concatenate([ps, ps], axis=0).astype(bf16)

    def project(meta, x, xh, cw, hp, hc, mask8, shards):
        outs = [
            o_rows((T, D), bf16), o_rows((T, PK), bf16), o_whole((8, PK), f32),
            o_rows((T, EXT), f32), o_rows((T, EXT), f32), o_rows((T, IN), f32),
            o_rows((T, IN), f32), o_cols((8, T), f32), o_cols((8, T), f32),
            o_whole(((nC + 1) * N, IN), f32), o_whole(((nC + 1) * 8, IN), f32),
            o_whole((N + SP, IN), bf16), o_whole((8, D), f32),
        ]
        ins = [SMEM, rows(x), whole(xh), whole(cw), whole(hp), whole(hc), cols(mask8)]
        ins += [whole(s) for s in shards]
        scratch = [
            pltpu.VMEM((D, PK), bf16), pltpu.VMEM((L + 8, EXT), f32),
            pltpu.VMEM((N, IN), f32), pltpu.VMEM((8, IN), f32),
        ]
        return call(k_project, nC, ins, outs, scratch, 2 * T * D * PK,
                    [meta, x, xh, cw, hp, hc, mask8, *shards], unroll=2)

    def head_decay(meta_mask, cum, cumr, h):
        gap = cum[:, h * HW : h * HW + 1] - cumr[h : h + 1, :]
        return jnp.where(meta_mask, jnp.exp(gap), 0.0)

    def k_intra(mref, act_ref, dt_ref, cum_ref, cumr_ref, y_ref):
        meta = Meta(mref, sizes)
        c = Step.chunk
        ok = allowed_mask(meta, c)
        b = act_ref[:, IN : IN + N]
        cc = act_ref[:, IN + N :]
        scores = dot3(cc, b, NT)
        cum, cumr = cum_ref[...], cumr_ref[...]
        for p in range(PAIRS):
            sl = slice(p * 128, p * 128 + 128)
            xd = (dt_ref[:, sl] * act_ref[:, sl])
            y = None
            for j in range(HPT):
                g = (scores * head_decay(ok, cum, cumr, p * HPT + j))
                part = dot3(g, xd)
                y = part if y is None else jnp.where(pair_mask(HW, j), part, y)
            y_ref[:, sl] = y

    def intra(meta, act, dt, cum, cumr):
        return call(k_intra, nC, [SMEM, rows(act), rows(dt), rows(cum), cols(cumr)],
                    [o_rows((T, IN), f32)], [], 4 * T * L * IN, [meta, act, dt, cum, cumr], unroll=2)[0]

    def k_gate(*refs):
        meta = Meta(refs[0], sizes)
        nb_ref, do_ref = refs[1:3]
        shards = refs[3 : 3 + NSH]
        z_ref, dm_ref, w_ref = refs[3 + NSH :]

        @when_first
        def _():
            load_weights(meta, shards, w_ref)

        z_ref[...] = dot(nb_ref[...], w_ref[:, :IN]).astype(bf16)
        dm_ref[...] = dot(do_ref[...].astype(bf16), w_ref[:, IN:])

    def gate(meta, nb, d_out, shards):
        return call(k_gate, nC, [SMEM, rows(nb), rows(d_out)] + [whole(s) for s in shards],
                    [o_rows((T, IN), bf16), o_rows((T, IN), f32)],
                    [pltpu.VMEM((D, 2 * IN), bf16)], 4 * T * D * IN, [meta, nb, d_out, *shards], unroll=2)

    def chain(packs):
        total = None
        for pack in reversed(packs):
            state = pack[:N, :].astype(f32)
            total = state if total is None else state + pack[N : N + 1, :].astype(f32) * total
        return total

    def k_output(*refs):
        meta = Meta(refs[0], sizes)
        act_ref, cum_ref, y_ref, z_ref, dm_ref, hpre_ref, pp_ref, hp_ref, gg_ref = refs[1:10]
        packs = refs[10 : 10 + n_ctx - 1]
        yo_ref, stat_ref, ent_ref = refs[9 + n_ctx :]
        c = Step.chunk

        @when_first
        def _():
            ent_ref[...] = chain(packs)

        prev, _ = chunk_edges(meta, c)
        hin = (hpre_ref[...] + pp_ref[0:1, :] * ent_ref[...])
        cum = cum_ref[...]
        ent = jnp.exp(cum) * in_segment(meta, c, prev)
        y = y_ref[...] + ent * dot3(act_ref[:, IN + N :], hin)
        yo_ref[...] = y
        out = y + hp_ref[2:3, :] * act_ref[:, :IN]
        z = z_ref[...].astype(f32)
        gated = out * (z * sigmoid(z))
        ones = jnp.ones((8, IN), bf16)
        sq = dot3(ones, gated * gated, NT)
        bd = dot3(ones, dm_ref[...] * gg_ref[0:1, :] * gated, NT)
        stat_ref[...] = jnp.where(iota((8, L), 0) == 0, sq, bd)

    def output(meta, act, cum, y, z, dm, hpre, pp, hp, gg, packs):
        ins = [SMEM, rows(act), rows(cum), rows(y), rows(z), rows(dm), rows(hpre, N), rows(pp, 8),
               whole(hp), whole(gg)] + [whole(p) for p in packs]
        outs = [o_rows((T, IN), f32), o_cols((8, T), f32), o_whole((N, IN), f32)]
        return call(k_output, nC, ins, outs, [], 4 * T * IN * N,
                    [meta, act, cum, y, z, dm, hpre, pp, hp, gg, *packs], unroll=2)

    def k_norm(*refs):
        meta = Meta(refs[0], sizes)
        act_ref, cum_ref, y_ref, z_ref, dm_ref, hp_ref, gg_ref = refs[1:8]
        stats = refs[8 : 8 + n_tp]
        mix_ref, dz_ref, dy_ref, suf_ref, psuf_ref, pack_ref, sums_ref = refs[8 + n_tp : 15 + n_tp]
        st_ref, ps_ref = refs[15 + n_tp :]
        c = nC - 1 - Step.chunk

        @when_first
        def _():
            st_ref[...] = jnp.zeros((N, IN), f32)
            ps_ref[...] = jnp.ones((8, IN), f32)
            sums_ref[...] = jnp.zeros((8, IN), f32)

        stat = stats[0][...]
        for s in stats[1:]:
            stat = stat + s[...]
        inner = float(IN * n_tp)
        inv_r = lax.rsqrt(stat[0:1, :] / inner + norm_eps)
        beta_r = inv_r * inv_r * inv_r * stat[1:2, :] / inner
        row = iota((8, L), 0)
        both = jnp.where(row == 0, inv_r, jnp.where(row == 1, beta_r, 0.0))
        inv = dot3(both, jnp.where(iota((8, IN), 0) == 0, 1.0, 0.0).astype(bf16), TN)
        beta = dot3(both, jnp.where(iota((8, IN), 0) == 1, 1.0, 0.0).astype(bf16), TN)
        gg, skip = gg_ref[0:1, :], hp_ref[2:3, :]
        x = act_ref[:, :IN]
        out = y_ref[...] + skip * x
        z = z_ref[...].astype(f32)
        sig = sigmoid(z)
        ga = z * sig
        gated = out * ga
        dm = dm_ref[...]
        normal = gated * inv
        mix_ref[...] = (normal * gg).astype(bf16)
        dg = dm * gg * inv - gated * beta
        dz_ref[...] = (dg * out * sig * (1.0 + z * (1.0 - sig))).astype(bf16)
        dy = dg * ga
        dyb = dy
        dy_ref[...] = dyb
        s0 = jnp.sum(dm * normal, axis=0, keepdims=True)
        s1 = jnp.sum(dy * x, axis=0, keepdims=True)
        r8 = iota((8, IN), 0)
        sums_ref[...] += jnp.where(r8 == 0, s0, jnp.where(r8 == 1, s1, 0.0))
        prev, last = chunk_edges(meta, c)
        cum = cum_ref[...]
        ent = jnp.exp(cum) * in_segment(meta, c, prev)
        passing = jnp.exp(cum[L - 1 : L, :]) * flag(prev == last)
        st, ps = st_ref[...], ps_ref[...]
        suf_ref[...] = st
        psuf_ref[...] = ps
        cc = act_ref[:, IN + N :]
        st = passing * st + dot3(cc, ent * dyb.astype(f32), TN)
        ps = passing * ps
        st_ref[...], ps_ref[...] = st, ps

        @when_last
        def _():
            pack_ref[:N, :] = st.astype(bf16)
            pack_ref[N:, :] = jnp.concatenate([ps, ps], axis=0).astype(bf16)

    def norm(meta, act, cum, y, z, dm, hp, gg, stats):
        def back(item):
            block, index = item[0], item[1]
            return (block, lambda i: index(nC - 1 - i)) + tuple(item[2:])

        ins = [SMEM] + [back(rows(a)) for a in (act, cum, y, z, dm)] + [whole(hp), whole(gg)]
        ins += [back(cols(s)) for s in stats]
        outs = [back(o_rows((T, IN), bf16)), back(o_rows((T, IN), bf16)), back(o_rows((T, IN), f32)),
                back(o_rows((nC * N, IN), f32, N)), back(o_rows((nC * 8, IN), f32, 8)),
                o_whole((N + SP, IN), bf16), o_whole((8, IN), f32)]
        scratch = [pltpu.VMEM((N, IN), f32), pltpu.VMEM((8, IN), f32)]
        return call(k_norm, nC, ins, outs, scratch, 2 * T * IN * N,
                    [meta, act, cum, y, z, dm, hp, gg, *stats], unroll=2)

    def k_intra_back(mref, act_ref, dt_ref, cum_ref, cumr_ref, dy_ref, dxd_ref, dbc_ref):
        meta = Meta(mref, sizes)
        c = Step.chunk
        ok = allowed_mask(meta, c)
        b = act_ref[:, IN : IN + N]
        cc = act_ref[:, IN + N :]
        scores = dot3(cc, b, NT)
        cum, cumr = cum_ref[...], cumr_ref[...]
        d_scores = jnp.zeros((L, L), f32)
        for p in range(PAIRS):
            sl = slice(p * 128, p * 128 + 128)
            xd = (dt_ref[:, sl] * act_ref[:, sl])
            dy = dy_ref[:, sl]
            dxd = None
            for j in range(HPT):
                decay = head_decay(ok, cum, cumr, p * HPT + j)
                g = (scores * decay)
                part = dot3(g, dy, TN)
                dxd = part if dxd is None else jnp.where(pair_mask(HW, j), part, dxd)
                own = jnp.where(pair_mask(HW, j), dy.astype(f32), 0.0)
                d_scores = d_scores + dot3(own, xd, NT) * decay
            dxd_ref[:, sl] = dxd
        ds = d_scores
        dbc_ref[:, :N] = dot3(ds, cc, TN)
        dbc_ref[:, N:] = dot3(ds, b)

    def intra_back(meta, act, dt, cum, cumr, dy):
        return call(k_intra_back, nC,
                    [SMEM, rows(act), rows(dt), rows(cum), cols(cumr), rows(dy)],
                    [o_rows((T, IN), f32), o_rows((T, 2 * N), f32)], [], 8 * T * L * IN,
                    [meta, act, dt, cum, cumr, dy], unroll=2)

    def write_blocks(meta, total, outs):
        if not DIRECT:
            outs[0][...] = total[...].astype(bf16)
            return
        br = D // NSH
        for i in range(NSH):
            at = pl.multiple_of(meta.block_row(i), 8)
            outs[i % n_ctx][(i // n_ctx) * br : (i // n_ctx + 1) * br, :] = total[
                pl.ds(at, br), :
            ].astype(bf16)

    n_groups = n_ctx if DIRECT else 1
    group_rows = D // n_ctx if DIRECT else D

    def split_rows(meta, c, value, keep, send):
        at = pl.multiple_of(lax.rem(c, nC // 2) * L, L)

        @pl.when(c // (nC // 2) == meta.half)
        def _():
            keep[pl.ds(at, L), :] = value

        @pl.when(c // (nC // 2) != meta.half)
        def _():
            send[pl.ds(at, L), :] = value.astype(bf16)

    def k_outer(*refs):
        meta = Meta(refs[0], sizes)
        nb_ref, do_ref, mix_ref, dz_ref = refs[1:5]
        shards = refs[5 : 5 + NSH]
        outs = refs[5 + NSH : 5 + NSH + n_groups]
        keep_ref, send_ref = refs[5 + NSH + n_groups : 7 + NSH + n_groups]
        w_ref, total = refs[7 + NSH + n_groups :]
        c = pl.program_id(0)

        @pl.when(c == 0)
        def _():
            load_weights(meta, shards, w_ref)

        mix = mix_ref[pl.ds(pl.multiple_of(c * L, L), L), :]
        split_rows(meta, c, dot(mix, w_ref[:, IN:], NT), keep_ref, send_ref)

        @pl.when(c == nC - 1)
        def _():
            total[:, :IN] = dot(nb_ref[...], dz_ref[...], TN)
            total[:, IN:] = dot(do_ref[...].astype(bf16), mix_ref[...], TN)
            write_blocks(meta, total, outs)

    def outer(meta, nb, d_out, mix, dz, shards):
        outs = [o_whole((group_rows, 2 * IN), bf16)] * n_groups
        outs += [o_whole((T // 2, D), f32), o_whole((T // 2, D), bf16)]
        ins = [SMEM] + [whole(a) for a in (nb, d_out, mix, dz, *shards)]
        scratch = [pltpu.VMEM((D, 2 * IN), bf16), pltpu.VMEM((D, 2 * IN), f32)]
        got = call(k_outer, nC, ins, outs, scratch, 6 * T * D * IN,
                   [meta, nb, d_out, mix, dz, *shards])
        return got[:n_groups], got[n_groups], got[n_groups + 1]

    def k_scan_back(*refs):
        meta = Meta(refs[0], sizes)
        (act_ref, sm_ref, pr_ref, dt_ref, cum_ref, dtr_ref, y_ref, dy_ref, dxd_ref, dbc_ref, hpre_ref,
         hnext_ref, pp_ref, pnext_ref, ent_ref, suf_ref, psuf_ref, hp_ref, hc_ref, mask_ref, bk_ref,
         bg_ref) = refs[1:23]
        packs, at = refs[23 : 22 + n_ctx], 22 + n_ctx
        dsx_ref, ddt_ref, sums_ref, edge_ref, pair_ref = refs[at : at + 5]
        slices = refs[at + 5 : at + 5 + n_tp]
        edges = refs[at + 5 + n_tp : at + 4 + 2 * n_tp]
        exit_ref = refs[at + 4 + 2 * n_tp]
        c = pl.program_id(0)
        pair_ref[...] = (bk_ref[...] + bg_ref[...].astype(f32)).astype(bf16)

        @pl.when(c == 0)
        def _():
            exit_ref[...] = chain(packs)
            sums_ref[...] = jnp.zeros((16, 128), f32)

        prev, last = chunk_edges(meta, c)
        hin = hpre_ref[...] + pp_ref[0:1, :] * ent_ref[...]
        hout = hnext_ref[...] + pnext_ref[0:1, :] * ent_ref[...]
        dh = suf_ref[...] + psuf_ref[0:1, :] * exit_ref[...]
        hinb, dhb = hin, dh
        cum, dt, x = cum_ref[...], dt_ref[...], act_ref[:, :IN]
        b = act_ref[:, IN : IN + N]
        ws = local_weights(cum, meta, c, last)
        ent = jnp.exp(cum) * in_segment(meta, c, prev)
        xd = dt * x
        dyf = dy_ref[...].astype(f32)
        leaving = dot3(b, dhb)
        wx = ws * xd
        dxd_in = dxd_ref[...]
        dxd = dxd_in + ws * leaving
        db = dbc_ref[:, :N] + dot3(wx, dhb, NT)
        dc = dbc_ref[:, N:] + dot3(ent * dyf, hinb, NT)
        hs = head_select().astype(bf16)
        dcum = dot3(hs, dyf * y_ref[...] - xd * dxd_in - wx.astype(f32) * leaving, NT)
        final = dot3(hs, jnp.zeros((8, IN), f32) + jnp.sum(dhb.astype(f32) * hout, axis=0, keepdims=True), NT)
        da = dot3(dcum, tri_leq(), NT) + final[:, 0:1]
        hc = hc_ref[...]
        dtr, mask8 = dtr_ref[...], mask_ref[...]
        ddt = da * hc[:, 1:2] + dot3(hs, dxd * x, NT)
        slab = pr_ref[:, IN : IN + 128]
        pre_r = dot(slab_select().astype(bf16), slab, NT) + hc[:, 0:1]
        dpre = ddt * mask8[0:1, :] * sigmoid(pre_r)
        ddt_ref[...] = dot(dpre.astype(bf16), slab_select().astype(bf16), TN).astype(bf16)
        ones = jnp.ones((L, 128), bf16)
        sums_ref[0:8, :] += dot3(dpre, ones)
        sums_ref[8:16, :] += dot3(da * dtr, ones)
        sm = sm_ref[...]
        sig = sigmoid(sm)
        dsilu = sig * (1.0 + sm * (1.0 - sig))
        dsx = (hp_ref[2:3, :] * dyf + dt * dxd) * dsilu[:, :IN]
        dsx_ref[...] = dsx
        dsb = (jnp.concatenate([db, dc], axis=1) * dsilu[:, IN:]).astype(bf16)
        quarter = c // (nC // 2)
        at = pl.multiple_of(lax.rem(c, nC // 2) * L, L)
        r, l = iota((2 * N, 128), 0), iota((2 * N, 128), 1)
        for k in range(n_tp):
            left = meta.peer(k) * SL
            lane0 = quarter * SL
            pick = jnp.where((r - left == l - lane0) & (l >= lane0) & (l < lane0 + SL), 1.0, 0.0)
            part = dot(dsb, pick.astype(bf16)).astype(bf16)

            @pl.when(quarter == 0)
            def _():
                slices[k][pl.ds(at, L), :] = part

            @pl.when(quarter != 0)
            def _():
                slices[k][pl.ds(at, L), :] = slices[k][pl.ds(at, L), :] + part

            @pl.when(c == 0)
            def _():
                if k == 0:
                    edge_ref[:, :IN] = dsx[0:8, :]
                    edge_ref[:, IN:] = part[0:8, :].astype(f32)
                else:
                    edges[k - 1][...] = part[0:8, :].astype(f32)

    def scan_back(meta, act, sm, pr, dt, cum, dtr, y, dy, dxd, dbc, hpre, pp, ent, suf, psuf, hp, hc,
                  mask8, b_keep, b_got, packs):
        def later(item):
            return (item[0], lambda i: item[1](i + 1))

        ins = [SMEM, rows(act), rows(sm), rows(pr), rows(dt), rows(cum), cols(dtr), rows(y), rows(dy),
               rows(dxd), rows(dbc), rows(hpre, N), later(rows(hpre, N)), rows(pp, 8),
               later(rows(pp, 8)), whole(ent), rows(suf, N), rows(psuf, 8), whole(hp), whole(hc),
               cols(mask8), rows(b_keep, HB), rows(b_got, HB)] + [whole(p) for p in packs]
        outs = [o_rows((T, IN), f32), o_rows((T, 128), bf16), o_whole((16, 128), f32),
                o_whole((8, IN + 128), f32), o_rows((T // 2, D), bf16, HB)]
        outs += [o_whole((T // 2, 128), bf16)] * n_tp + [o_whole((8, 128), f32)] * (n_tp - 1)
        got = call(k_scan_back, nC, ins, outs, [pltpu.VMEM((N, IN), f32)],
                   6 * T * IN * N,
                   [meta, act, sm, pr, dt, cum, dtr, y, dy, dxd, dbc, hpre, hpre, pp, pp, ent, suf,
                    psuf, hp, hc, mask8, b_keep, b_got, *packs])
        return got[:5], got[5 : 5 + n_tp], got[5 + n_tp :]

    PW = IN + 128
    br9 = D // NSH

    def k_conv_back(*refs):
        meta = Meta(refs[0], sizes)
        nb_ref, pr_ref, prp_ref, prh_ref, dz_ref, ddt_ref, dsx_ref, dsn_ref = refs[1:9]
        cw_ref, sums_ref, ssum_ref, edge_ref = refs[9:13]
        at = 13
        slices, at = refs[at : at + n_tp], at + n_tp
        edges, at = refs[at : at + n_tp - 1], at + n_tp - 1
        shards, at = refs[at : at + NSH], at + NSH
        zshards, at = refs[at : at + NSH], at + NSH
        gs, at = refs[at : at + NSH], at + NSH
        keep_ref, send_ref = refs[at : at + 2]
        at += 2
        w_ref, wz_ref, ex_ref, px_ref, sl_ref, total, tap_ref, dp_ref = refs[at:]
        c = pl.program_id(0)

        @pl.when(c == 0)
        def _():
            load_weights(meta, shards, w_ref)
            load_weights(meta, zshards, wz_ref)
            tap_ref[...] = jnp.zeros((8, PW), f32)
            sl = slices[0][...].astype(f32)
            for s in slices[1:]:
                sl = sl + s[...].astype(f32)
            low = iota((T // 2, 128), 1) < SL
            sl_ref[0 : T // 2, :] = jnp.where(low, sl, 0.0)
            sl_ref[T // 2 : T, :] = jnp.where(low, pltpu.roll(sl, 128 - SL, 1), 0.0)
            e = edge_ref[:, IN:]
            for s in edges:
                e = e + s[...]
            sl_ref[T : T + 8, :] = jnp.where(iota((8, 128), 1) < SL, e, 0.0)

        here = pl.multiple_of(c * L, L)
        after = pl.multiple_of(c * L + L, L)
        ex_ref[0:L, :IN] = dsx_ref[...]
        ex_ref[0:L, IN:] = sl_ref[pl.ds(here, L), :]
        ex_ref[L : L + 8, IN:] = sl_ref[pl.ds(after, 8), :]
        ex_ref[L : L + 8, :IN] = jnp.where(c == nC - 1, edge_ref[:, :IN], dsn_ref[...])
        low = iota((L, PW), 1) < IN + SL
        px_ref[8 : 8 + L, :] = pr_ref[:, :PW].astype(f32)
        px_ref[0:8, :] = jnp.where(c == 0, prh_ref[:, :PW], prp_ref[8:16, :PW].astype(f32))
        cw = cw_ref[...]
        ds = ex_ref[0:L, :]
        dpre = jnp.zeros((L, PW), f32)
        pos = meta.base + c * L + iota((L, 128), 0)
        seg = meta.segment(pos)
        group = T * n_ctx
        r8 = iota((8, PW), 0)
        taps = jnp.where(r8 == TAPS, jnp.sum(ds, axis=0, keepdims=True), 0.0)
        for k in range(TAPS):
            d = TAPS - 1 - k
            reach = cw[k : k + 1, :] * ex_ref[d : d + L, :]
            prior = ds * px_ref[8 - d : 8 - d + L, :]
            if d > 0:
                ahead = jnp.where((seg == meta.segment(pos + d)) & (pos + d < group), 1.0, 0.0)
                reach = reach * tiled(ahead, PW)
                prior = prior * to_shift(meta, c, PW, d)
            dpre = dpre + reach
            taps = taps + jnp.where(r8 == k, jnp.sum(prior, axis=0, keepdims=True), 0.0)
        tap_ref[...] += taps
        dpre = jnp.where(low, dpre, 0.0)
        dproj = dpre.astype(bf16)
        dslab = (dpre[:, IN:] + ddt_ref[...].astype(f32)).astype(bf16)
        dproj = jnp.concatenate([dproj[:, :IN], dslab], axis=1)
        dp_ref[pl.ds(here, L), :] = dproj
        q = dot(dproj, w_ref[:, :PW], NT) + dot(dz_ref[...], wz_ref[:, :IN], NT)
        split_rows(meta, c, q, keep_ref, send_ref)

        @pl.when(c == nC - 1)
        def _():
            total[...] = dot(nb_ref[...], dp_ref[...], TN)
            low8 = iota((8, PW), 1) < IN + SL
            s = ssum_ref[...]
            zero = jnp.zeros((8, 128), f32)
            pad = jnp.concatenate([s, jnp.zeros((8, PW - IN), f32)], axis=1)
            first = jnp.where(low8, tap_ref[...], 0.0)
            first = jnp.where(r8 == 5, pad[0:1, :], jnp.where(r8 == 6, pad[1:2, :], first))
            lead = first.astype(bf16).astype(f32)
            first = jnp.where(r8 == 7, (first - lead)[TAPS : TAPS + 1, :], first)
            pair = [sums_ref[0:8, :], sums_ref[8:16, :]]
            rest = [p - p.astype(bf16).astype(f32) for p in pair]
            tail = pair + rest + [zero] * (PW // 128 - 4)
            small = jnp.concatenate([first, jnp.concatenate(tail, axis=1)], axis=0).astype(bf16)
            if not DIRECT:
                gs[0][:D, :] = total[...].astype(bf16)
                gs[0][D:, :] = small
            else:
                for i in range(NSH):
                    at = pl.multiple_of(meta.block_row(i), 8)
                    gs[i][:br9, :] = total[pl.ds(at, br9), :].astype(bf16)
                    gs[i][br9:, :] = small

    def conv_back(meta, nb, pr, prh, dz, ddt, dsx, cw9, sums, ssum, edge, slices, edges, shards,
                  zshards):
        step = L // 16
        prior = ((16, PK), lambda i: (jnp.maximum(i * step - 1, 0), 0))
        after = ((8, IN), lambda i: (jnp.minimum((i + 1) * (L // 8), T // 8 - 1), 0))
        ins = [SMEM, whole(nb), rows(pr), prior, whole(prh), rows(dz), rows(ddt), rows(dsx), after,
               whole(cw9), whole(sums), whole(ssum), whole(edge)]
        ins += [whole(a) for a in (*slices, *edges, *shards, *zshards)]
        outs = [o_whole((br9 + 16, PW), bf16)] * NSH
        outs += [o_whole((T // 2, D), f32), o_whole((T // 2, D), bf16)]
        scratch = [pltpu.VMEM((D, PK), bf16), pltpu.VMEM((D, 2 * IN), bf16),
                   pltpu.VMEM((L + 8, PW), f32), pltpu.VMEM((L + 8, PW), f32),
                   pltpu.VMEM((T + 8, 128), f32), pltpu.VMEM((D, PW), f32),
                   pltpu.VMEM((8, PW), f32), pltpu.VMEM((T, PW), bf16)]
        got = call(k_conv_back, nC, ins, outs, scratch, 4 * T * D * (PW + IN),
                    [meta, nb, pr, pr, prh, dz, ddt, dsx, dsx, cw9, sums, ssum, edge, *slices, *edges,
                     *shards, *zshards])
        return got[:NSH], got[NSH:]

    def k_tables(mref, wx, bx, wbc, bbc, bias, alog, skip, gain, mask, cw, cw9, hp, hc, gg, mask8):
        meta = Meta(mref, sizes)
        zeros = lambda n, w: jnp.zeros((n, w), f32)
        left = jnp.concatenate([wx[...], bx[...], zeros(7 - TAPS, IN)], axis=0)
        right = jnp.concatenate([wbc[...], bbc[...], zeros(7 - TAPS, 2 * N)], axis=0)
        cw[...] = jnp.concatenate([left, right], axis=1)
        r, l = iota((2 * N, 128), 0), iota((2 * N, 128), 1)
        pick = jnp.where((r == l + meta.me_t * SL) & (l < SL), 1.0, 0.0)
        cw9[...] = jnp.concatenate([left, dot(right, pick, NN, HI)], axis=1)
        rate = -jnp.exp(alog[...])
        row = iota((8, H), 0)
        rows8 = jnp.where(row == 0, bias[...], jnp.where(row == 1, rate, jnp.where(row == 2, skip[...], 0.0)))
        spread = jnp.where(iota((H, IN), 1) // HW == iota((H, IN), 0), 1.0, 0.0)
        hp[...] = dot(rows8, spread, NN, HI)
        eye = jnp.where(iota((8, 128), 0) == iota((8, 128), 1), 1.0, 0.0)
        turn = jnp.where(iota((8, H), 0) == iota((8, H), 1), 1.0, 0.0)
        hc[...] = dot(dot(turn, rows8, NT, HI), eye, NN, HI)
        gg[...] = jnp.zeros((8, IN), f32) + gain[...]
        mask8[...] = jnp.zeros((8, T), f32) + mask[...].astype(f32)

    def tables(*args):
        outs = [o_whole((8, EXT), f32), o_whole((8, PW), f32), o_whole((8, IN), f32),
                o_whole((8, 128), f32), o_whole((8, IN), f32), o_whole((8, T), f32)]
        return call(k_tables, 1, [SMEM] + [whole(a) for a in args[1:]], outs, [], 0, args)

    def k_finish(*refs):
        meta = Meta(refs[0], sizes)
        first_ref, second_ref = refs[1:3]
        blocks, parts = refs[3 : 3 + n_ctx], refs[3 + n_ctx : 5 + n_ctx]
        alog = refs[5 + n_ctx]
        gz, go, gx, slab_ref, wx, bx, gain_row, h_dt, h_log, h_skip, last, order = refs[6 + n_ctx :]
        zo = parts[0][...]
        for p in parts[1:]:
            zo = zo + p[...].astype(f32)
        gz[...], go[...] = zo[:, :IN], zo[:, IN:]
        total = None
        for r in range(n_ctx):
            b = blocks[r][...].astype(f32)
            total = b[:br9] if total is None else total + b[:br9]
            order[lax.rem(meta.me_c - r + n_ctx, n_ctx)] = b[br9:]
        small = order[0]
        for r in range(1, n_ctx):
            small = small + order[r]
        gx[...] = total[:, :IN]
        slab = total[:, IN:]
        slab_ref[...] = slab
        lane = iota((br9, 128), 1)
        w_slab = first_ref[:, IN : IN + 128].astype(f32)
        gain = jnp.sum(jnp.where(lane == SL + H, w_slab, 0.0), axis=1, keepdims=True)
        d_gain = jnp.sum(first_ref[:, :IN].astype(f32) * total[:, :IN], axis=1, keepdims=True)
        d_gain = d_gain + jnp.sum(second_ref[:, :IN].astype(f32) * zo[:, :IN], axis=1, keepdims=True)
        d_gain = d_gain + jnp.sum(jnp.where(lane < SL + H, w_slab * slab, 0.0), axis=1, keepdims=True)
        last[:br9, :] = jnp.where(lane < SL, slab, jnp.where(lane == SL, d_gain / gain, 0.0))
        top = small[0:8]
        bias = top[TAPS : TAPS + 1] + top[7:8]
        wx[...] = top[:TAPS, :IN]
        bx[...] = bias[:, :IN].reshape(IN)
        gain_row[...] = top[5:6, :IN].reshape(IN)
        taps = jnp.where(iota((8, PW), 0) == TAPS, bias, top)
        last[br9:, :] = jnp.where(iota((8, 128), 1) < SL, taps[:, IN:], 0.0)
        pair = small[8:16, 0:256] + small[8:16, 256:512]
        skip = dot(head_select(), jnp.zeros((8, IN), f32) + top[6:7, :IN], NT, HI)
        eye8 = iota((8, 128), 0) == iota((8, 128), 1)

        def flat(col):
            return jnp.sum(jnp.where(eye8, col, 0.0), axis=0, keepdims=True)[:, :H]

        h_dt[...] = flat(pair[:, 0:1]).reshape(H)
        h_log[...] = (flat(pair[:, 128:129]) * -jnp.exp(alog[...])).reshape(H)
        h_skip[...] = flat(skip[:, 0:1]).reshape(H)

    def finish(meta, first, second, blocks, parts, a_log):
        args = [meta, first, second, *blocks, *parts, a_log]
        outs = [o_whole((br9, IN), f32)] * 3 + [o_whole((br9, 128), f32), o_whole((TAPS, IN), f32),
                o_whole((IN,), f32), o_whole((IN,), f32), o_whole((H,), f32), o_whole((H,), f32),
                o_whole((H,), f32), o_whole((br9 + 8, 128), f32)]
        return call(k_finish, 1, [SMEM] + [whole(a) for a in args[1:]], outs,
                    [pltpu.VMEM((n_ctx, 16, PW), f32)], 0, args)

    def k_spread(mref, *refs):
        meta = Meta(mref, sizes)
        parts = refs[:n_tp]
        wbc, gain, taps, bias, last = refs[n_tp:]
        for k in range(n_tp):
            last[meta.peer(k)] = parts[k][...]
        per = 128 // SL
        lane = iota((br9 + 8, 128), 1)
        for t in range(n_tp // per):
            tile = last[t * per]
            for j in range(1, per):
                tile = jnp.where(lane >= j * SL, pltpu.roll(last[t * per + j], j * SL, 1), tile)
            sl = slice(t * 128, t * 128 + 128)
            wbc[:, sl] = tile[:br9]
            taps[:, sl] = tile[br9 : br9 + TAPS]
            bias[sl] = tile[br9 + TAPS : br9 + TAPS + 1].reshape(128)
        total = last[0][:br9]
        for k in range(1, n_tp):
            total = total + last[k][:br9]
        col = jnp.sum(jnp.where(iota((br9, 128), 1) == SL, total, 0.0), axis=1, keepdims=True)
        eye = iota((br9, br9), 0) == iota((br9, br9), 1)
        gain[...] = jnp.sum(jnp.where(eye, col, 0.0), axis=0, keepdims=True).reshape(br9)

    def spread(meta, parts):
        outs = [o_whole((br9, 2 * N), f32), o_whole((br9,), f32), o_whole((TAPS, 2 * N), f32),
                o_whole((2 * N,), f32)]
        return call(k_spread, 1, [SMEM] + [whole(p) for p in parts], outs,
                    [pltpu.VMEM((n_tp, br9 + 8, 128), f32)], 0, [meta, *parts])

    return dict(tables=tables, finish=finish, spread=spread, project=project, intra=intra, gate=gate, output=output, norm=norm,
                intra_back=intra_back, outer=outer, scan_back=scan_back, conv_back=conv_back,
                SL=SL, PW=PW)


def block(x_in, norm_gain, w_z, w_x, w_bc, w_dt, w_out, conv_wx, conv_bx, conv_wbc, conv_bbc, dt_bias,
          a_log, d_skip, gate_gain, seq_lens, token_mask, d_out):
    T, D = x_in.shape
    H, IN, N, TAPS = dt_bias.shape[0], w_z.shape[1], w_bc.shape[1] // 2, conv_wx.shape[0]
    n_sh, n_ctx, n_tp = (lax.axis_size(a) for a in (AS, AC, AT))
    me_s, me_c, me_t = (lax.axis_index(a) for a in (AS, AC, AT))
    direct = n_sh == 2 and n_ctx == 4
    NSH = n_sh * n_ctx if direct else 1
    seqs = seq_lens.shape[1]
    sizes = dict(T=T, D=D, IN=IN, N=N, H=H, TAPS=TAPS, tp=n_tp, ctx=n_ctx, seqs=seqs, shards=NSH)
    ops = build(sizes)
    SL = ops["SL"]
    HW = IN // H
    br = w_z.shape[0]

    def ring(count, step):
        return [(i, (i + step) % count) for i in range(count)]

    def xor(count, step):
        return [(i, i ^ step) for i in range(count)]

    def gather(part):
        if not direct:
            return [lax.all_gather(part, (AS, AC), axis=0, tiled=True)]
        here = [part]
        for k in range(1, n_ctx):
            here.append(lax.ppermute(part, AC, ring(n_ctx, k)))
        there = []
        for p in here:
            there.append(lax.ppermute(p, AS, ring(n_sh, 1)))
        return here + there

    meta = jnp.concatenate([jnp.stack([me_s, me_c, me_t]).astype(jnp.int32), seq_lens[0]])

    w_slice = lax.dynamic_slice_in_dim(w_bc, me_t * SL, SL, 1)
    first = jnp.concatenate(
        [w_x, w_slice, w_dt, norm_gain[:, None], jnp.zeros((br, 127 - SL - H), bf16), w_bc], axis=1
    )
    x_tail = lax.ppermute(x_in[T - 8 :], AC, [(i, i + 1) for i in range(n_ctx - 1)])
    shards = gather(first)
    second = jnp.concatenate([w_z, w_out], axis=1)
    shards2 = gather(second)

    cw, cw9, hp, hc, gg, mask8 = ops["tables"](
        meta, conv_wx, conv_bx[None, :], conv_wbc, conv_bbc[None, :], dt_bias[None, :],
        a_log[None, :], d_skip[None, :], gate_gain[None, :], token_mask[None, :])

    (nb, pr, prh, sm, act, dt, cum, dtr, cumr, hpre, pp, pack, gain_row) = ops["project"](
        meta, x_in, x_tail, cw, hp, hc, mask8, shards)
    packs = [lax.ppermute(pack, AC, [(i, i + k) for i in range(n_ctx - k)]) for k in range(1, n_ctx)]
    y_in = ops["intra"](meta, act, dt, cum, cumr)
    z, dm = ops["gate"](meta, nb, d_out, shards2)
    y, stat, entry = ops["output"](meta, act, cum, y_in, z, dm, hpre, pp, hp, gg, packs)
    stats = [stat] + [lax.ppermute(stat, AT, xor(n_tp, k)) for k in range(1, n_tp)]
    mix, dz, dy, suf, psuf, bpack, ssum = ops["norm"](meta, act, cum, y, z, dm, hp, gg, stats)
    bpacks = []
    for k in range(1, n_ctx):
        bpacks.append(lax.ppermute(bpack, AC, [(i + k, i) for i in range(n_ctx - k)]))
    dxd, dbc = ops["intra_back"](meta, act, dt, cum, cumr, dy)
    groups, b_keep, b_send = ops["outer"](meta, nb, d_out, mix, dz, shards2)

    def both_halves(part):
        mine = part.astype(bf16)
        other = lax.ppermute(mine, AT, xor(n_tp, 1))
        flip = me_t % 2 == 1
        low, high = jnp.where(flip, other, mine), jnp.where(flip, mine, other)
        return jnp.concatenate([low, high], axis=0).astype(f32)

    b_got = lax.ppermute(b_send, AT, xor(n_tp, 1))
    (dsx, ddt, sums, edge, b_pair), slices, edges = ops["scan_back"](
        meta, act, sm, pr, dt, cum, dtr, y, dy, dxd, dbc, hpre, pp, entry, suf, psuf, hp, hc, mask8,
        b_keep, b_got, bpacks)
    got_edge = lax.ppermute(edge, AC, [(i + 1, i) for i in range(n_ctx - 1)])
    got_slices, got_edges = [slices[0]], []
    for k in range(1, n_tp):
        got_slices.append(lax.ppermute(slices[k], AT, xor(n_tp, k)))
        across = [((i + 1) * n_tp + j, i * n_tp + (j ^ k)) for i in range(n_ctx - 1) for j in range(n_tp)]
        got_edges.append(lax.ppermute(edges[k - 1], (AC, AT), across))
    b_half = b_pair.astype(f32)
    for k in range(2, n_tp, 2):
        b_half = b_half + lax.ppermute(b_pair, AT, xor(n_tp, k)).astype(f32)
    if direct:
        total = groups[0].astype(f32)
        for r in range(1, n_ctx):
            got = lax.ppermute(groups[r], AC, ring(n_ctx, r))
            total = total + got.astype(f32)
        other = lax.ppermute(total[br:].astype(bf16), AS, ring(n_sh, 1))
        parts = [total[:br], other]
    grads, (q_keep, q_send) = ops["conv_back"](
        meta, nb, pr, prh, dz, ddt, dsx, cw9, sums, ssum, got_edge, got_slices, got_edges, shards,
        shards2)
    if direct:
        moved = []
        for r in [*range(1, n_ctx), 0]:
            got = lax.ppermute(grads[n_ctx + r], AS, ring(n_sh, 1))
            moved.append(pair_sum(grads[r], got))
        blocks = [moved[-1]]
        for r in range(1, n_ctx):
            blocks.append(lax.ppermute(moved[r - 1], AC, ring(n_ctx, r)))

    q_got = lax.ppermute(q_send, AT, xor(n_tp, 1))
    q_pair = pair_sum(q_keep, q_got)
    q_half = q_pair.astype(f32)
    for k in range(2, n_tp, 2):
        q_half = q_half + lax.ppermute(q_pair, AT, xor(n_tp, k)).astype(f32)
    block_whole = both_halves(b_half)
    block_out = x_in + block_whole

    x_half = lax.dynamic_slice_in_dim(x_in, (me_t % 2) * (T // 2), T // 2, 0)
    inv = lax.rsqrt(jnp.mean(x_half * x_half, axis=1, keepdims=True) + norm_eps)
    q_half = q_half * gain_row[0:1, :]
    row_dot = jnp.sum(q_half * x_half, axis=1, keepdims=True)
    q_whole = both_halves(q_half * inv - x_half * (inv * inv * inv) * row_dot / D)
    d_input = d_out + q_whole

    if direct:
        g_z, g_out, g_x, g_slab, d_cx, d_bx, d_gg, d_dt_bias, d_a_log, d_skips, last = ops["finish"](
            meta, first, second, blocks, parts, a_log[None, :])
        lasts = [last]
        for k in range(1, n_tp):
            lasts.append(lax.ppermute(last, AT, xor(n_tp, k)))
        d_w_dt = g_slab[:, SL : SL + H]
        d_w_bc, d_norm_gain, d_cbc, d_bbc = ops["spread"](meta, lasts)
        return (
            block_out, d_input, d_norm_gain, g_z, g_x, d_w_bc, d_w_dt, g_out,
            d_cx, d_bx, d_cbc, d_bbc, d_dt_bias, d_a_log, d_skips, d_gg,
        )

    axes = (AS, AC)
    total = lax.psum_scatter(groups[0].astype(f32), axes, scatter_dimension=0, tiled=True)
    g_first = lax.psum_scatter(grads[0][:D].astype(f32), axes, scatter_dimension=0, tiled=True)
    small = lax.psum(grads[0][D:].astype(f32), axes)
    bias_row = small[TAPS] + small[7]
    sums = small[8 : 8 + H, 0:256] + small[8 : 8 + H, 256:512]
    gain = norm_gain.astype(f32)[:, None]
    g_z, g_out = total[:, :IN], total[:, IN:]
    w_slab = jnp.concatenate([w_slice, w_dt], axis=1).astype(f32)
    g_slab = g_first[:, IN : IN + SL + H]
    d_gain = jnp.sum(w_z.astype(f32) * g_z + w_x.astype(f32) * g_first[:, :IN], axis=1)
    d_gain = (d_gain + jnp.sum(w_slab * g_slab, axis=1)) / gain[:, 0]
    last = jnp.concatenate([
        jnp.concatenate([g_slab[:, :SL], d_gain[:, None], jnp.zeros((br, 127 - SL), f32)], axis=1),
        jnp.pad(jnp.concatenate([small[:TAPS], bias_row[None, :]], axis=0)[:, IN : IN + SL],
                ((0, 7 - TAPS), (0, 128 - SL)))], axis=0)
    last = lax.all_gather(last, AT)
    d_w_bc = jnp.concatenate([last[k, :br, :SL] for k in range(n_tp)], axis=1)
    d_norm_gain = jnp.sum(last[:, :br, SL], axis=0)
    d_cbc = jnp.concatenate([last[k, br : br + TAPS + 1, :SL] for k in range(n_tp)], axis=1)
    return (
        block_out, d_input, d_norm_gain,
        g_z, g_first[:, :IN], d_w_bc, g_slab[:, SL:], g_out,
        small[:TAPS, :IN], bias_row[:IN], d_cbc[:TAPS], d_cbc[TAPS],
        sums[:, 0], sums[:, 128] * -jnp.exp(a_log),
        jnp.sum(small[6, :IN].reshape(H, HW), axis=1), small[5, :IN],
    )


def solution(mesh):
    row = (AS, AC)
    in_specs = (
        P(row, None), P(row), P(row, AT), P(row, AT), P(row, None), P(row, AT), P(row, AT),
        P(None, AT), P(AT), P(), P(), P(AT), P(AT), P(AT), P(AT), P(AS, None), P(row),
        P(row, None),
    )
    out_specs = (
        P(row, None), P(row, None), P(row), P(row, AT), P(row, AT), P(row, None), P(row, AT),
        P(row, AT), P(None, AT), P(AT), P(), P(), P(AT), P(AT), P(AT), P(AT),
    )
    return jax.shard_map(block, mesh=mesh, in_specs=in_specs, out_specs=out_specs, check_vma=False)
```
